32 devices in a mesh: stream: 2 (over core), dp: 16 (over z, y, x).
Axes of the slice: x: 2, y: 2, z: 4, core: 2. Of those that a mesh axis runs over, the one named last changes fastest.
Arguments:
- stream_rows: bfloat16 [2, 16, 784, 768], P('stream', 'dp'), may hold values from -6 to 6
- dest: int32 [16, 4], P('dp'), may hold values from 0 to 7, as said below
- prefix_len: int32 [16, 8], P('dp'), may hold values from 0 to 64, as said below
- weights: float32 [9984, 768], P(('stream', 'dp'))
- momentum: float32 [9984, 768], P(('stream', 'dp')), may hold values from -320 to 320
- average: float32 [9984, 768], P(('stream', 'dp'))
- vectors: float32 [9, 768], P(None, ('stream', 'dp'))
- vec_momentum: float32 [9, 768], P(None, ('stream', 'dp')), may hold values from -320 to 320
- vec_average: float32 [9, 768], P(None, ('stream', 'dp'))
- cotangent: bfloat16 [16, 8, 260, 768], P('dp', None, None, 'stream'), may hold values from -6 to 6
Outputs:
- enc_out: bfloat16 [16, 8, 260, 768], P('dp', None, None, 'stream')
- d_rows: float32 [2, 16, 784, 768], P('stream', 'dp')
- weight_grad: float32 [9984, 768], P(('stream', 'dp'))
- new_momentum: float32 [9984, 768], P(('stream', 'dp'))
- new_average: float32 [9984, 768], P(('stream', 'dp'))
- new_weights: float32 [9984, 768], P(('stream', 'dp'))
- new_weights_bf16: bfloat16 [9984, 768], P(('stream', 'dp'))
- vec_grad: float32 [9, 768], P(None, ('stream', 'dp'))
- vec_new_momentum: float32 [9, 768], P(None, ('stream', 'dp'))
- vec_new_average: float32 [9, 768], P(None, ('stream', 'dp'))
- vec_new: float32 [9, 768], P(None, ('stream', 'dp'))
- vec_new_bf16: bfloat16 [9, 768], P(None, ('stream', 'dp'))
The draws below stay inside these ranges and needn't reach their ends.
Inputs may be any that keep to these rules, and one draw needn't show every extreme that they name: `dest`: the entries of a row are distinct. Slot s of image device a belongs to text device (a + 1 + s // 2) mod 16, so one image device sends at most 2 images to one text device, and every image device sends exactly 2 to one of them. `prefix_len`: entry [b, s] is 0 exactly where slot s of text device b receives no image, otherwise 1 or more; some slot holds 64, and some text device receives 8 images.
All inputs are finite; a program needn't handle non-finite values.
Results may differ from the reference program's by a relative error of at most 0.012.
Values may be sent and summed in bfloat16 or wider, within the bound.
A program may use at most 384 MiB of HBM per device.

```python
import jax
import jax.numpy as jnp
from jax import lax

D = 768
HEADS = 12
HD = 64
FF = 3072
PIX = 768
NP = 196
PMAX = 64
SPAN = 4
IMG_DEV = 4
CAP = 2
RSLOT = 8
SEQ = 260
ROWS = 784
NROWS = 9984
IMAGES = 64
N_DP = 16


def slot_table(key):
    device_count = IMAGES // IMG_DEV
    table_key = jax.random.fold_in(key, 11)
    group_key, score_key = jax.random.split(table_key)
    device_ids = jnp.arange(device_count, dtype=jnp.int32)
    full_group = jax.random.randint(group_key, (device_count,), 0, SPAN, dtype=jnp.int32)
    full_group = jnp.where(device_ids < SPAN, SPAN - 1 - device_ids, full_group)
    slot_ids = jnp.arange(RSLOT, dtype=jnp.int32)
    ranking = jax.random.randint(score_key, (device_count, RSLOT), 0, 1 << 20, dtype=jnp.int32) * RSLOT + slot_ids[None, :]
    in_group = slot_ids[None, :] // CAP == full_group[:, None]
    ranking = ranking + jnp.where(in_group, 1 << 28, 0).astype(jnp.int32)
    _, picked = lax.top_k(ranking, IMG_DEV)
    return picked.astype(jnp.int32)


def draw_dest(key, part):
    return slot_table(key)


def draw_prefix_len(key, part):
    slot_map = slot_table(key)
    device_count = IMAGES // IMG_DEV
    slot_ids = jnp.arange(RSLOT, dtype=jnp.int32)
    device_ids = jnp.arange(device_count, dtype=jnp.int32)
    occupied = jnp.any(slot_map[:, :, None] == slot_ids[None, None, :], axis=1)
    source = (device_ids[:, None] - 1 - slot_ids[None, :] // CAP) % device_count
    slot_grid = jnp.broadcast_to(slot_ids[None, :], source.shape)
    filled = occupied[source, slot_grid]
    length_key = jax.random.fold_in(key, 23)
    exponent_key, excess_key = jax.random.split(length_key)
    exponent = jax.random.randint(exponent_key, (device_count, RSLOT), 0, 7, dtype=jnp.int32)
    excess = jax.random.randint(excess_key, (device_count, RSLOT), 0, jnp.left_shift(1, exponent), dtype=jnp.int32)
    lengths = jnp.minimum(1 + excess, PMAX)
    forced = (device_ids[:, None] == SPAN) & (slot_ids[None, :] == 0)
    lengths = jnp.where(forced, PMAX, lengths)
    return jnp.where(filled, lengths, 0).astype(jnp.int32)


def weight_scale():
    row_ids = jnp.arange(NROWS)[:, None]
    scale = jnp.where(row_ids < PIX + 4 * D + FF, D ** (-0.5), FF ** (-0.5))
    scale = jnp.where(row_ids < PIX + 4 * D, 4.0 * D ** (-0.5), scale)
    scale = jnp.where(row_ids < PIX + 3 * D, D ** (-0.5), scale)
    scale = jnp.where(row_ids < PIX, PIX ** (-0.5), scale)
    return scale.astype(jnp.float32)


def draw_weights(key, part):
    return jax.random.normal(jax.random.fold_in(key, 5), (NROWS, D), jnp.float32) * weight_scale()


def draw_average(key, part):
    current = draw_weights(key, part)
    noise = jax.random.normal(jax.random.fold_in(key, 6), (NROWS, D), jnp.float32)
    return current + 0.5 * weight_scale() * noise


def vector_base(key):
    noise = jax.random.normal(jax.random.fold_in(key, 7), (9, D), jnp.float32)
    row_ids = jnp.arange(9)
    is_gain = (row_ids == 0) | (row_ids == 2)
    return jnp.where(is_gain[:, None], 1.0 + 0.1 * noise, 0.3 * noise)


def draw_vectors(key, part):
    return vector_base(key)


def draw_vec_average(key, part):
    noise = jax.random.normal(jax.random.fold_in(key, 8), (9, D), jnp.float32)
    return vector_base(key) + 0.1 * noise


def levels(stream_key, extent, cuts, least, largest):
    loudness = 1.0
    for dim, shards_of in cuts:
        steps = jax.random.uniform(jax.random.fold_in(jax.random.fold_in(stream_key, 6), dim), (shards_of,), jnp.float32, least / len(cuts), largest / len(cuts))
        loudness = loudness * jnp.repeat(jnp.exp(steps), extent[dim] // shards_of).reshape((-1,) + (1,) * (len(extent) - 1 - dim))
    return loudness


def gaussian(stream_key, dims, deviation, bound, shards=(), held_as=jnp.bfloat16):
    loudness = levels(stream_key, dims, shards, -0.22, 0.18) if shards else 1.0
    result = jax.random.normal(stream_key, dims, jnp.float32) * deviation * loudness
    return jnp.minimum(jnp.maximum(result, -bound), bound).astype(held_as)


def setup_inputs(seed: int = 0) -> dict:
    streams_of = jax.random.split(jax.random.key(seed), 11)
    stream_rows = gaussian(streams_of[0], (2, N_DP, ROWS, D), 1.0, 6.0, ((0, 2), (1, 16)))
    dest = draw_dest(jax.random.fold_in(streams_of[10], 71), 0)
    prefix_len = draw_prefix_len(jax.random.fold_in(streams_of[10], 71), 0)
    weights = draw_weights(jax.random.fold_in(streams_of[10], 71), 0)
    momentum = gaussian(streams_of[4], (NROWS, D), (0.5 * (IMAGES * NP) ** 0.5), 320.0, ((0, 32),), jnp.float32)
    average = draw_average(jax.random.fold_in(streams_of[10], 71), 0)
    vectors = draw_vectors(jax.random.fold_in(streams_of[10], 71), 0)
    vec_momentum = gaussian(streams_of[7], (9, D), (0.5 * (IMAGES * NP) ** 0.5), 320.0, ((1, 32),), jnp.float32)
    vec_average = draw_vec_average(jax.random.fold_in(streams_of[10], 71), 0)
    cotangent = gaussian(streams_of[9], (N_DP, RSLOT, SEQ, D), 1.0, 6.0, ((0, 16), (3, 2)))
    return dict(stream_rows=stream_rows, dest=dest, prefix_len=prefix_len, weights=weights, momentum=momentum, average=average, vectors=vectors, vec_momentum=vec_momentum, vec_average=vec_average, cotangent=cotangent)


@jax.custom_vjp
def low(v):
    return lax.optimization_barrier(v.astype(jnp.bfloat16)).astype(jnp.float32)

@jax.custom_vjp
def low_back(v):
    return v

def low_keep(v):
    return (low(v), None)

def low_pass(kept, grad):
    return (grad,)

def back_keep(v):
    return (v, None)

def back_low(kept, grad):
    return (low(grad),)
low.defvjp(low_keep, low_pass)
low_back.defvjp(back_keep, back_low)
HIGHEST = lax.Precision.HIGHEST
EPSILON = 1e-06
MASKED = -1e+30
MOMENT = 0.5
DECAY = 0.5

def layer_norm(values, gain_row, shift_row):
    centre = lax.optimization_barrier(jnp.mean(values, axis=-1, keepdims=True))
    offset = values - centre
    spread = lax.optimization_barrier(jnp.mean(offset * offset, axis=-1, keepdims=True))
    return offset * lax.rsqrt(spread + EPSILON) * gain_row + shift_row

def text_device(low_weights, low_vectors, image_rows, packed, lengths):
    qkv_w = low_weights[PIX:PIX + 3 * D]
    out_w = low_weights[PIX + 3 * D:PIX + 4 * D]
    up_w = low_weights[PIX + 4 * D:PIX + 4 * D + FF]
    down_w = low_weights[PIX + 4 * D + FF:]
    hidden_bias = low_vectors[5:9].reshape(FF)
    offsets = (jnp.cumsum(lengths) - lengths).astype(jnp.int32)
    places = jnp.arange(PMAX, dtype=jnp.int32)
    row_index = (offsets[:, None] + places[None, :]).astype(jnp.int32)
    keep_mask = (places[None, :] < lengths[:, None]).astype(jnp.float32)
    prefix = packed[row_index] * keep_mask[:, :, None]
    sequence = jnp.concatenate([image_rows, prefix], axis=1)
    columns = jnp.arange(SEQ, dtype=jnp.int32)
    key_ok = columns[None, :] < NP + lengths[:, None]
    row_ok = (key_ok & (lengths[:, None] > 0)).astype(jnp.float32)
    normed = low(layer_norm(sequence, low_vectors[0], low_vectors[1]))
    qkv_rows = low(low_back(jnp.einsum('srk,nk->srn', normed, qkv_w, precision=HIGHEST)))
    queries = qkv_rows[..., :D].reshape(RSLOT, SEQ, HEADS, HD)
    key_rows = qkv_rows[..., D:2 * D].reshape(RSLOT, SEQ, HEADS, HD)
    value_rows = qkv_rows[..., 2 * D:].reshape(RSLOT, SEQ, HEADS, HD)
    scores = low_back(jnp.einsum('sqhd,skhd->shqk', queries, key_rows, precision=HIGHEST) * HD ** (-0.5))
    scores = jnp.where(key_ok[:, None, None, :], scores, MASKED)
    attention = low(jax.nn.softmax(scores, axis=-1))
    context = jnp.einsum('shqk,skhd->sqhd', attention, value_rows, precision=HIGHEST).reshape(RSLOT, SEQ, D)
    context = low(low_back(context))
    residual = sequence + low_back(jnp.einsum('srk,nk->srn', context, out_w, precision=HIGHEST))
    mlp_in = low(layer_norm(residual, low_vectors[2], low_vectors[3]))
    pre_hidden = low_back(jnp.einsum('srk,fk->srf', mlp_in, up_w, precision=HIGHEST) + hidden_bias)
    hidden = low(jax.nn.gelu(pre_hidden, approximate=False))
    mlp_out = low_back(jnp.einsum('srf,fk->srk', hidden, down_w, precision=HIGHEST))
    return (residual + low_vectors[4] + mlp_out) * row_ok[:, :, None]

def forward(weights, vectors, pixels, packed, dest, prefix_len):
    low_weights = low(weights)
    low_vectors = low(vectors)
    stem_w = low_weights[:PIX]
    patches = low(low_back(jnp.einsum('nrp,pd->nrd', pixels, stem_w, precision=HIGHEST)))
    patches = patches.reshape(N_DP, IMG_DEV, NP, D)
    slot_ids = jnp.arange(RSLOT, dtype=jnp.int32)
    chooser = (dest[:, :, None] == slot_ids[None, None, :]).astype(jnp.float32)
    routed = jnp.einsum('njs,njpd->nspd', chooser, patches, precision=HIGHEST)
    device_ids = jnp.arange(N_DP, dtype=jnp.int32)
    source = ((device_ids[:, None] - 1 - slot_ids[None, :] // CAP) % N_DP).astype(jnp.int32)
    slot_grid = jnp.broadcast_to(slot_ids[None, :], source.shape).astype(jnp.int32)
    image_rows = routed[source, slot_grid]

    def one_device(carry, inputs):
        return (carry, text_device(low_weights, low_vectors, inputs[0], inputs[1], inputs[2]))
    _, outputs = lax.scan(jax.checkpoint(one_device), jnp.zeros((), jnp.float32), (image_rows, packed, prefix_len))
    return outputs

def reference(stream_rows, dest, prefix_len, weights, momentum, average, vectors, vec_momentum, vec_average, cotangent):
    rows_wide = stream_rows.astype(jnp.float32)

    def run(weight_in, vector_in, pixels, packed):
        return forward(weight_in, vector_in, pixels, packed, dest, prefix_len)
    outputs, pull = jax.vjp(run, weights, vectors, rows_wide[0], rows_wide[1])
    weight_grad, vec_grad, pixel_grad, packed_grad = pull(cotangent.astype(jnp.float32))
    rate = 0.5 * (D * IMAGES * NP) ** (-0.5)
    new_momentum = MOMENT * momentum + weight_grad
    new_weights = weights - rate * (weight_grad + MOMENT * new_momentum)
    new_average = DECAY * average + (1.0 - DECAY) * new_weights
    vec_new_momentum = MOMENT * vec_momentum + vec_grad
    vec_new = vectors - rate * (vec_grad + MOMENT * vec_new_momentum)
    vec_new_average = DECAY * vec_average + (1.0 - DECAY) * vec_new
    d_rows = jnp.stack([pixel_grad, packed_grad])
    return (outputs.astype(jnp.bfloat16), d_rows, weight_grad, new_momentum, new_average, new_weights, new_weights.astype(jnp.bfloat16), vec_grad, vec_new_momentum, vec_new_average, vec_new, vec_new.astype(jnp.bfloat16))
```

```python
import jax
import jax.numpy as jnp
from jax import lax
from jax.sharding import PartitionSpec as P

D = 768
HEADS = 12
HD = 64
FF = 3072
PIX = 768
NP = 196
PMAX = 64
SPAN = 4
IMG_DEV = 4
CAP = 2
RSLOT = 8
SEQ = 260
ROWS = 784
HALF = D // 2
OWN = IMG_DEV // 2
MSG = 336
VLANES = 256

EPSILON = 1e-06
MASKED = -1e30
MOMENT = 0.5
DECAY = 0.5
BF = jnp.bfloat16
F32 = jnp.float32
ALL = ("stream", "dp")


def along(value, steps):
    count = lax.axis_size("dp")
    pairs = [(source, (source + steps) % count) for source in range(count)]
    return lax.ppermute(value, "dp", pairs)


def swapped(value):
    return lax.ppermute(value, "stream", [(0, 1), (1, 0)])


def dot(a, b, contract):
    return lax.dot_general(a, b, ((contract[0:1], contract[1:2]), ((), ())), preferred_element_type=F32)


def layer_norm(values, gain_row, shift_row):
    centre = jnp.mean(values, axis=-1, keepdims=True)
    offset = values - centre
    spread = jnp.mean(offset * offset, axis=-1, keepdims=True)
    return offset * lax.rsqrt(spread + EPSILON) * gain_row + shift_row


def exact_gelu(values):
    return jax.nn.gelu(values, approximate=False)


def split_heads(rows):
    return rows.reshape(OWN, SEQ, HEADS, HD)


def body(
    stream_rows,
    dest,
    prefix_len,
    weights,
    momentum,
    average,
    vectors,
    vec_momentum,
    vec_average,
    cotangent,
):
    core = lax.axis_index("stream")
    first = core == 0
    n_dp = lax.axis_size("dp")
    n_dev = 2 * n_dp
    lane = vectors.shape[1]

    vec_flat = jnp.pad(vectors.astype(BF).reshape(9 * lane), (0, VLANES - 9 * lane))
    full_weights = lax.all_gather(weights.astype(BF), ALL, axis=0, tiled=True)
    full_vectors = lax.all_gather(vec_flat, ALL, axis=0, tiled=True)
    vector_rows = (
        full_vectors.reshape(n_dev, VLANES)[:, : 9 * lane]
        .reshape(n_dev, 9, lane)
        .transpose(1, 0, 2)
        .reshape(9, D)
        .astype(F32)
    )
    stem_w = full_weights[:PIX]
    qkv_w = full_weights[PIX : PIX + 3 * D]
    out_w = full_weights[PIX + 3 * D : PIX + 4 * D]
    up_w = full_weights[PIX + 4 * D : PIX + 4 * D + FF]
    down_w = full_weights[PIX + 4 * D + FF :]
    hidden_bias = vector_rows[5:9].reshape(FF)

    own_rows = stream_rows[0, 0]
    half_rows = ROWS // 2
    narrow = own_rows[:, :HALF]
    give = jnp.where(first, own_rows[half_rows:], jnp.concatenate([narrow[:half_rows], narrow[half_rows:]], axis=1))
    got = swapped(give)
    pixels = jnp.where(first, own_rows[:half_rows], got)
    packed = jnp.where(first, jnp.concatenate([got[:, :HALF], got[:, HALF:]], axis=0), own_rows[:, HALF:])

    lengths = prefix_len[0]
    offsets = jnp.cumsum(lengths) - lengths
    places = jnp.arange(PMAX, dtype=jnp.int32)
    row_index = offsets[:, None] + places[None, :]
    keep_mask = places[None, :] < lengths[:, None]
    rows_at = jnp.arange(ROWS, dtype=jnp.int32)
    pick = (
        (row_index.reshape(-1)[:, None] == rows_at[None, :]) & keep_mask.reshape(-1)[:, None]
    ).astype(BF)
    prefix_slots = dot(pick, packed, (1, 0)).astype(BF).reshape(RSLOT, PMAX, HALF)
    length_rows = jnp.broadcast_to(
        lengths.astype(BF)[:, None, None], (RSLOT, MSG - SEQ - PMAX, HALF)
    )
    messages = jnp.concatenate([cotangent[0], prefix_slots, length_rows], axis=1)
    arrived = jnp.concatenate(
        [along(messages[CAP * step : CAP * (step + 1)], -(step + 1)) for step in range(SPAN)]
    )
    slots = dest[0]

    def at_slot(j):
        return lax.dynamic_index_in_dim(arrived, slots[j], 0, keepdims=False)

    mine = jnp.stack([at_slot(OWN * core + k) for k in range(OWN)])
    others = jnp.stack([at_slot(OWN * (1 - core) + k) for k in range(OWN)])
    got = swapped(others)
    message = jnp.where(
        first, jnp.concatenate([mine, got], axis=-1), jnp.concatenate([got, mine], axis=-1)
    )
    seq_len = message[:, SEQ + PMAX, 0].astype(jnp.int32)
    columns = jnp.arange(SEQ, dtype=jnp.int32)
    key_ok = columns[None, :] < NP + seq_len[:, None]
    row_ok = key_ok.astype(F32)[:, :, None]
    out_grad = (message[:, :SEQ].astype(F32) * row_ok).astype(BF)
    prefix = message[:, SEQ : SEQ + PMAX]

    patches = dot(pixels, stem_w, (1, 0)).astype(BF).reshape(OWN, NP, D)
    sequence = jnp.concatenate([patches, prefix], axis=1).astype(F32)
    normed = layer_norm(sequence, vector_rows[0], vector_rows[1]).astype(BF)
    qkv_rows = dot(normed, qkv_w, (2, 1)).astype(BF)
    queries, keys, values = (split_heads(part) for part in jnp.split(qkv_rows, 3, axis=-1))
    scores = jnp.einsum("sqhd,skhd->shqk", queries, keys, preferred_element_type=F32) * HD ** (-0.5)
    scores = jnp.where(key_ok[:, None, None, :], scores, MASKED)
    attention = jax.nn.softmax(scores, axis=-1)
    attention_low = attention.astype(BF)
    context = jnp.einsum("shqk,skhd->sqhd", attention_low, values, preferred_element_type=F32)
    context = context.astype(BF).reshape(OWN, SEQ, D)
    residual = sequence + dot(context, out_w, (2, 1))
    mlp_in = layer_norm(residual, vector_rows[2], vector_rows[3]).astype(BF)
    pre_hidden = dot(mlp_in, up_w, (2, 1)) + hidden_bias
    hidden = exact_gelu(pre_hidden).astype(BF)
    part_out = dot(hidden, down_w, (2, 0))
    out_rows = ((part_out + residual + vector_rows[4]) * row_ok).astype(BF)

    def to_text(rows):
        count = rows.shape[1]
        kept = jnp.where(first, rows[..., :HALF], rows[..., HALF:])
        sent = jnp.where(first, rows[..., HALF:], rows[..., :HALF])
        other = swapped(sent)
        images = jnp.where(
            first, jnp.concatenate([kept, other]), jnp.concatenate([other, kept])
        ).reshape(IMG_DEV, count * HALF)
        slot_ids = jnp.arange(RSLOT, dtype=jnp.int32)
        chooser = (slot_ids[:, None] == slots[None, :]).astype(BF)
        placed = dot(chooser, images, (1, 0)).astype(BF).reshape(RSLOT, count, HALF)
        return jnp.concatenate(
            [along(placed[CAP * step : CAP * (step + 1)], step + 1) for step in range(SPAN)]
        )

    enc_out = to_text(out_rows)[None]

    d_down = jnp.einsum("srf,srk->fk", hidden, out_grad, preferred_element_type=F32).astype(BF)
    d_hidden = dot(out_grad, down_w, (2, 1))
    _, gelu_pull = jax.vjp(exact_gelu, pre_hidden)
    d_pre = gelu_pull(d_hidden)[0].astype(BF)
    d_bias = jnp.sum(d_pre, axis=(0, 1), dtype=F32)
    d_up = jnp.einsum("srf,srk->fk", d_pre, mlp_in, preferred_element_type=F32).astype(BF)
    d_mlp_in = dot(d_pre, up_w, (2, 0))
    _, norm2_pull = jax.vjp(layer_norm, residual, vector_rows[2], vector_rows[3])
    d_res_norm, d_gain2, d_shift2 = norm2_pull(d_mlp_in)
    d_residual = out_grad.astype(F32) + d_res_norm
    d_out_bias = jnp.sum(out_grad, axis=(0, 1), dtype=F32)

    d_attended = d_residual.astype(BF)
    d_out_w = jnp.einsum("srn,srk->nk", d_attended, context, preferred_element_type=F32).astype(BF)
    d_context = dot(d_attended, out_w, (2, 0)).astype(BF)
    d_context = split_heads(d_context)
    d_values = jnp.einsum(
        "shqk,sqhd->skhd", attention_low, d_context, preferred_element_type=F32
    )
    d_attention = jnp.einsum("sqhd,skhd->shqk", d_context, values, preferred_element_type=F32)
    d_scores = attention * (
        d_attention - jnp.sum(attention * d_attention, axis=-1, keepdims=True)
    )
    d_scores = d_scores.astype(BF)
    d_queries = jnp.einsum(
        "shqk,skhd->sqhd", d_scores, keys, preferred_element_type=F32
    ) * HD ** (-0.5)
    d_keys = jnp.einsum(
        "shqk,sqhd->skhd", d_scores, queries, preferred_element_type=F32
    ) * HD ** (-0.5)
    d_qkv = jnp.concatenate(
        [part.reshape(OWN, SEQ, D) for part in (d_queries, d_keys, d_values)], axis=-1
    ).astype(BF)
    d_qkv_w = jnp.einsum("srn,srk->nk", d_qkv, normed, preferred_element_type=F32).astype(BF)
    d_normed = dot(d_qkv, qkv_w, (2, 0))
    _, norm1_pull = jax.vjp(layer_norm, sequence, vector_rows[0], vector_rows[1])
    d_seq_norm, d_gain1, d_shift1 = norm1_pull(d_normed)
    d_sequence = (d_residual + d_seq_norm).astype(BF)
    d_patches = d_sequence[:, :NP].reshape(half_rows, D)
    d_prefix = d_sequence[:, NP:]
    d_stem = dot(pixels, d_patches, (0, 0)).astype(BF)
    d_pixels = dot(d_patches, stem_w, (1, 1))

    grad_local = jnp.concatenate([d_stem, d_qkv_w, d_out_w, d_up, d_down], axis=0)
    vec_local = jnp.concatenate(
        [jnp.stack([d_gain1, d_shift1, d_gain2, d_shift2, d_out_bias]), d_bias.reshape(4, D)]
    )
    vec_local = vec_local.reshape(9, n_dev, lane).transpose(1, 0, 2).reshape(n_dev, 9 * lane)
    vec_local = jnp.pad(vec_local, ((0, 0), (0, VLANES - 9 * lane)))
    weight_grad = lax.psum_scatter(grad_local, ALL, scatter_dimension=0, tiled=True).astype(F32)
    vec_grad = lax.psum_scatter(vec_local, ALL, scatter_dimension=0, tiled=True)
    vec_grad = vec_grad.reshape(VLANES)[: 9 * lane].reshape(9, lane)

    back = to_text(d_prefix).reshape(RSLOT * PMAX, HALF)
    d_packed = dot(pick, back, (0, 0)).astype(BF)
    pixels_low = d_pixels.astype(BF)
    give = jnp.where(
        first, jnp.concatenate([d_packed[:half_rows], d_packed[half_rows:]], axis=1), pixels_low
    )
    got = swapped(give)
    d_image_rows = jnp.concatenate([d_pixels, got.astype(F32)])
    d_text_rows = jnp.concatenate(
        [jnp.concatenate([got[:, :HALF], got[:, HALF:]], axis=0), d_packed], axis=1
    ).astype(F32)
    d_rows = jnp.where(first, d_image_rows, d_text_rows)[None, None]

    rate = 0.5 * (D * IMG_DEV * n_dp * NP) ** (-0.5)
    new_momentum = MOMENT * momentum + weight_grad
    new_weights = weights - rate * (weight_grad + MOMENT * new_momentum)
    new_average = DECAY * average + (1.0 - DECAY) * new_weights
    vec_new_momentum = MOMENT * vec_momentum + vec_grad
    vec_new = vectors - rate * (vec_grad + MOMENT * vec_new_momentum)
    vec_new_average = DECAY * vec_average + (1.0 - DECAY) * vec_new
    return (
        enc_out,
        d_rows,
        weight_grad,
        new_momentum,
        new_average,
        new_weights,
        new_weights.astype(BF),
        vec_grad,
        vec_new_momentum,
        vec_new_average,
        vec_new,
        vec_new.astype(BF),
    )


def solution(mesh):
    both = P(ALL, None)
    lanes = P(None, ALL)
    in_specs = (
        P("stream", "dp", None, None),
        P("dp", None),
        P("dp", None),
        both,
        both,
        both,
        lanes,
        lanes,
        lanes,
        P("dp", None, None, "stream"),
    )
    out_specs = (
        P("dp", None, None, "stream"),
        P("stream", "dp", None, None),
        both,
        both,
        both,
        both,
        both,
        lanes,
        lanes,
        lanes,
        lanes,
        lanes,
    )
    return jax.shard_map(body, mesh=mesh, in_specs=in_specs, out_specs=out_specs, check_vma=False)
```

```python
import jax
import jax.numpy as jnp
from jax import lax
from jax.experimental import pallas as pl
from jax.experimental.pallas import tpu as pltpu
from jax.sharding import PartitionSpec as P

D = 768
HEADS = 12
HD = 64
FF = 3072
PIX = 768
NP = 196
PMAX = 64
SPAN = 4
IMG_DEV = 4
CAP = 2
RSLOT = 8
SEQ = 260
ROWS = 784
HALF = D // 2
OWN = IMG_DEV // 2
MSG = 80
VLANES = 256

EPSILON = 1e-06
MASKED = -1e30
MOMENT = 0.5
DECAY = 0.5
BF = jnp.bfloat16
F32 = jnp.float32
ALL = ("stream", "dp")
MESH = pl.DeviceIdType.MESH
SLAB = 312
CUT = 160


def place():
    core = lax.axis_index("stream"); chip = lax.axis_index("dp")
    return core, chip, chip % 2, (chip // 2) % 2, chip // 4

def greet(core, chip):
    barrier = pltpu.get_barrier_semaphore()
    me = core*16+chip
    def one(k, carry):
        peer = (me + k) % 32
        pl.semaphore_signal(barrier, inc=1, device_id=(peer // 16, peer % 16), device_id_type=MESH)
        return carry
    lax.fori_loop(1, 32, one, 0)
    pl.semaphore_wait(barrier, 31)


NZ = 4

class Sends:
    def __init__(self): self.kept=[]
    def go(self, cond, make):
        if cond is None: make().start()
        else:
            @pl.when(cond)
            def _(): make().start()
        self.kept.append((cond, make))
    def drain(self):
        for cond, make in self.kept:
            if cond is None: make().wait_send()
            else:
                @pl.when(cond)
                def _(make=make): make().wait_send()

def gather_schedule(w_ref, out, core, chip, x, y, z, sems, sends):
    zs, zr, ds, dr, xs, xr, ys, yr, as_, ar, bs, br, ss, sr = sems
    base = core*16
    me = base + chip
    flat = chip % 4
    xn = chip + 1 - 2*x
    yn = chip + 2 - 4*y
    TOP=pl.ds(0,CUT); BOT=pl.ds(CUT,SLAB-CUT)
    sib=(1-core, chip)
    def rc(src, slab, ssem, rsem, dev, rows=None):
        dst = out.at[slab] if rows is None else out.at[slab, rows]
        return pltpu.make_async_remote_copy(src_ref=src, dst_ref=dst, send_sem=ssem, recv_sem=rsem, device_id=dev, device_id_type=MESH)
    def to_sib(src, slab, rows=None):
        rc(src, slab, ss, sr, sib, rows).start()
    def own():
        sends.go(None, lambda: rc(w_ref, me, xs.at[z], xr.at[z], (core, xn)))
        sends.go(None, lambda: rc(w_ref, me, ys.at[z], yr.at[z], (core, yn)))
        for k, sign in enumerate((1,-1)):
            sends.go((z+sign>=0)&(z+sign<NZ), lambda k=k, sign=sign: rc(w_ref, me, zs.at[k,z], zr.at[z], (core, chip+4*sign)))
        to_sib(w_ref, me)
    def column(t, sign):
        zz = z + sign*t
        here = (zz>=0)&(zz<NZ)
        slab = base + zz*4 + flat
        @pl.when(here)
        def _():
            rc(w_ref, slab, ss, zr.at[zz], sib).wait_recv()
        k = 0 if sign < 0 else 1
        onward = here & (z-sign>=0) & (z-sign<NZ)
        sends.go(onward, lambda: rc(out.at[slab], slab, zs.at[k,zz], zr.at[zz], (core, chip-4*sign)))
        sends.go(here, lambda: rc(out.at[slab], slab, xs.at[zz], xr.at[zz], (core,xn)))
        sends.go(here, lambda: rc(out.at[slab], slab, ys.at[zz], yr.at[zz], (core,yn)))
        @pl.when(here)
        def _(): to_sib(out.at[slab], slab)
    def plane(t, sign):
        zz = z + sign*t
        here = (zz>=0)&(zz<NZ)
        xslab = base + zz*4 + flat + 1 - 2*x
        yslab = base + zz*4 + flat + 2 - 4*y
        half = t in (0,3)
        def wx():
            rc(w_ref, xslab, ss, xr.at[zz], sib).wait_recv()
        def wy():
            rc(w_ref, yslab, ss, yr.at[zz], sib).wait_recv()
        pl.when(here)(wx)
        if half: sends.go(here, lambda: rc(out.at[xslab,TOP], xslab, as_.at[zz], ar.at[zz], (core,yn), TOP))
        pl.when(here)(wy)
        if half: sends.go(here, lambda: rc(out.at[yslab,BOT], yslab, bs.at[zz], br.at[zz], (core,xn), BOT))
        @pl.when(here)
        def _():
            to_sib(out.at[xslab], xslab); to_sib(out.at[yslab], yslab)
    def diag(t, sign):
        zz = z + sign*t
        here = (zz>=0)&(zz<NZ)
        slab = base + zz*4 + 3 - flat
        if t in (0,3):
            @pl.when(here)
            def _():
                rc(out.at[slab,TOP], slab, ss, ar.at[zz], sib, TOP).wait_recv()
                rc(out.at[slab,BOT], slab, ss, br.at[zz], sib, BOT).wait_recv()
        else:
            @pl.when(here)
            def _():
                rc(w_ref, slab, ss, dr.at[zz], sib).wait_recv()
        if t == 0:
            for k, s in enumerate((1,-1)):
                sends.go((z+s>=0)&(z+s<NZ), lambda k=k, s=s: rc(out.at[slab], slab, ds.at[k,zz], dr.at[zz], (core, chip+4*s)))
        if t == 1:
            k = 0 if sign < 0 else 1
            sends.go(here & (z-sign>=0) & (z-sign<NZ), lambda: rc(out.at[slab], slab, ds.at[k,zz], dr.at[zz], (core, chip-4*sign)))
        @pl.when(here)
        def _(): to_sib(out.at[slab], slab)
    def both(f, t):
        def run():
            f(t, 1)
            if t: f(t, -1)
        return run
    return [own, both(column,1), both(plane,0), both(column,2), both(diag,0), both(plane,1), both(column,3),
            both(diag,1), both(plane,2), both(plane,3), both(diag,2), both(diag,3)]

def gather_sems():
    dma=pltpu.SemaphoreType.DMA
    return [dma((2,4)), dma((4,)), dma((2,4)), dma((4,)), dma((4,)), dma((4,)), dma((4,)), dma((4,)), dma((4,)), dma((4,)), dma((4,)), dma((4,)), dma, dma]

def ag_kernel(w_ref, v_ref, out, vout, stage, lsem, vs, vr, *sems):
    core, chip, x, y, z = place()
    me = core*16+chip
    greet(core, chip)
    sends = Sends()
    steps = gather_schedule(w_ref, out, core, chip, x, y, z, sems, sends)
    steps[0]()
    cp = pltpu.make_async_copy(w_ref, stage, lsem.at[0]); cp.start()
    vcp = pltpu.make_async_copy(v_ref, vout.at[me], lsem.at[2]); vcp.start()
    def vsend(k, carry):
        peer = (me+k)%32
        pltpu.make_async_remote_copy(src_ref=v_ref, dst_ref=vout.at[me], send_sem=vs, recv_sem=vr, device_id=(peer//16, peer%16), device_id_type=MESH).start()
        return carry
    lax.fori_loop(1,32,vsend,0)
    cp.wait()
    cp2 = pltpu.make_async_copy(stage, out.at[me], lsem.at[1]); cp2.start()
    for step in steps[1:]: step()
    cp2.wait(); vcp.wait()
    other = pl.ds((1-core)*16,16)
    pltpu.make_async_copy(out.at[other], out.at[other], sems[-1]).wait()
    pltpu.make_async_copy(out.at[other], out.at[other], sems[-2]).wait()
    sends.drain()
    pltpu.make_async_copy(vout.at[pl.ds(0,31)], vout.at[pl.ds(0,31)], vr).wait()
    pltpu.make_async_copy(vout.at[pl.ds(0,31)], vout.at[pl.ds(0,31)], vs).wait()

def all_gather(w, v):
    A = pl.BlockSpec(memory_space=pl.ANY)
    dma=pltpu.SemaphoreType.DMA
    return pl.pallas_call(ag_kernel,
        out_shape=(jax.ShapeDtypeStruct((32,SLAB,D),BF), jax.ShapeDtypeStruct((32,8,128),BF)),
        in_specs=[A,A], out_specs=(A,A),
        scratch_shapes=[pltpu.VMEM((SLAB,D),BF), dma((3,)), dma, dma]+gather_sems(),
        cost_estimate=pl.CostEstimate(flops=0, bytes_accessed=200*2**20, transcendentals=0),
        compiler_params=pltpu.CompilerParams(collective_id=1, has_side_effects=True))(w,v)


STEP=48
def add_rows(dst, sources, lo, hi, out=None):
    n = (hi-lo)//STEP
    def piece(r, rows):
        tot = None
        for ref, off in sources:
            v = ref[pl.ds(r-off, rows), :].astype(F32)
            tot = v if tot is None else tot+v
        dst[pl.ds(r, rows), :] = tot.astype(dst.dtype)
    def loop(i, c):
        piece(pl.multiple_of(lo+i*STEP, 16), STEP); return c
    lax.fori_loop(0, n, loop, 0)
    if (hi-lo) % STEP: piece(lo+n*STEP, (hi-lo)%STEP)

def rs_kernel(g, vg, out, vout, obuf, sbuf, dzb, xb, yb, czb, ab, bb, vbuf, lsem, dzs, dzr, czs, czr, xs, xr, ys, yr, as_, ar, bs, br, ss, sr, vs, vr, vl):
    core, chip, x, y, z = place()
    me = core*16+chip
    flat = chip % 4
    xn = chip + 1 - 2*x
    yn = chip + 2 - 4*y
    sib = (1-core, chip)
    greet(core, chip)
    sends = Sends()
    def rc(src, dst, ssem, rsem, dev):
        return pltpu.make_async_remote_copy(src_ref=src, dst_ref=dst, send_sem=ssem, recv_sem=rsem, device_id=dev, device_id_type=MESH)
    fd, fx, fy = 3-flat, flat+1-2*x, flat+2-4*y
    order = [(fd,3),(fd,2),(fx,3),(fy,3),(fx,2),(fy,2),(fd,1),(flat,3),(fx,1),(fy,1),(fd,0),(flat,2),(fx,0),(fy,0),(flat,1),(flat,0)]
    def each(t, f):
        if t == 0: f(z, 0, None); return
        for sign in (1,-1):
            zz = z + sign*t
            here = (zz>=0)&(zz<NZ)
            f(zz, sign, here)
    def when(c, f):
        if c is None: f()
        else: pl.when(c)(f)
    for f, t in order:
        def st(zz, sign, here, f=f):
            i = zz*4+f
            def go():
                rc(g.at[(1-core)*16+i], sbuf.at[i], ss, sr.at[i], sib).start()
                pltpu.make_async_copy(g.at[core*16+i], obuf.at[i], lsem.at[i]).start()
            when(here, go)
        each(t, st)
    def vsend(k, carry):
        peer = (me+k)%32
        rc(vg.at[peer], vbuf.at[me], vs, vr, (peer//16, peer%16)).start()
        return carry
    lax.fori_loop(1,32,vsend,0)
    vcp = pltpu.make_async_copy(vg.at[me], vbuf.at[me], vl); vcp.start()
    def ready(i):
        pltpu.make_async_copy(g.at[i], obuf.at[i], lsem.at[i]).wait()
        rc(g.at[i], sbuf.at[i], ss, sr.at[i], sib).wait_recv()
    def diag(t):
        def f(zz, sign, here):
            i = zz*4+fd
            def work():
                ready(i)
                src=[(obuf.at[i],0),(sbuf.at[i],0)]
                if t == 1:
                    k = 0 if sign > 0 else 1
                    far = (z-sign>=0)&(z-sign<NZ)
                    @pl.when(far)
                    def _():
                        rc(g.at[i], dzb.at[k,zz], dzs.at[k,zz], dzr.at[k,zz], sib).wait_recv()
                        add_rows(obuf.at[i], src+[(dzb.at[k,zz],0)], 0, SLAB)
                    @pl.when(jnp.logical_not(far))
                    def _(): add_rows(obuf.at[i], src, 0, SLAB)
                elif t == 0:
                    for k, s in enumerate((1,-1)):
                        @pl.when((z-s>=0)&(z-s<NZ))
                        def _(k=k):
                            rc(g.at[i], dzb.at[k,zz], dzs.at[k,zz], dzr.at[k,zz], sib).wait_recv()
                    @pl.when((z>0)&(z<NZ-1))
                    def _(): add_rows(obuf.at[i], src+[(dzb.at[0,zz],0),(dzb.at[1,zz],0)], 0, SLAB)
                    @pl.when(z==0)
                    def _(): add_rows(obuf.at[i], src+[(dzb.at[1,zz],0)], 0, SLAB)
                    @pl.when(z==NZ-1)
                    def _(): add_rows(obuf.at[i], src+[(dzb.at[0,zz],0)], 0, SLAB)
                else:
                    add_rows(obuf.at[i], src, 0, SLAB)
            when(here, work)
            if t in (0,3):
                sends.go(here, lambda: rc(obuf.at[i, pl.ds(0,CUT)], ab.at[zz], as_.at[zz], ar.at[zz], (core,yn)))
                sends.go(here, lambda: rc(obuf.at[i, pl.ds(CUT,SLAB-CUT)], bb.at[zz], bs.at[zz], br.at[zz], (core,xn)))
            else:
                k = 0 if sign > 0 else 1
                sends.go(here, lambda: rc(obuf.at[i], dzb.at[k,zz], dzs.at[k,zz], dzr.at[k,zz], (core, chip+4*sign)))
        each(t, f)
    def plane(t):
        def f(zz, sign, here):
            ix, iy = zz*4+fx, zz*4+fy
            def work():
                ready(ix)
                sx=[(obuf.at[ix],0),(sbuf.at[ix],0)]
                if t in (0,3):
                    add_rows(obuf.at[ix], sx, CUT, SLAB)
                    rc(g.at[ix,pl.ds(0,CUT)], ab.at[zz], as_.at[zz], ar.at[zz], sib).wait_recv()
                    add_rows(obuf.at[ix], sx+[(ab.at[zz],0)], 0, CUT)
                else: add_rows(obuf.at[ix], sx, 0, SLAB)
            when(here, work)
            sends.go(here, lambda: rc(obuf.at[ix], xb.at[zz], xs.at[zz], xr.at[zz], (core,xn)))
            def work2():
                ready(iy)
                sy=[(obuf.at[iy],0),(sbuf.at[iy],0)]
                if t in (0,3):
                    add_rows(obuf.at[iy], sy, 0, CUT)
                    rc(g.at[iy,pl.ds(CUT,SLAB-CUT)], bb.at[zz], bs.at[zz], br.at[zz], sib).wait_recv()
                    add_rows(obuf.at[iy], sy+[(bb.at[zz],CUT)], CUT, SLAB)
                else: add_rows(obuf.at[iy], sy, 0, SLAB)
            when(here, work2)
            sends.go(here, lambda: rc(obuf.at[iy], yb.at[zz], ys.at[zz], yr.at[zz], (core,yn)))
        each(t, f)
    def column(t):
        def f(zz, sign, here):
            i = zz*4+flat
            k = 0 if sign > 0 else 1
            def work():
                ready(i)
                rc(g.at[i], xb.at[zz], xs.at[zz], xr.at[zz], sib).wait_recv()
                rc(g.at[i], yb.at[zz], ys.at[zz], yr.at[zz], sib).wait_recv()
                src=[(obuf.at[i],0),(sbuf.at[i],0),(xb.at[zz],0),(yb.at[zz],0)]
                far = (z-sign>=0)&(z-sign<NZ)
                @pl.when(far)
                def _():
                    rc(g.at[i], czb.at[k,zz], czs.at[k,zz], czr.at[k,zz], sib).wait_recv()
                    add_rows(obuf.at[i], src+[(czb.at[k,zz],0)], 0, SLAB)
                @pl.when(jnp.logical_not(far))
                def _(): add_rows(obuf.at[i], src, 0, SLAB)
            when(here, work)
            sends.go(here, lambda: rc(obuf.at[i], czb.at[k,zz], czs.at[k,zz], czr.at[k,zz], (core, chip+4*sign)))
        each(t, f)
    def final():
        i = z*4+flat
        ready(i)
        rc(g.at[i], xb.at[z], xs.at[z], xr.at[z], sib).wait_recv()
        rc(g.at[i], yb.at[z], ys.at[z], yr.at[z], sib).wait_recv()
        src=[(obuf.at[i],0),(sbuf.at[i],0),(xb.at[z],0),(yb.at[z],0)]
        for k, s in enumerate((1,-1)):
            @pl.when((z-s>=0)&(z-s<NZ))
            def _(k=k): rc(g.at[i], czb.at[k,z], czs.at[k,z], czr.at[k,z], sib).wait_recv()
        @pl.when((z>0)&(z<NZ-1))
        def _(): add_rows(out, src+[(czb.at[0,z],0),(czb.at[1,z],0)], 0, SLAB)
        @pl.when(z==0)
        def _(): add_rows(out, src+[(czb.at[1,z],0)], 0, SLAB)
        @pl.when(z==NZ-1)
        def _(): add_rows(out, src+[(czb.at[0,z],0)], 0, SLAB)
    diag(3); diag(2); plane(3); plane(2); diag(1); column(3); plane(1); diag(0); column(2); plane(0); column(1); final()
    vcp.wait()
    pltpu.make_async_copy(vbuf.at[pl.ds(0,31)], vbuf.at[pl.ds(0,31)], vr).wait()
    vout[...] = jnp.sum(vbuf[...], axis=0)
    pltpu.make_async_copy(vbuf.at[pl.ds(0,31)], vbuf.at[pl.ds(0,31)], vs).wait()
    pltpu.make_async_copy(sbuf, sbuf, ss).wait()
    sends.drain()

def reduce_scatter(g, vg):
    A = pl.BlockSpec(memory_space=pl.ANY)
    VM = pl.BlockSpec(memory_space=pltpu.VMEM)
    dma=pltpu.SemaphoreType.DMA
    slab=lambda *n: pltpu.VMEM(n+(SLAB,D),BF)
    return pl.pallas_call(rs_kernel,
        out_shape=(jax.ShapeDtypeStruct((SLAB,D),F32), jax.ShapeDtypeStruct((8,128),F32)),
        in_specs=[A,A], out_specs=(VM,VM),
        scratch_shapes=[slab(16), slab(16), slab(2,4), slab(4), slab(4), slab(2,4), pltpu.VMEM((4,CUT,D),BF), pltpu.VMEM((4,SLAB-CUT,D),BF), pltpu.VMEM((32,8,128),F32),
           dma((16,)), dma((2,4)), dma((2,4)), dma((2,4)), dma((2,4)), dma((4,)), dma((4,)), dma((4,)), dma((4,)), dma((4,)), dma((4,)), dma((4,)), dma((4,)), dma, dma((16,)), dma, dma, dma],
        cost_estimate=pl.CostEstimate(flops=0, bytes_accessed=200*2**20, transcendentals=0),
        compiler_params=pltpu.CompilerParams(collective_id=2, has_side_effects=True, vmem_limit_bytes=60*2**20))(g,vg)


def along(value, steps):
    count = lax.axis_size("dp")
    pairs = [(source, (source + steps) % count) for source in range(count)]
    return lax.ppermute(value, "dp", pairs)


def swapped(value):
    return lax.ppermute(value, "stream", [(0, 1), (1, 0)])


def dot(a, b, contract):
    return lax.dot_general(a, b, ((contract[0:1], contract[1:2]), ((), ())), preferred_element_type=F32)


NPAD=208
R=PMAX+NPAD
M=OWN*R
CH=512
LNB=32

def nn(a,b): return lax.dot_general(a,b,(((1,),(0,)),((),())),preferred_element_type=F32)
def nt(a,b): return lax.dot_general(a,b,(((1,),(1,)),((),())),preferred_element_type=F32)
def tn(a,b): return lax.dot_general(a,b,(((0,),(0,)),((),())),preferred_element_type=F32)

def erf(v):
    v = jnp.clip(v, -3.832506856900711, 3.832506856900711)
    s = v*v
    top = 0.00022905065861350646
    for c in (0.0034082910107109506, 0.050955695062380861, 0.18520832239976145, 1.128379143519084): top = top*s + c
    low = -1.1791602954361697e-7
    for c in (0.000023547966471313185, 0.0010179625278914885, 0.014070470171167667, 0.11098505178285362, 0.49746925110067538, 1.0): low = low*s + c
    return v*top/low

def gelu_both(v):
    phi = 0.5*(1.0+erf(v*0.7071067811865476))
    return v*phi, phi + v*(0.3989422804014327*jnp.exp(-0.5*v*v))

def rows_loop(f, block=LNB, total=M):
    def run(i, c):
        f(pl.ds(pl.multiple_of(i*block,16),block)); return c
    lax.fori_loop(0,total//block,run,0)

def norm_parts(v):
    centre = jnp.mean(v,axis=-1,keepdims=True); off = v-centre
    inv = lax.rsqrt(jnp.mean(off*off,axis=-1,keepdims=True)+EPSILON)
    return off*inv, inv

def norm_back(v, dn, gain):
    xhat, inv = norm_parts(v)
    dx = dn*gain
    d = (dx - jnp.mean(dx,axis=-1,keepdims=True) - xhat*jnp.mean(dx*xhat,axis=-1,keepdims=True))*inv
    return d, jnp.sum(dn*xhat,axis=0,keepdims=True), jnp.sum(dn,axis=0,keepdims=True)

def block_kernel(lens, pix, pre, og, vec, bias, w, enc, dx, dpix, vgrad, bgrad, g,
                 stem, qkvw, outw, upb, downb, gub, gdb, x, nrm, qkv, prob, ctx, res, mlp, big, acc, hid, dpr, f1, f2, wsem, csem, osem):
    def load(dst, lo, n, sem): return pltpu.make_async_copy(w.at[pl.ds(lo,n)], dst, sem)
    ls = load(stem,0,PIX,wsem.at[0]); lq = load(qkvw,PIX,3*D,wsem.at[1]); lo_ = load(outw,PIX+3*D,D,wsem.at[2])
    ls.start(); lq.start(); lo_.start()
    U=PIX+4*D; DN=U+FF
    def chunk(c, slot):
        at = pl.multiple_of(c*CH,16)
        return (pltpu.make_async_copy(w.at[pl.ds(U+at,CH)], upb.at[slot], csem.at[0,slot]),
                pltpu.make_async_copy(w.at[pl.ds(DN+at,CH)], downb.at[slot], csem.at[1,slot]))
    for cp in chunk(0,0): cp.start()
    ls.wait()
    for i in range(OWN):
        x[R*i:R*i+PMAX,:] = pre[i]
        x[R*i+PMAX:R*(i+1),:] = nn(pix[i], stem[...]).astype(BF)
    def norm1(rows):
        xhat,_ = norm_parts(x[rows,:].astype(F32))
        nrm[rows,:] = (xhat*vec[0:1,:]+vec[1:2,:]).astype(BF)
    rows_loop(norm1)
    lq.wait()
    for k in range(3):
        qkv[:,k*D:(k+1)*D] = nt(nrm[...], qkvw[k*D:(k+1)*D,:]).astype(BF)
    lane = lax.broadcasted_iota(jnp.int32,(1,128),1)
    low_half = lane < HD
    key = lax.broadcasted_iota(jnp.int32,(1,R),1)
    def heads(i, p):
        ln = lens[i]
        ok = (key < ln) | ((key >= PMAX) & (key < PMAX+NP))
        rows = pl.ds(pl.multiple_of(i*R,16),R)
        def part(k): return qkv[rows, pl.ds(pl.multiple_of(k*D+p*128,128),128)]
        return rows, ok, part(0), part(1), part(2)
    zero = jnp.zeros((),BF)
    def halves(v): return jnp.where(low_half,v,zero), jnp.where(low_half,zero,v)
    def attend(n, c):
        i, p = n//6, n%6
        rows, ok, q, k, v = heads(i,p)
        outs=[]
        for h, qh in enumerate(halves(q)):
            s = jnp.where(ok, nt(qh,k)*(HD**-0.5), MASKED)
            e = jnp.exp(s-jnp.max(s,axis=-1,keepdims=True))
            a = (e*(1.0/jnp.sum(e,axis=-1,keepdims=True))).astype(BF)
            prob[2*n+h] = a
            outs.append(nn(a,v))
        ctx[rows, pl.ds(pl.multiple_of(p*128,128),128)] = jnp.where(low_half,outs[0],outs[1]).astype(BF)
        return c
    lax.fori_loop(0,OWN*6,attend,0)
    lo_.wait()
    res[...] = nt(ctx[...], outw[...])
    def norm2(rows):
        r = res[rows,:] + x[rows,:].astype(F32)
        res[rows,:] = r
        xhat,_ = norm_parts(r)
        mlp[rows,:] = (xhat*vec[2:3,:]+vec[3:4,:]).astype(BF)
        big[rows,:] = r + vec[4:5,:]
        acc[rows,:] = jnp.zeros((LNB,D),F32)
    rows_loop(norm2)
    steps = FF//CH
    def store(c, slot):
        at = pl.multiple_of(c*CH,16)
        return (pltpu.make_async_copy(gub.at[slot], g.at[pl.ds(U+at,CH)], osem.at[0,slot]),
                pltpu.make_async_copy(gdb.at[slot], g.at[pl.ds(DN+at,CH)], osem.at[1,slot]))
    def ffn(c, carry):
        slot = lax.rem(c,2)
        for cp in chunk(c,slot): cp.wait()
        @pl.when(c+1<steps)
        def _():
            for cp in chunk(c+1,1-slot): cp.start()
        @pl.when(c>=2)
        def _():
            for cp in store(c-2,slot): cp.wait()
        cols = pl.ds(pl.multiple_of(c*CH,128),CH)
        f1[...] = nt(mlp[...], upb[slot])
        f2[...] = nt(og[...], downb[slot])
        b = bias[:,cols]
        def act(i, tot):
            rows = pl.ds(pl.multiple_of(i*16,16),16)
            h, dh = gelu_both(f1[rows,:]+b)
            hid[rows,:] = h.astype(BF)
            dp = (f2[rows,:]*dh).astype(BF)
            dpr[rows,:] = dp
            return tot + dp.astype(F32)
        tot = lax.fori_loop(0,M//16,act,jnp.zeros((16,CH),F32))
        bgrad[:,cols] = jnp.sum(tot,axis=0,keepdims=True)
        big[...] += nn(hid[...], downb[slot])
        acc[...] += nn(dpr[...], upb[slot])
        gub[slot] = tn(dpr[...], mlp[...]).astype(BF)
        gdb[slot] = tn(hid[...], og[...]).astype(BF)
        for cp in store(c,slot): cp.start()
        return carry
    lax.fori_loop(0,steps,ffn,0)
    def finish(rows):
        enc[rows,:] = big[rows,:].astype(BF)
    rows_loop(finish)
    def back2(i, c):
        rows = pl.ds(pl.multiple_of(i*LNB,16),LNB)
        o = og[rows,:].astype(F32)
        d, dg, dc = norm_back(res[rows,:], acc[rows,:], vec[2:3,:])
        d = d + o
        res[rows,:] = d
        dx[rows,:] = d.astype(BF)
        return (c[0]+dg, c[1]+dc, c[2]+jnp.sum(o,axis=0,keepdims=True))
    z = jnp.zeros((1,D),F32)
    dg2, dc2, dob = lax.fori_loop(0,M//LNB,back2,(z,z,z))
    vgrad[2:3,:] = dg2; vgrad[3:4,:] = dc2; vgrad[4:5,:] = dob
    for slot in range(2):
        for cp in store(steps-2+slot, slot): cp.wait()
    def put(src, lo, n, sem): return pltpu.make_async_copy(src, g.at[pl.ds(lo,n)], sem)
    big[...] = nn(dx[...], outw[...])

    dctx = mlp
    def lowc(rows): dctx[rows,:] = big[rows,:].astype(BF)
    rows_loop(lowc)
    outw[...] = tn(dx[...], ctx[...]).astype(BF)
    po = put(outw, PIX+3*D, D, wsem.at[2]); po.start()
    def attend_back(n, c):
        i, p = n//6, n%6
        rows, ok, q, k, v = heads(i,p)
        here = pl.ds(pl.multiple_of(p*128,128),128)
        dc = dctx[rows, here]
        dq=[]; dk=None; dv=None
        for h, (qh, dch) in enumerate(zip(halves(q), halves(dc))):
            a = prob[2*n+h]
            af = a.astype(F32)
            da = nt(dch, v)
            t = af*da
            ds_ = (t - af*jnp.sum(t,axis=-1,keepdims=True)).astype(BF)
            dq.append(nn(ds_,k))
            dk_ = tn(ds_,qh); dv_ = tn(a,dch)
            dk = dk_ if dk is None else dk+dk_
            dv = dv_ if dv is None else dv+dv_
        s = HD**-0.5
        def at(j): return pl.ds(pl.multiple_of(j*D+p*128,128),128)
        qkv[rows, at(0)] = (jnp.where(low_half,dq[0],dq[1])*s).astype(BF)
        qkv[rows, at(1)] = (dk*s).astype(BF)
        qkv[rows, at(2)] = dv.astype(BF)
        return c
    lax.fori_loop(0,OWN*6,attend_back,0)
    acc[...] = nn(qkv[...], qkvw[...])
    def back1(i, c):
        rows = pl.ds(pl.multiple_of(i*LNB,16),LNB)
        d, dg, dc = norm_back(x[rows,:].astype(F32), acc[rows,:], vec[0:1,:])
        dx[rows,:] = (res[rows,:] + d).astype(BF)
        return (c[0]+dg, c[1]+dc)
    dg1, dc1 = lax.fori_loop(0,M//LNB,back1,(z,z))
    vgrad[0:1,:] = dg1; vgrad[1:2,:] = dc1
    for k in range(3):
        qkvw[k*D:(k+1)*D,:] = tn(qkv[:,k*D:(k+1)*D], nrm[...]).astype(BF)
    pq = put(qkvw, PIX, 3*D, wsem.at[1]); pq.start()
    tot = None
    for i in range(OWN):
        dp = dx[R*i+PMAX:R*(i+1),:]
        dpix[i] = nt(dp, stem[...]).astype(BF)
        t = tn(pix[i], dp)
        tot = t if tot is None else tot+t
    stem[...] = tot.astype(BF)
    ps = put(stem, 0, PIX, wsem.at[0]); ps.start()
    po.wait(); pq.wait(); ps.wait()

def block(lens, pix, pre, og, vec, bias, w):
    A = pl.BlockSpec(memory_space=pl.ANY); V = pl.BlockSpec(memory_space=pltpu.VMEM); S=pl.BlockSpec(memory_space=pltpu.SMEM)
    dma=pltpu.SemaphoreType.DMA
    vm=lambda *s, t=BF: pltpu.VMEM(s,t)
    return pl.pallas_call(block_kernel,
        out_shape=(jax.ShapeDtypeStruct((M,D),BF), jax.ShapeDtypeStruct((M,D),BF), jax.ShapeDtypeStruct((OWN,NPAD,D),BF),
                   jax.ShapeDtypeStruct((8,D),F32), jax.ShapeDtypeStruct((1,FF),F32), jax.ShapeDtypeStruct((w.shape[0],D),BF)),
        in_specs=[S,V,V,V,V,V,A], out_specs=(V,V,V,V,V,A),
        scratch_shapes=[vm(PIX,D), vm(3*D,D), vm(D,D), vm(2,CH,D), vm(2,CH,D), vm(2,CH,D), vm(2,CH,D),
            vm(M,D), vm(M,D), vm(M,3*D), vm(2*OWN*6,R,R), vm(M,D), vm(M,D,t=F32), vm(M,D), vm(M,D,t=F32), vm(M,D,t=F32),
            vm(M,CH), vm(M,CH), vm(M,CH,t=F32), vm(M,CH,t=F32), dma((3,)), dma((2,2)), dma((2,2))],
        compiler_params=pltpu.CompilerParams(vmem_limit_bytes=62*2**20))(lens,pix,pre,og,vec,bias,w)


def gathered(weights, vectors, n_dp):
    n_dev = 2 * n_dp
    lane = vectors.shape[1]
    if n_dp == 16:
        block = jnp.pad(vectors.reshape(9 * lane), (0, 1024 - 9 * lane)).reshape(8, 128)
        slabs, blocks = all_gather(weights, block)
        full = slabs.reshape(n_dev * SLAB, D)
        blocks = blocks.reshape(n_dev, 1024)
    else:
        block = jnp.pad(vectors.reshape(9 * lane), (0, VLANES - 9 * lane))
        full = lax.all_gather(weights, ALL, axis=0, tiled=True)
        blocks = lax.all_gather(block, ALL, axis=0, tiled=True).reshape(n_dev, VLANES)
    rows = blocks[:, : 9 * lane].reshape(n_dev, 9, lane).transpose(1, 0, 2).reshape(9, D)
    return full, rows.astype(F32)


def summed(grads, vec_grads, n_dp):
    n_dev = 2 * n_dp
    lane = D // n_dev
    blocks = vec_grads.reshape(9, n_dev, lane).transpose(1, 0, 2).reshape(n_dev, 9 * lane)
    if n_dp == 16:
        blocks = jnp.pad(blocks, ((0, 0), (0, 1024 - 9 * lane))).reshape(n_dev, 8, 128)
        weight_grad, vec_grad = reduce_scatter(grads.reshape(n_dev, SLAB, D), blocks)
        vec_grad = vec_grad.reshape(1024)
    else:
        blocks = jnp.pad(blocks, ((0, 0), (0, VLANES - 9 * lane)))
        weight_grad = lax.psum_scatter(grads, ALL, scatter_dimension=0, tiled=True).astype(F32)
        vec_grad = lax.psum_scatter(blocks, ALL, scatter_dimension=0, tiled=True).reshape(VLANES)
    return weight_grad, vec_grad[: 9 * lane].reshape(9, lane)


def body(
    stream_rows,
    dest,
    prefix_len,
    weights,
    momentum,
    average,
    vectors,
    vec_momentum,
    vec_average,
    cotangent,
):
    core = lax.axis_index("stream")
    first = core == 0
    n_dp = lax.axis_size("dp")

    full_weights, vector_rows = gathered(weights.astype(BF), vectors.astype(BF), n_dp)
    own_rows = stream_rows[0, 0]
    half_rows = ROWS // 2
    narrow = own_rows[:, :HALF]
    give = jnp.where(first, own_rows[half_rows:], jnp.concatenate([narrow[:half_rows], narrow[half_rows:]], axis=1))
    got = swapped(give)
    pixels = jnp.where(first, own_rows[:half_rows], got)
    packed = jnp.where(first, jnp.concatenate([got[:, :HALF], got[:, HALF:]], axis=0), own_rows[:, HALF:])

    lengths = prefix_len[0]
    offsets = jnp.cumsum(lengths) - lengths
    places = jnp.arange(PMAX, dtype=jnp.int32)
    row_index = offsets[:, None] + places[None, :]
    keep_mask = places[None, :] < lengths[:, None]
    rows_at = jnp.arange(ROWS, dtype=jnp.int32)
    pick = (
        (row_index.reshape(-1)[:, None] == rows_at[None, :]) & keep_mask.reshape(-1)[:, None]
    ).astype(BF)
    prefix_slots = dot(pick, packed, (1, 0)).astype(BF).reshape(RSLOT, PMAX, HALF)
    length_rows = jnp.broadcast_to(
        lengths.astype(BF)[:, None, None], (RSLOT, MSG - PMAX, HALF)
    )
    columns = jnp.arange(SEQ, dtype=jnp.int32)
    row_ok = (columns[None, :] < NP + lengths[:, None]) & (lengths[:, None] > 0)
    kept_cot = jnp.where(row_ok[:, :, None], cotangent[0], jnp.zeros((), BF))
    cot_slots = jnp.concatenate(
        [kept_cot[:, NP:], kept_cot[:, :NP], jnp.zeros((RSLOT, NPAD - NP, HALF), BF)], axis=1
    )
    slots = dest[0]

    def to_images(rows):
        arrived = jnp.concatenate(
            [along(rows[CAP * step : CAP * (step + 1)], -(step + 1)) for step in range(SPAN)]
        )

        def at_slot(j):
            return lax.dynamic_index_in_dim(arrived, slots[j], 0, keepdims=False)

        mine = jnp.stack([at_slot(OWN * core + k) for k in range(OWN)])
        others = jnp.stack([at_slot(OWN * (1 - core) + k) for k in range(OWN)])
        got = swapped(others)
        return jnp.where(
            first, jnp.concatenate([mine, got], axis=-1), jnp.concatenate([got, mine], axis=-1)
        )

    message = to_images(jnp.concatenate([prefix_slots, length_rows], axis=1))
    seq_len = message[:, PMAX, 0].astype(jnp.int32)
    late, _ = lax.optimization_barrier((cot_slots, full_weights[:8, :128]))
    out_grad = to_images(late).reshape(M, D)
    prefix = message[:, :PMAX]
    pixels = jnp.pad(pixels.reshape(OWN, NP, D), ((0, 0), (0, NPAD - NP), (0, 0)))
    vec_in = jnp.pad(vector_rows[:5], ((0, 3), (0, 0)))
    enc, d_seq, d_pixels, vec5, d_bias, grad_local = block(
        seq_len, pixels, prefix, out_grad, vec_in, vector_rows[5:9].reshape(1, FF), full_weights
    )
    vec_local = jnp.concatenate([vec5[:5], d_bias.reshape(4, D)])
    d_pixels = d_pixels[:, :NP].reshape(half_rows, D)

    def to_text(rows):
        count = rows.shape[1]
        kept = jnp.where(first, rows[..., :HALF], rows[..., HALF:])
        sent = jnp.where(first, rows[..., HALF:], rows[..., :HALF])
        other = swapped(sent)
        images = jnp.where(
            first, jnp.concatenate([kept, other]), jnp.concatenate([other, kept])
        ).reshape(IMG_DEV, count * HALF)
        slot_ids = jnp.arange(RSLOT, dtype=jnp.int32)
        chooser = (slot_ids[:, None] == slots[None, :]).astype(BF)
        placed = dot(chooser, images, (1, 0)).astype(BF).reshape(RSLOT, count, HALF)
        return jnp.concatenate(
            [along(placed[CAP * step : CAP * (step + 1)], step + 1) for step in range(SPAN)]
        )

    back = to_text(jnp.concatenate([enc.reshape(OWN, R, D), d_seq.reshape(OWN, R, D)[:, :PMAX]], axis=1))
    enc_out = jnp.concatenate([back[:, PMAX : PMAX + NP], back[:, :PMAX]], axis=1)
    enc_out = jnp.where(row_ok[:, :, None], enc_out, jnp.zeros((), BF))[None]
    weight_grad, vec_grad = summed(grad_local, vec_local, n_dp)

    d_packed = dot(pick, back[:, R:].reshape(RSLOT * PMAX, HALF), (0, 0)).astype(BF)
    give = jnp.where(
        first, jnp.concatenate([d_packed[:half_rows], d_packed[half_rows:]], axis=1), d_pixels
    )
    got = swapped(give)
    d_image_rows = jnp.concatenate([d_pixels, got]).astype(F32)
    d_text_rows = jnp.concatenate(
        [jnp.concatenate([got[:, :HALF], got[:, HALF:]], axis=0), d_packed], axis=1
    ).astype(F32)
    d_rows = jnp.where(first, d_image_rows, d_text_rows)[None, None]

    rate = 0.5 * (D * IMG_DEV * n_dp * NP) ** (-0.5)
    new_momentum = MOMENT * momentum + weight_grad
    new_weights = weights - rate * (weight_grad + MOMENT * new_momentum)
    new_average = DECAY * average + (1.0 - DECAY) * new_weights
    vec_new_momentum = MOMENT * vec_momentum + vec_grad
    vec_new = vectors - rate * (vec_grad + MOMENT * vec_new_momentum)
    vec_new_average = DECAY * vec_average + (1.0 - DECAY) * vec_new
    return (
        enc_out,
        d_rows,
        weight_grad,
        new_momentum,
        new_average,
        new_weights,
        new_weights.astype(BF),
        vec_grad,
        vec_new_momentum,
        vec_new_average,
        vec_new,
        vec_new.astype(BF),
    )


def solution(mesh):
    both = P(ALL, None)
    lanes = P(None, ALL)
    in_specs = (
        P("stream", "dp", None, None),
        P("dp", None),
        P("dp", None),
        both,
        both,
        both,
        lanes,
        lanes,
        lanes,
        P("dp", None, None, "stream"),
    )
    out_specs = (
        P("dp", None, None, "stream"),
        P("stream", "dp", None, None),
        both,
        both,
        both,
        both,
        both,
        lanes,
        lanes,
        lanes,
        lanes,
        lanes,
    )
    return jax.shard_map(body, mesh=mesh, in_specs=in_specs, out_specs=out_specs, check_vma=False)
```

```python
import jax
import jax.numpy as jnp
from jax import lax
from jax.experimental import pallas as pl
from jax.experimental.pallas import tpu as pltpu
from jax.sharding import PartitionSpec as P

D = 768
HEADS = 12
HD = 64
FF = 3072
PIX = 768
NP = 196
PMAX = 64
SPAN = 4
IMG_DEV = 4
CAP = 2
RSLOT = 8
SEQ = 260
ROWS = 784
HALF = D // 2
OWN = IMG_DEV // 2
MSG = 80
VLANES = 256

EPSILON = 1e-06
MASKED = -1e30
MOMENT = 0.5
DECAY = 0.5
BF = jnp.bfloat16
F32 = jnp.float32
ALL = ("stream", "dp")
MESH = pl.DeviceIdType.MESH
SLAB = 312
CUT = 160


def place():
    core = lax.axis_index("stream"); chip = lax.axis_index("dp")
    return core, chip, chip % 2, (chip // 2) % 2, chip // 4

def greet(core, chip):
    barrier = pltpu.get_barrier_semaphore()
    me = core*16+chip
    def one(k, carry):
        peer = (me + k) % 32
        pl.semaphore_signal(barrier, inc=1, device_id=(peer // 16, peer % 16), device_id_type=MESH)
        return carry
    lax.fori_loop(1, 32, one, 0)
    pl.semaphore_wait(barrier, 31)


NZ = 4

class Sends:
    def __init__(self): self.kept=[]
    def go(self, cond, make):
        if cond is None: make().start()
        else:
            @pl.when(cond)
            def _(): make().start()
        self.kept.append((cond, make))
    def drain(self):
        for cond, make in self.kept:
            if cond is None: make().wait_send()
            else:
                @pl.when(cond)
                def _(make=make): make().wait_send()

def gather_schedule(w_ref, out, core, chip, x, y, z, sems, sends):
    zs, zr, ds, dr, xs, xr, ys, yr, as_, ar, bs, br, ss, sr = sems
    base = core*16
    me = base + chip
    flat = chip % 4
    xn = chip + 1 - 2*x
    yn = chip + 2 - 4*y
    TOP=pl.ds(0,CUT); BOT=pl.ds(CUT,SLAB-CUT)
    sib=(1-core, chip)
    def rc(src, slab, ssem, rsem, dev, rows=None):
        dst = out.at[slab] if rows is None else out.at[slab, rows]
        return pltpu.make_async_remote_copy(src_ref=src, dst_ref=dst, send_sem=ssem, recv_sem=rsem, device_id=dev, device_id_type=MESH)
    def to_sib(src, slab, rows=None):
        rc(src, slab, ss, sr, sib, rows).start()
    def own():
        sends.go(None, lambda: rc(w_ref, me, xs.at[z], xr.at[z], (core, xn)))
        sends.go(None, lambda: rc(w_ref, me, ys.at[z], yr.at[z], (core, yn)))
        for k, sign in enumerate((1,-1)):
            sends.go((z+sign>=0)&(z+sign<NZ), lambda k=k, sign=sign: rc(w_ref, me, zs.at[k,z], zr.at[z], (core, chip+4*sign)))
        to_sib(w_ref, me)
    def column(t, sign):
        zz = z + sign*t
        here = (zz>=0)&(zz<NZ)
        slab = base + zz*4 + flat
        @pl.when(here)
        def _():
            rc(w_ref, slab, ss, zr.at[zz], sib).wait_recv()
        k = 0 if sign < 0 else 1
        onward = here & (z-sign>=0) & (z-sign<NZ)
        sends.go(onward, lambda: rc(out.at[slab], slab, zs.at[k,zz], zr.at[zz], (core, chip-4*sign)))
        sends.go(here, lambda: rc(out.at[slab], slab, xs.at[zz], xr.at[zz], (core,xn)))
        sends.go(here, lambda: rc(out.at[slab], slab, ys.at[zz], yr.at[zz], (core,yn)))
        @pl.when(here)
        def _(): to_sib(out.at[slab], slab)
    def plane(t, sign):
        zz = z + sign*t
        here = (zz>=0)&(zz<NZ)
        xslab = base + zz*4 + flat + 1 - 2*x
        yslab = base + zz*4 + flat + 2 - 4*y
        half = t in (0,3)
        def wx():
            rc(w_ref, xslab, ss, xr.at[zz], sib).wait_recv()
        def wy():
            rc(w_ref, yslab, ss, yr.at[zz], sib).wait_recv()
        pl.when(here)(wx)
        if half: sends.go(here, lambda: rc(out.at[xslab,TOP], xslab, as_.at[zz], ar.at[zz], (core,yn), TOP))
        pl.when(here)(wy)
        if half: sends.go(here, lambda: rc(out.at[yslab,BOT], yslab, bs.at[zz], br.at[zz], (core,xn), BOT))
        @pl.when(here)
        def _():
            to_sib(out.at[xslab], xslab); to_sib(out.at[yslab], yslab)
    def diag(t, sign):
        zz = z + sign*t
        here = (zz>=0)&(zz<NZ)
        slab = base + zz*4 + 3 - flat
        if t in (0,3):
            @pl.when(here)
            def _():
                rc(out.at[slab,TOP], slab, ss, ar.at[zz], sib, TOP).wait_recv()
                rc(out.at[slab,BOT], slab, ss, br.at[zz], sib, BOT).wait_recv()
        else:
            @pl.when(here)
            def _():
                rc(w_ref, slab, ss, dr.at[zz], sib).wait_recv()
        if t == 0:
            for k, s in enumerate((1,-1)):
                sends.go((z+s>=0)&(z+s<NZ), lambda k=k, s=s: rc(out.at[slab], slab, ds.at[k,zz], dr.at[zz], (core, chip+4*s)))
        if t == 1:
            k = 0 if sign < 0 else 1
            sends.go(here & (z-sign>=0) & (z-sign<NZ), lambda: rc(out.at[slab], slab, ds.at[k,zz], dr.at[zz], (core, chip-4*sign)))
        @pl.when(here)
        def _(): to_sib(out.at[slab], slab)
    def both(f, t):
        def run():
            f(t, 1)
            if t: f(t, -1)
        return run
    return [own, both(column,1), both(plane,0), both(column,2), both(diag,0), both(plane,1), both(column,3),
            both(diag,1), both(plane,2), both(plane,3), both(diag,2), both(diag,3)]

def gather_sems():
    dma=pltpu.SemaphoreType.DMA
    return [dma((2,4)), dma((4,)), dma((2,4)), dma((4,)), dma((4,)), dma((4,)), dma((4,)), dma((4,)), dma((4,)), dma((4,)), dma((4,)), dma((4,)), dma, dma]

def ag_kernel(w_ref, v_ref, out, vout, stage, lsem, vs, vr, *sems):
    core, chip, x, y, z = place()
    me = core*16+chip
    greet(core, chip)
    sends = Sends()
    steps = gather_schedule(w_ref, out, core, chip, x, y, z, sems, sends)
    steps[0]()
    cp = pltpu.make_async_copy(w_ref, stage, lsem.at[0]); cp.start()
    vcp = pltpu.make_async_copy(v_ref, vout.at[me], lsem.at[2]); vcp.start()
    def vsend(k, carry):
        peer = (me+k)%32
        pltpu.make_async_remote_copy(src_ref=v_ref, dst_ref=vout.at[me], send_sem=vs, recv_sem=vr, device_id=(peer//16, peer%16), device_id_type=MESH).start()
        return carry
    lax.fori_loop(1,32,vsend,0)
    cp.wait()
    cp2 = pltpu.make_async_copy(stage, out.at[me], lsem.at[1]); cp2.start()
    for step in steps[1:]: step()
    cp2.wait(); vcp.wait()
    other = pl.ds((1-core)*16,16)
    pltpu.make_async_copy(out.at[other], out.at[other], sems[-1]).wait()
    pltpu.make_async_copy(out.at[other], out.at[other], sems[-2]).wait()
    sends.drain()
    pltpu.make_async_copy(vout.at[pl.ds(0,31)], vout.at[pl.ds(0,31)], vr).wait()
    pltpu.make_async_copy(vout.at[pl.ds(0,31)], vout.at[pl.ds(0,31)], vs).wait()

def all_gather(w, v):
    A = pl.BlockSpec(memory_space=pl.ANY)
    dma=pltpu.SemaphoreType.DMA
    return pl.pallas_call(ag_kernel,
        out_shape=(jax.ShapeDtypeStruct((32,SLAB,D),BF), jax.ShapeDtypeStruct((32,8,128),BF)),
        in_specs=[A,A], out_specs=(A,A),
        scratch_shapes=[pltpu.VMEM((SLAB,D),BF), dma((3,)), dma, dma]+gather_sems(),
        cost_estimate=pl.CostEstimate(flops=0, bytes_accessed=200*2**20, transcendentals=0),
        compiler_params=pltpu.CompilerParams(collective_id=1, has_side_effects=True))(w,v)


STEP=48
def add_rows(dst, sources, lo, hi, out=None):
    n = (hi-lo)//STEP
    def piece(r, rows):
        tot = None
        for ref, off in sources:
            v = ref[pl.ds(r-off, rows), :].astype(F32)
            tot = v if tot is None else tot+v
        dst[pl.ds(r, rows), :] = tot.astype(dst.dtype)
    def loop(i, c):
        piece(pl.multiple_of(lo+i*STEP, 16), STEP); return c
    lax.fori_loop(0, n, loop, 0)
    if (hi-lo) % STEP: piece(lo+n*STEP, (hi-lo)%STEP)

def rs_kernel(g, vg, out, vout, obuf, sbuf, dzb, xb, yb, czb, ab, bb, vbuf, lsem, dzs, dzr, czs, czr, xs, xr, ys, yr, as_, ar, bs, br, ss, sr, vs, vr, vl):
    core, chip, x, y, z = place()
    me = core*16+chip
    flat = chip % 4
    xn = chip + 1 - 2*x
    yn = chip + 2 - 4*y
    sib = (1-core, chip)
    greet(core, chip)
    sends = Sends()
    def rc(src, dst, ssem, rsem, dev):
        return pltpu.make_async_remote_copy(src_ref=src, dst_ref=dst, send_sem=ssem, recv_sem=rsem, device_id=dev, device_id_type=MESH)
    fd, fx, fy = 3-flat, flat+1-2*x, flat+2-4*y
    order = [(fd,3),(fd,2),(fx,3),(fy,3),(fx,2),(fy,2),(fd,1),(flat,3),(fx,1),(fy,1),(fd,0),(flat,2),(fx,0),(fy,0),(flat,1),(flat,0)]
    def each(t, f):
        if t == 0: f(z, 0, None); return
        for sign in (1,-1):
            zz = z + sign*t
            here = (zz>=0)&(zz<NZ)
            f(zz, sign, here)
    def when(c, f):
        if c is None: f()
        else: pl.when(c)(f)
    for f, t in order:
        def st(zz, sign, here, f=f):
            i = zz*4+f
            def go():
                rc(g.at[(1-core)*16+i], sbuf.at[i], ss, sr.at[i], sib).start()
                pltpu.make_async_copy(g.at[core*16+i], obuf.at[i], lsem.at[i]).start()
            when(here, go)
        each(t, st)
    def vsend(k, carry):
        peer = (me+k)%32
        rc(vg.at[peer], vbuf.at[me], vs, vr, (peer//16, peer%16)).start()
        return carry
    lax.fori_loop(1,32,vsend,0)
    vcp = pltpu.make_async_copy(vg.at[me], vbuf.at[me], vl); vcp.start()
    def ready(i):
        pltpu.make_async_copy(g.at[i], obuf.at[i], lsem.at[i]).wait()
        rc(g.at[i], sbuf.at[i], ss, sr.at[i], sib).wait_recv()
    def diag(t):
        def f(zz, sign, here):
            i = zz*4+fd
            def work():
                ready(i)
                src=[(obuf.at[i],0),(sbuf.at[i],0)]
                if t == 1:
                    k = 0 if sign > 0 else 1
                    far = (z-sign>=0)&(z-sign<NZ)
                    @pl.when(far)
                    def _():
                        rc(g.at[i], dzb.at[k,zz], dzs.at[k,zz], dzr.at[k,zz], sib).wait_recv()
                        add_rows(obuf.at[i], src+[(dzb.at[k,zz],0)], 0, SLAB)
                    @pl.when(jnp.logical_not(far))
                    def _(): add_rows(obuf.at[i], src, 0, SLAB)
                elif t == 0:
                    for k, s in enumerate((1,-1)):
                        @pl.when((z-s>=0)&(z-s<NZ))
                        def _(k=k):
                            rc(g.at[i], dzb.at[k,zz], dzs.at[k,zz], dzr.at[k,zz], sib).wait_recv()
                    @pl.when((z>0)&(z<NZ-1))
                    def _(): add_rows(obuf.at[i], src+[(dzb.at[0,zz],0),(dzb.at[1,zz],0)], 0, SLAB)
                    @pl.when(z==0)
                    def _(): add_rows(obuf.at[i], src+[(dzb.at[1,zz],0)], 0, SLAB)
                    @pl.when(z==NZ-1)
                    def _(): add_rows(obuf.at[i], src+[(dzb.at[0,zz],0)], 0, SLAB)
                else:
                    add_rows(obuf.at[i], src, 0, SLAB)
            when(here, work)
            if t in (0,3):
                sends.go(here, lambda: rc(obuf.at[i, pl.ds(0,CUT)], ab.at[zz], as_.at[zz], ar.at[zz], (core,yn)))
                sends.go(here, lambda: rc(obuf.at[i, pl.ds(CUT,SLAB-CUT)], bb.at[zz], bs.at[zz], br.at[zz], (core,xn)))
            else:
                k = 0 if sign > 0 else 1
                sends.go(here, lambda: rc(obuf.at[i], dzb.at[k,zz], dzs.at[k,zz], dzr.at[k,zz], (core, chip+4*sign)))
        each(t, f)
    def plane(t):
        def f(zz, sign, here):
            ix, iy = zz*4+fx, zz*4+fy
            def work():
                ready(ix)
                sx=[(obuf.at[ix],0),(sbuf.at[ix],0)]
                if t in (0,3):
                    add_rows(obuf.at[ix], sx, CUT, SLAB)
                    rc(g.at[ix,pl.ds(0,CUT)], ab.at[zz], as_.at[zz], ar.at[zz], sib).wait_recv()
                    add_rows(obuf.at[ix], sx+[(ab.at[zz],0)], 0, CUT)
                else: add_rows(obuf.at[ix], sx, 0, SLAB)
            when(here, work)
            sends.go(here, lambda: rc(obuf.at[ix], xb.at[zz], xs.at[zz], xr.at[zz], (core,xn)))
            def work2():
                ready(iy)
                sy=[(obuf.at[iy],0),(sbuf.at[iy],0)]
                if t in (0,3):
                    add_rows(obuf.at[iy], sy, 0, CUT)
                    rc(g.at[iy,pl.ds(CUT,SLAB-CUT)], bb.at[zz], bs.at[zz], br.at[zz], sib).wait_recv()
                    add_rows(obuf.at[iy], sy+[(bb.at[zz],CUT)], CUT, SLAB)
                else: add_rows(obuf.at[iy], sy, 0, SLAB)
            when(here, work2)
            sends.go(here, lambda: rc(obuf.at[iy], yb.at[zz], ys.at[zz], yr.at[zz], (core,yn)))
        each(t, f)
    def column(t):
        def f(zz, sign, here):
            i = zz*4+flat
            k = 0 if sign > 0 else 1
            def work():
                ready(i)
                rc(g.at[i], xb.at[zz], xs.at[zz], xr.at[zz], sib).wait_recv()
                rc(g.at[i], yb.at[zz], ys.at[zz], yr.at[zz], sib).wait_recv()
                src=[(obuf.at[i],0),(sbuf.at[i],0),(xb.at[zz],0),(yb.at[zz],0)]
                far = (z-sign>=0)&(z-sign<NZ)
                @pl.when(far)
                def _():
                    rc(g.at[i], czb.at[k,zz], czs.at[k,zz], czr.at[k,zz], sib).wait_recv()
                    add_rows(obuf.at[i], src+[(czb.at[k,zz],0)], 0, SLAB)
                @pl.when(jnp.logical_not(far))
                def _(): add_rows(obuf.at[i], src, 0, SLAB)
            when(here, work)
            sends.go(here, lambda: rc(obuf.at[i], czb.at[k,zz], czs.at[k,zz], czr.at[k,zz], (core, chip+4*sign)))
        each(t, f)
    def final():
        i = z*4+flat
        ready(i)
        rc(g.at[i], xb.at[z], xs.at[z], xr.at[z], sib).wait_recv()
        rc(g.at[i], yb.at[z], ys.at[z], yr.at[z], sib).wait_recv()
        src=[(obuf.at[i],0),(sbuf.at[i],0),(xb.at[z],0),(yb.at[z],0)]
        for k, s in enumerate((1,-1)):
            @pl.when((z-s>=0)&(z-s<NZ))
            def _(k=k): rc(g.at[i], czb.at[k,z], czs.at[k,z], czr.at[k,z], sib).wait_recv()
        @pl.when((z>0)&(z<NZ-1))
        def _(): add_rows(out, src+[(czb.at[0,z],0),(czb.at[1,z],0)], 0, SLAB)
        @pl.when(z==0)
        def _(): add_rows(out, src+[(czb.at[1,z],0)], 0, SLAB)
        @pl.when(z==NZ-1)
        def _(): add_rows(out, src+[(czb.at[0,z],0)], 0, SLAB)
    diag(3); diag(2); plane(3); plane(2); diag(1); column(3); plane(1); diag(0); column(2); plane(0); column(1); final()
    vcp.wait()
    pltpu.make_async_copy(vbuf.at[pl.ds(0,31)], vbuf.at[pl.ds(0,31)], vr).wait()
    vout[...] = jnp.sum(vbuf[...], axis=0)
    pltpu.make_async_copy(vbuf.at[pl.ds(0,31)], vbuf.at[pl.ds(0,31)], vs).wait()
    pltpu.make_async_copy(sbuf, sbuf, ss).wait()
    sends.drain()

def reduce_scatter(g, vg):
    A = pl.BlockSpec(memory_space=pl.ANY)
    VM = pl.BlockSpec(memory_space=pltpu.VMEM)
    dma=pltpu.SemaphoreType.DMA
    slab=lambda *n: pltpu.VMEM(n+(SLAB,D),BF)
    return pl.pallas_call(rs_kernel,
        out_shape=(jax.ShapeDtypeStruct((SLAB,D),F32), jax.ShapeDtypeStruct((8,128),F32)),
        in_specs=[A,A], out_specs=(VM,VM),
        scratch_shapes=[slab(16), slab(16), slab(2,4), slab(4), slab(4), slab(2,4), pltpu.VMEM((4,CUT,D),BF), pltpu.VMEM((4,SLAB-CUT,D),BF), pltpu.VMEM((32,8,128),F32),
           dma((16,)), dma((2,4)), dma((2,4)), dma((2,4)), dma((2,4)), dma((4,)), dma((4,)), dma((4,)), dma((4,)), dma((4,)), dma((4,)), dma((4,)), dma((4,)), dma, dma((16,)), dma, dma, dma],
        cost_estimate=pl.CostEstimate(flops=0, bytes_accessed=200*2**20, transcendentals=0),
        compiler_params=pltpu.CompilerParams(collective_id=2, has_side_effects=True, vmem_limit_bytes=60*2**20))(g,vg)


def swapped(value):
    return lax.ppermute(value, "stream", [(0, 1), (1, 0)])


def dot(a, b, contract):
    return lax.dot_general(a, b, ((contract[0:1], contract[1:2]), ((), ())), preferred_element_type=F32)


NPAD=208
R=PMAX+NPAD
M=OWN*R
CH=512
LNB=32

def nn(a,b): return lax.dot_general(a,b,(((1,),(0,)),((),())),preferred_element_type=F32)
def nt(a,b): return lax.dot_general(a,b,(((1,),(1,)),((),())),preferred_element_type=F32)
def tn(a,b): return lax.dot_general(a,b,(((0,),(0,)),((),())),preferred_element_type=F32)

def erf(v):
    v = jnp.clip(v, -3.832506856900711, 3.832506856900711)
    s = v*v
    top = 0.00022905065861350646
    for c in (0.0034082910107109506, 0.050955695062380861, 0.18520832239976145, 1.128379143519084): top = top*s + c
    low = -1.1791602954361697e-7
    for c in (0.000023547966471313185, 0.0010179625278914885, 0.014070470171167667, 0.11098505178285362, 0.49746925110067538, 1.0): low = low*s + c
    return v*top/low

def gelu_both(v):
    phi = 0.5*(1.0+erf(v*0.7071067811865476))
    return v*phi, phi + v*(0.3989422804014327*jnp.exp(-0.5*v*v))

def rows_loop(f, block=LNB, total=M):
    def run(i, c):
        f(pl.ds(pl.multiple_of(i*block,16),block)); return c
    lax.fori_loop(0,total//block,run,0)

def norm_parts(v):
    centre = jnp.mean(v,axis=-1,keepdims=True); off = v-centre
    inv = lax.rsqrt(jnp.mean(off*off,axis=-1,keepdims=True)+EPSILON)
    return off*inv, inv

def norm_back(v, dn, gain):
    xhat, inv = norm_parts(v)
    dx = dn*gain
    d = (dx - jnp.mean(dx,axis=-1,keepdims=True) - xhat*jnp.mean(dx*xhat,axis=-1,keepdims=True))*inv
    return d, jnp.sum(dn*xhat,axis=0,keepdims=True), jnp.sum(dn,axis=0,keepdims=True)

def block_kernel(dest, inv, prefm, cotm, pix, vec, bias, w, dx, dpix, vgrad, bgrad, g, encm, dprem,
                 arp, arc, gvp, gtp, gvc, gtc, img, msg, pim, pmsg, og, psem, gsem, stem, qkvw, outw, upb, downb, gub, gdb, x, nrm, qkv, prob, ctx, res, mlp, big, acc, hid, dpr, f1, f2, wsem, csem, osem):
    core = lax.axis_index("stream")
    chip = lax.axis_index("dp")
    n_dp = lax.axis_size("dp")
    sib = (1-core, chip)
    barrier = pltpu.get_barrier_semaphore()
    for t in range(1, SPAN+1):
        for peer in ((chip+t)%n_dp, (chip+n_dp-t)%n_dp):
            pl.semaphore_signal(barrier, inc=1, device_id=(core,peer), device_id_type=MESH)
    pl.semaphore_signal(barrier, inc=1, device_id=sib, device_id_type=MESH)
    pl.semaphore_wait(barrier, 2*SPAN+1)
    def rc(src, dst, k, i, dev):
        return pltpu.make_async_remote_copy(src_ref=src, dst_ref=dst, send_sem=psem.at[0,k,i], recv_sem=psem.at[1,k,i], device_id=dev, device_id_type=MESH)
    def pair(t): return pl.ds(CAP*t,CAP)
    down = [(core,(chip+n_dp-t-1)%n_dp) for t in range(SPAN)]
    up = [(core,(chip+t+1)%n_dp) for t in range(SPAN)]
    pin = [rc(prefm.at[pair(t)], arp.at[pair(t)], 0, t, down[t]) for t in range(SPAN)]
    cin = [rc(cotm.at[pair(t)], arc.at[pair(t)], 1, t, down[t]) for t in range(SPAN)]
    for cp in pin: cp.start()
    def mine(k): return dest[OWN*core+k]
    def theirs(k): return dest[OWN*(1-core)+k]
    own_half = pl.ds(pl.multiple_of(core*HALF,128),HALF)
    other_half = pl.ds(pl.multiple_of((1-core)*HALF,128),HALF)
    pswap = pltpu.make_async_remote_copy(src_ref=gvp, dst_ref=gtp, send_sem=gsem.at[0,0], recv_sem=gsem.at[1,0], device_id=sib, device_id_type=MESH)
    cswap = pltpu.make_async_remote_copy(src_ref=gvc, dst_ref=gtc, send_sem=gsem.at[0,1], recv_sem=gsem.at[1,1], device_id=sib, device_id_type=MESH)
    def load(dst, lo, n, sem): return pltpu.make_async_copy(w.at[pl.ds(lo,n)], dst, sem)
    ls = load(stem,0,PIX,wsem.at[0]); lq = load(qkvw,PIX,3*D,wsem.at[1]); lo_ = load(outw,PIX+3*D,D,wsem.at[2])
    ls.start(); lq.start(); lo_.start()
    U=PIX+4*D; DN=U+FF
    def chunk(c, slot):
        at = pl.multiple_of(c*CH,16)
        return (pltpu.make_async_copy(w.at[pl.ds(U+at,CH)], upb.at[slot], csem.at[0,slot]),
                pltpu.make_async_copy(w.at[pl.ds(DN+at,CH)], downb.at[slot], csem.at[1,slot]))
    for cp in chunk(0,0): cp.start()
    for cp in cin: cp.start()
    for cp in pin: cp.wait_recv()
    for k in range(OWN):
        gvp[k] = arp[theirs(k)]
    lens = []
    for k in range(OWN):
        x[R*k:R*k+PMAX, own_half] = arp[mine(k), 0:PMAX, :]
        lens.append(arp[mine(k), PMAX:PMAX+16, :].astype(F32)[0:1,0:1])
    pswap.start()
    ls.wait()
    for i in range(OWN):
        x[R*i+PMAX:R*(i+1),:] = nn(pix[i], stem[...]).astype(BF)
    pswap.wait_recv()
    for k in range(OWN):
        x[R*k:R*k+PMAX, other_half] = gtp[k, 0:PMAX, :]
    def norm1(rows):
        xhat,_ = norm_parts(x[rows,:].astype(F32))
        nrm[rows,:] = (xhat*vec[0:1,:]+vec[1:2,:]).astype(BF)
    rows_loop(norm1)
    lq.wait()
    for k in range(3):
        qkv[:,k*D:(k+1)*D] = nt(nrm[...], qkvw[k*D:(k+1)*D,:]).astype(BF)
    lane = lax.broadcasted_iota(jnp.int32,(1,128),1)
    low_half = lane < HD
    key = lax.broadcasted_iota(jnp.int32,(1,R),1)
    def heads(i, p):
        ln = jnp.where(i == 0, lens[0], lens[1])
        ok = (key.astype(F32) < ln) | ((key >= PMAX) & (key < PMAX+NP))
        rows = pl.ds(pl.multiple_of(i*R,16),R)
        def part(k): return qkv[rows, pl.ds(pl.multiple_of(k*D+p*128,128),128)]
        return rows, ok, part(0), part(1), part(2)
    zero = jnp.zeros((),BF)
    def halves(v): return jnp.where(low_half,v,zero), jnp.where(low_half,zero,v)
    def attend(n, c):
        i, p = n//6, n%6
        rows, ok, q, k, v = heads(i,p)
        outs=[]
        for h, qh in enumerate(halves(q)):
            s = jnp.where(ok, nt(qh,k)*(HD**-0.5), MASKED)
            e = jnp.exp(s-jnp.max(s,axis=-1,keepdims=True))
            a = (e*(1.0/jnp.sum(e,axis=-1,keepdims=True))).astype(BF)
            prob[2*n+h] = a
            outs.append(nn(a,v))
        ctx[rows, pl.ds(pl.multiple_of(p*128,128),128)] = jnp.where(low_half,outs[0],outs[1]).astype(BF)
        return c
    lax.fori_loop(0,OWN*6,attend,0)
    lo_.wait()
    res[...] = nt(ctx[...], outw[...])
    def norm2(rows):
        r = res[rows,:] + x[rows,:].astype(F32)
        res[rows,:] = r
        xhat,_ = norm_parts(r)
        mlp[rows,:] = (xhat*vec[2:3,:]+vec[3:4,:]).astype(BF)
        big[rows,:] = r + vec[4:5,:]
        acc[rows,:] = jnp.zeros((LNB,D),F32)
    rows_loop(norm2)
    for cp in cin: cp.wait_recv()
    for k in range(OWN):
        gvc[k] = arc[theirs(k)]
    for k in range(OWN):
        og[R*k:R*(k+1), own_half] = arc[mine(k)]
    cswap.start()
    cswap.wait_recv()
    for k in range(OWN):
        og[R*k:R*(k+1), other_half] = gtc[k]
    steps = FF//CH
    def store(c, slot):
        at = pl.multiple_of(c*CH,16)
        return (pltpu.make_async_copy(gub.at[slot], g.at[pl.ds(U+at,CH)], osem.at[0,slot]),
                pltpu.make_async_copy(gdb.at[slot], g.at[pl.ds(DN+at,CH)], osem.at[1,slot]))
    def ffn(c, carry):
        slot = lax.rem(c,2)
        for cp in chunk(c,slot): cp.wait()
        @pl.when(c+1<steps)
        def _():
            for cp in chunk(c+1,1-slot): cp.start()
        @pl.when(c>=2)
        def _():
            for cp in store(c-2,slot): cp.wait()
        cols = pl.ds(pl.multiple_of(c*CH,128),CH)
        f1[...] = nt(mlp[...], upb[slot])
        f2[...] = nt(og[...], downb[slot])
        b = bias[:,cols]
        def act(i, tot):
            rows = pl.ds(pl.multiple_of(i*16,16),16)
            h, dh = gelu_both(f1[rows,:]+b)
            hid[rows,:] = h.astype(BF)
            dp = (f2[rows,:]*dh).astype(BF)
            dpr[rows,:] = dp
            return tot + dp.astype(F32)
        tot = lax.fori_loop(0,M//16,act,jnp.zeros((16,CH),F32))
        bgrad[:,cols] = jnp.sum(tot,axis=0,keepdims=True)
        big[...] += nn(hid[...], downb[slot])
        acc[...] += nn(dpr[...], upb[slot])
        gub[slot] = tn(dpr[...], mlp[...]).astype(BF)
        gdb[slot] = tn(hid[...], og[...]).astype(BF)
        for cp in store(c,slot): cp.start()
        return carry
    lax.fori_loop(0,steps,ffn,0)
    for k in range(OWN):
        gvc2 = msg
        gvc2[k] = big[R*k:R*(k+1), other_half].astype(BF)
    for k in range(OWN):
        img[OWN*core+k] = big[R*k:R*(k+1), own_half].astype(BF)
    img[IMG_DEV] = jnp.zeros((R,HALF),BF)
    oswap = pltpu.make_async_remote_copy(src_ref=msg.at[pl.ds(0,OWN)], dst_ref=img.at[pl.ds(OWN*core,OWN)], send_sem=gsem.at[0,2], recv_sem=gsem.at[1,2], device_id=sib, device_id_type=MESH)
    oswap.start()
    def back2(i, c):
        rows = pl.ds(pl.multiple_of(i*LNB,16),LNB)
        o = og[rows,:].astype(F32)
        d, dg, dc = norm_back(res[rows,:], acc[rows,:], vec[2:3,:])
        d = d + o
        res[rows,:] = d
        dx[rows,:] = d.astype(BF)
        return (c[0]+dg, c[1]+dc, c[2]+jnp.sum(o,axis=0,keepdims=True))
    z = jnp.zeros((1,D),F32)
    dg2, dc2, dob = lax.fori_loop(0,M//LNB,back2,(z,z,z))
    oswap.wait()
    for k in range(RSLOT):
        msg[k] = img[inv[k]]
    eout = [rc(msg.at[pair(t)], encm.at[pair(t)], 2, t, up[t]) for t in range(SPAN)]
    for cp in eout: cp.start()
    vgrad[2:3,:] = dg2; vgrad[3:4,:] = dc2; vgrad[4:5,:] = dob
    for slot in range(2):
        for cp in store(steps-2+slot, slot): cp.wait()
    def put(src, lo, n, sem): return pltpu.make_async_copy(src, g.at[pl.ds(lo,n)], sem)
    big[...] = nn(dx[...], outw[...])

    dctx = mlp
    def lowc(rows): dctx[rows,:] = big[rows,:].astype(BF)
    rows_loop(lowc)
    outw[...] = tn(dx[...], ctx[...]).astype(BF)
    po = put(outw, PIX+3*D, D, wsem.at[2]); po.start()
    def attend_back(n, c):
        i, p = n//6, n%6
        rows, ok, q, k, v = heads(i,p)
        here = pl.ds(pl.multiple_of(p*128,128),128)
        dc = dctx[rows, here]
        dq=[]; dk=None; dv=None
        for h, (qh, dch) in enumerate(zip(halves(q), halves(dc))):
            a = prob[2*n+h]
            af = a.astype(F32)
            da = nt(dch, v)
            t = af*da
            ds_ = (t - af*jnp.sum(t,axis=-1,keepdims=True)).astype(BF)
            dq.append(nn(ds_,k))
            dk_ = tn(ds_,qh); dv_ = tn(a,dch)
            dk = dk_ if dk is None else dk+dk_
            dv = dv_ if dv is None else dv+dv_
        s = HD**-0.5
        def at(j): return pl.ds(pl.multiple_of(j*D+p*128,128),128)
        qkv[rows, at(0)] = (jnp.where(low_half,dq[0],dq[1])*s).astype(BF)
        qkv[rows, at(1)] = (dk*s).astype(BF)
        qkv[rows, at(2)] = dv.astype(BF)
        return c
    lax.fori_loop(0,OWN*6,attend_back,0)
    acc[...] = nn(qkv[...], qkvw[...])
    def back1(i, c):
        rows = pl.ds(pl.multiple_of(i*LNB,16),LNB)
        d, dg, dc = norm_back(x[rows,:].astype(F32), acc[rows,:], vec[0:1,:])
        dx[rows,:] = (res[rows,:] + d).astype(BF)
        return (c[0]+dg, c[1]+dc)
    dg1, dc1 = lax.fori_loop(0,M//LNB,back1,(z,z))
    pswap.wait_send()
    for k in range(OWN):
        gvp[k, 0:PMAX, :] = dx[R*k:R*k+PMAX, other_half]
    for k in range(OWN):
        pim[OWN*core+k] = dx[R*k:R*k+PMAX, own_half]
    pim[IMG_DEV] = jnp.zeros((PMAX,HALF),BF)
    dswap = pltpu.make_async_remote_copy(src_ref=gvp.at[:, pl.ds(0,PMAX)], dst_ref=pim.at[pl.ds(OWN*core,OWN)], send_sem=gsem.at[0,3], recv_sem=gsem.at[1,3], device_id=sib, device_id_type=MESH)
    dswap.start()
    vgrad[0:1,:] = dg1; vgrad[1:2,:] = dc1
    for k in range(3):
        qkvw[k*D:(k+1)*D,:] = tn(qkv[:,k*D:(k+1)*D], nrm[...]).astype(BF)
    pq = put(qkvw, PIX, 3*D, wsem.at[1]); pq.start()
    dswap.wait()
    for k in range(RSLOT):
        pmsg[k] = pim[inv[k]]
    dout = [rc(pmsg.at[pair(t)], dprem.at[pair(t)], 3, t, up[t]) for t in range(SPAN)]
    for cp in dout: cp.start()
    tot = None
    for i in range(OWN):
        dp = dx[R*i+PMAX:R*(i+1),:]
        dpix[i] = nt(dp, stem[...]).astype(BF)
        t = tn(pix[i], dp)
        tot = t if tot is None else tot+t
    stem[...] = tot.astype(BF)
    ps = put(stem, 0, PIX, wsem.at[0]); ps.start()
    for cp in eout: cp.wait()
    po.wait(); pq.wait(); ps.wait()
    for cp in pin+cin: cp.wait_send()
    cswap.wait_send()
    for cp in dout: cp.wait()

def block(dest, inv, prefm, cotm, pix, vec, bias, w):
    A = pl.BlockSpec(memory_space=pl.ANY); V = pl.BlockSpec(memory_space=pltpu.VMEM); S=pl.BlockSpec(memory_space=pltpu.SMEM)
    dma=pltpu.SemaphoreType.DMA
    vm=lambda *s, t=BF: pltpu.VMEM(s,t)
    return pl.pallas_call(block_kernel,
        out_shape=(jax.ShapeDtypeStruct((M,D),BF), jax.ShapeDtypeStruct((OWN,NPAD,D),BF),
                   jax.ShapeDtypeStruct((8,D),F32), jax.ShapeDtypeStruct((1,FF),F32), jax.ShapeDtypeStruct((w.shape[0],D),BF),
                   jax.ShapeDtypeStruct((RSLOT,R,HALF),BF), jax.ShapeDtypeStruct((RSLOT,PMAX,HALF),BF)),
        in_specs=[S,S,A,A,V,V,V,A], out_specs=(V,V,V,V,A,A,A),
        scratch_shapes=[vm(RSLOT,MSG,HALF), vm(RSLOT,R,HALF), vm(OWN,MSG,HALF), vm(OWN,MSG,HALF), vm(OWN,R,HALF), vm(OWN,R,HALF),
            vm(IMG_DEV+1,R,HALF), vm(RSLOT,R,HALF), vm(IMG_DEV+1,PMAX,HALF), vm(RSLOT,PMAX,HALF), vm(M,D), dma((2,4,SPAN)), dma((2,4)),
            vm(PIX,D), vm(3*D,D), vm(D,D), vm(2,CH,D), vm(2,CH,D), vm(2,CH,D), vm(2,CH,D),
            vm(M,D), vm(M,D), vm(M,3*D), vm(2*OWN*6,R,R), vm(M,D), vm(M,D,t=F32), vm(M,D), vm(M,D,t=F32), vm(M,D,t=F32),
            vm(M,CH), vm(M,CH), vm(M,CH,t=F32), vm(M,CH,t=F32), dma((3,)), dma((2,2)), dma((2,2))],
        compiler_params=pltpu.CompilerParams(collective_id=3, has_side_effects=True, vmem_limit_bytes=63*2**20))(dest,inv,prefm,cotm,pix,vec,bias,w)


def gathered(weights, vectors, n_dp):
    n_dev = 2 * n_dp
    lane = vectors.shape[1]
    if n_dp == 16:
        block = jnp.pad(vectors.reshape(9 * lane), (0, 1024 - 9 * lane)).reshape(8, 128)
        slabs, blocks = all_gather(weights, block)
        full = slabs.reshape(n_dev * SLAB, D)
        blocks = blocks.reshape(n_dev, 1024)
    else:
        block = jnp.pad(vectors.reshape(9 * lane), (0, VLANES - 9 * lane))
        full = lax.all_gather(weights, ALL, axis=0, tiled=True)
        blocks = lax.all_gather(block, ALL, axis=0, tiled=True).reshape(n_dev, VLANES)
    rows = blocks[:, : 9 * lane].reshape(n_dev, 9, lane).transpose(1, 0, 2).reshape(9, D)
    return full, rows.astype(F32)


def summed(grads, vec_grads, n_dp):
    n_dev = 2 * n_dp
    lane = D // n_dev
    blocks = vec_grads.reshape(9, n_dev, lane).transpose(1, 0, 2).reshape(n_dev, 9 * lane)
    if n_dp == 16:
        blocks = jnp.pad(blocks, ((0, 0), (0, 1024 - 9 * lane))).reshape(n_dev, 8, 128)
        weight_grad, vec_grad = reduce_scatter(grads.reshape(n_dev, SLAB, D), blocks)
        vec_grad = vec_grad.reshape(1024)
    else:
        blocks = jnp.pad(blocks, ((0, 0), (0, VLANES - 9 * lane)))
        weight_grad = lax.psum_scatter(grads, ALL, scatter_dimension=0, tiled=True).astype(F32)
        vec_grad = lax.psum_scatter(blocks, ALL, scatter_dimension=0, tiled=True).reshape(VLANES)
    return weight_grad, vec_grad[: 9 * lane].reshape(9, lane)


def body(
    stream_rows,
    dest,
    prefix_len,
    weights,
    momentum,
    average,
    vectors,
    vec_momentum,
    vec_average,
    cotangent,
):
    core = lax.axis_index("stream")
    first = core == 0
    n_dp = lax.axis_size("dp")

    full_weights, vector_rows = gathered(weights.astype(BF), vectors.astype(BF), n_dp)
    own_rows = stream_rows[0, 0]
    half_rows = ROWS // 2
    narrow = own_rows[:, :HALF]
    give = jnp.where(first, own_rows[half_rows:], jnp.concatenate([narrow[:half_rows], narrow[half_rows:]], axis=1))
    got = swapped(give)
    pixels = jnp.where(first, own_rows[:half_rows], got)
    packed = jnp.where(first, jnp.concatenate([got[:, :HALF], got[:, HALF:]], axis=0), own_rows[:, HALF:])

    lengths = prefix_len[0]
    offsets = jnp.cumsum(lengths) - lengths
    places = jnp.arange(PMAX, dtype=jnp.int32)
    row_index = offsets[:, None] + places[None, :]
    keep_mask = places[None, :] < lengths[:, None]
    rows_at = jnp.arange(ROWS, dtype=jnp.int32)
    pick = (
        (row_index.reshape(-1)[:, None] == rows_at[None, :]) & keep_mask.reshape(-1)[:, None]
    ).astype(BF)
    prefix_slots = dot(pick, packed, (1, 0)).astype(BF).reshape(RSLOT, PMAX, HALF)
    length_rows = jnp.broadcast_to(
        lengths.astype(BF)[:, None, None], (RSLOT, MSG - PMAX, HALF)
    )
    columns = jnp.arange(SEQ, dtype=jnp.int32)
    row_ok = (columns[None, :] < NP + lengths[:, None]) & (lengths[:, None] > 0)
    kept_cot = jnp.where(row_ok[:, :, None], cotangent[0], jnp.zeros((), BF))
    cot_slots = jnp.concatenate(
        [kept_cot[:, NP:], kept_cot[:, :NP], jnp.zeros((RSLOT, NPAD - NP, HALF), BF)], axis=1
    )
    slots = dest[0]

    prefix_msgs = jnp.concatenate([prefix_slots, length_rows], axis=1)
    pixels = jnp.pad(pixels.reshape(OWN, NP, D), ((0, 0), (0, NPAD - NP), (0, 0)))
    vec_in = jnp.pad(vector_rows[:5], ((0, 3), (0, 0)))
    slot_ids = jnp.arange(RSLOT, dtype=jnp.int32)
    taken = slot_ids[:, None] == slots[None, :]
    inverse = jnp.where(
        jnp.any(taken, axis=1), jnp.argmax(taken, axis=1).astype(jnp.int32), IMG_DEV
    ).astype(jnp.int32)
    _, d_pixels, vec5, d_bias, grad_local, enc_back, prefix_back = block(
        slots, inverse, prefix_msgs, cot_slots, pixels, vec_in, vector_rows[5:9].reshape(1, FF), full_weights
    )
    vec_local = jnp.concatenate([vec5[:5], d_bias.reshape(4, D)])
    d_pixels = d_pixels[:, :NP].reshape(half_rows, D)

    enc_out = jnp.concatenate([enc_back[:, PMAX : PMAX + NP], enc_back[:, :PMAX]], axis=1)
    enc_out = jnp.where(row_ok[:, :, None], enc_out, jnp.zeros((), BF))[None]
    weight_grad, vec_grad = summed(grad_local, vec_local, n_dp)

    d_packed = dot(pick, prefix_back.reshape(RSLOT * PMAX, HALF), (0, 0)).astype(BF)
    give = jnp.where(
        first, jnp.concatenate([d_packed[:half_rows], d_packed[half_rows:]], axis=1), d_pixels
    )
    got = swapped(give)
    d_image_rows = jnp.concatenate([d_pixels, got]).astype(F32)
    d_text_rows = jnp.concatenate(
        [jnp.concatenate([got[:, :HALF], got[:, HALF:]], axis=0), d_packed], axis=1
    ).astype(F32)
    d_rows = jnp.where(first, d_image_rows, d_text_rows)[None, None]

    rate = 0.5 * (D * IMG_DEV * n_dp * NP) ** (-0.5)
    new_momentum = MOMENT * momentum + weight_grad
    new_weights = weights - rate * (weight_grad + MOMENT * new_momentum)
    new_average = DECAY * average + (1.0 - DECAY) * new_weights
    vec_new_momentum = MOMENT * vec_momentum + vec_grad
    vec_new = vectors - rate * (vec_grad + MOMENT * vec_new_momentum)
    vec_new_average = DECAY * vec_average + (1.0 - DECAY) * vec_new
    return (
        enc_out,
        d_rows,
        weight_grad,
        new_momentum,
        new_average,
        new_weights,
        new_weights.astype(BF),
        vec_grad,
        vec_new_momentum,
        vec_new_average,
        vec_new,
        vec_new.astype(BF),
    )


def solution(mesh):
    both = P(ALL, None)
    lanes = P(None, ALL)
    in_specs = (
        P("stream", "dp", None, None),
        P("dp", None),
        P("dp", None),
        both,
        both,
        both,
        lanes,
        lanes,
        lanes,
        P("dp", None, None, "stream"),
    )
    out_specs = (
        P("dp", None, None, "stream"),
        P("stream", "dp", None, None),
        both,
        both,
        both,
        both,
        both,
        lanes,
        lanes,
        lanes,
        lanes,
        lanes,
    )
    return jax.shard_map(body, mesh=mesh, in_specs=in_specs, out_specs=out_specs, check_vma=False)
```

```python
import functools
from types import SimpleNamespace

import jax
import jax.numpy as jnp
from jax import lax
from jax.experimental import pallas as pl
from jax.experimental.pallas import tpu as pltpu
from jax.sharding import PartitionSpec as P

D = 768
HEADS = 12
HD = 64
FF = 3072
PIX = 768
NP = 196
PMAX = 64
SPAN = 4
IMG_DEV = 4
CAP = 2
RSLOT = 8
SEQ = 260
ROWS = 784
HALF = D // 2
OWN = IMG_DEV // 2
SLAB = 312
CUT = 160
NZ = 4

EPSILON = 1e-06
MASKED = -1e30
MOMENT = 0.5
DECAY = 0.5
BF = jnp.bfloat16
F32 = jnp.float32
ALL = ("stream", "dp")
MESH = pl.DeviceIdType.MESH


NPAD = 208
R = PMAX + NPAD
M = OWN * R
CH = 512
LNB = 32
MSG = PMAX + 16
VEC = 16
UP = PIX + 4 * D
DOWN = UP + FF
VIA_Z = (1, 2)
CIN_AT = 12
ISSUE = (1, 3, 0, 2)
SUM_VIA = (1, 2)
dma = pltpu.SemaphoreType.DMA


def nn(a, b):
    return lax.dot_general(a, b, (((1,), (0,)), ((), ())), preferred_element_type=F32)


def nt(a, b):
    return lax.dot_general(a, b, (((1,), (1,)), ((), ())), preferred_element_type=F32)


def tn(a, b):
    return lax.dot_general(a, b, (((0,), (0,)), ((), ())), preferred_element_type=F32)


def erf(v):
    v = jnp.clip(v, -3.832506856900711, 3.832506856900711)
    s = v * v
    top = 0.00022905065861350646
    for c in (0.0034082910107109506, 0.050955695062380861, 0.18520832239976145, 1.128379143519084):
        top = top * s + c
    low = -1.1791602954361697e-7
    for c in (
        0.000023547966471313185,
        0.0010179625278914885,
        0.014070470171167667,
        0.11098505178285362,
        0.49746925110067538,
        1.0,
    ):
        low = low * s + c
    return v * top / low


def gelu_both(v):
    phi = 0.5 * (1.0 + erf(v * 0.7071067811865476))
    return v * phi, phi + v * (0.3989422804014327 * jnp.exp(-0.5 * v * v))


def rows_loop(f, block=LNB, total=M):
    def run(i, c):
        f(pl.ds(pl.multiple_of(i * block, 16), block))
        return c

    lax.fori_loop(0, total // block, run, 0, unroll=True)


def norm_parts(v):
    off = v - jnp.mean(v, axis=-1, keepdims=True)
    inv = lax.rsqrt(jnp.mean(off * off, axis=-1, keepdims=True) + EPSILON)
    return off * inv, inv


def norm_back(v, dn, gain):
    xhat, inv = norm_parts(v)
    dx = dn * gain
    low = jnp.mean(dx, axis=-1, keepdims=True)
    slope = jnp.mean(dx * xhat, axis=-1, keepdims=True)
    return (
        (dx - low - xhat * slope) * inv,
        jnp.sum(dn * xhat, axis=0, keepdims=True),
        jnp.sum(dn, axis=0, keepdims=True),
    )


def remote(src, dst, send, recv, dev):
    return pltpu.make_async_remote_copy(
        src_ref=src, dst_ref=dst, send_sem=send, recv_sem=recv, device_id=dev, device_id_type=MESH
    )


def place():
    core = lax.axis_index("stream")
    chip = lax.axis_index("dp")
    return core, chip, chip % 2, (chip // 2) % 2, chip // 4


def greet_all(core, chip):
    barrier = pltpu.get_barrier_semaphore()
    me = core * 16 + chip

    def one(k, carry):
        peer = (me + k) % 32
        pl.semaphore_signal(barrier, inc=1, device_id=(peer // 16, peer % 16), device_id_type=MESH)
        return carry

    lax.fori_loop(1, 32, one, 0)
    pl.semaphore_wait(barrier, 31)


def greet_near(core, chip, n_dp):
    barrier = pltpu.get_barrier_semaphore()
    for t in range(1, SPAN + 1):
        for peer in ((chip + t) % n_dp, (chip + n_dp - t) % n_dp):
            pl.semaphore_signal(barrier, inc=1, device_id=(core, peer), device_id_type=MESH)
    pl.semaphore_signal(barrier, inc=1, device_id=(1 - core, chip), device_id_type=MESH)
    pl.semaphore_wait(barrier, 2 * SPAN + 1)


def gather_sems():
    four = dma((4,))
    return [dma((2, 4)), four, dma((2, 4)), four] + [four] * 8 + [dma, dma]


def gather_steps(w_ref, out, sems, part, draining=False):
    core, chip, x, y, z = place()
    zs, zr, ds, dr, xs, xr, ys, yr, as_, ar, bs, br, ss, sr = sems
    base = core * 16
    me = base + chip
    flat = chip % 4
    xn = chip + 1 - 2 * x
    yn = chip + 2 - 4 * y
    start, size = ((0, CUT), (CUT, SLAB - CUT))[part]
    top = pl.ds(0, 80)
    bottom = pl.ds(80, size - 80)
    sib = (1 - core, chip)
    w_ref = w_ref.at[pl.ds(start, size)]

    def slab_of(slab, rows=None):
        whole = out.at[pl.ds(pl.multiple_of(slab * SLAB + start, 8), size)]
        return whole if rows is None else whole.at[rows]

    def rc(src, slab, ssem, rsem, dev, rows=None):
        return remote(src, slab_of(slab, rows), ssem, rsem, dev)

    def go(cond, make):
        def act():
            if draining:
                make().wait_send()
            else:
                make().start()

        if cond is None:
            act()
        else:
            pl.when(cond)(act)

    def to_sib(src, slab):
        if not draining:
            rc(src, slab, ss, sr, sib).start()

    def arrive(copy):
        if not draining:
            copy().wait_recv()

    def at(t, sign):
        zz = z + sign * t
        return zz, (zz >= 0) & (zz < NZ)

    def own():
        go(None, lambda: rc(w_ref, me, xs.at[z], xr.at[z], (core, xn)))
        go(None, lambda: rc(w_ref, me, ys.at[z], yr.at[z], (core, yn)))
        for k, s in enumerate((1, -1)):
            go(
                (z + s >= 0) & (z + s < NZ),
                lambda k=k, s=s: rc(w_ref, me, zs.at[k, z], zr.at[z], (core, chip + 4 * s)),
            )
        to_sib(w_ref, me)

    def column(t, sign):
        zz, here = at(t, sign)
        slab = base + zz * 4 + flat
        k = 0 if sign < 0 else 1

        @pl.when(here)
        def _():
            arrive(lambda: rc(w_ref, slab, ss, zr.at[zz], sib))

        src = slab_of(slab)
        go(
            here & (z - sign >= 0) & (z - sign < NZ),
            lambda: rc(src, slab, zs.at[k, zz], zr.at[zz], (core, chip - 4 * sign)),
        )
        go(here, lambda: rc(src, slab, xs.at[zz], xr.at[zz], (core, xn)))
        go(here, lambda: rc(src, slab, ys.at[zz], yr.at[zz], (core, yn)))

        @pl.when(here)
        def _():
            to_sib(src, slab)

    def plane(t, sign):
        zz, here = at(t, sign)
        xslab = base + zz * 4 + flat + 1 - 2 * x
        yslab = base + zz * 4 + flat + 2 - 4 * y

        @pl.when(here)
        def _():
            arrive(lambda: rc(w_ref, xslab, ss, xr.at[zz], sib))

        if t not in VIA_Z:
            go(
                here,
                lambda: rc(slab_of(xslab, top), xslab, as_.at[zz], ar.at[zz], (core, yn), top),
            )

        @pl.when(here)
        def _():
            arrive(lambda: rc(w_ref, yslab, ss, yr.at[zz], sib))

        if t not in VIA_Z:
            go(
                here,
                lambda: rc(slab_of(yslab, bottom), yslab, bs.at[zz], br.at[zz], (core, xn), bottom),
            )

        @pl.when(here)
        def _():
            to_sib(slab_of(xslab), xslab)
            to_sib(slab_of(yslab), yslab)

    def diag(t, sign):
        zz, here = at(t, sign)
        slab = base + zz * 4 + 3 - flat
        src = slab_of(slab)
        if t in VIA_Z:

            @pl.when(here)
            def _():
                arrive(lambda: rc(w_ref, slab, ss, dr.at[zz], sib))
        else:

            @pl.when(here)
            def _():
                arrive(lambda: rc(slab_of(slab, top), slab, ss, ar.at[zz], sib, top))
                arrive(lambda: rc(slab_of(slab, bottom), slab, ss, br.at[zz], sib, bottom))

        if t == 0 and 1 in VIA_Z:
            for k, s in enumerate((1, -1)):
                go(
                    (z + s >= 0) & (z + s < NZ),
                    lambda k=k, s=s: rc(src, slab, ds.at[k, zz], dr.at[zz], (core, chip + 4 * s)),
                )
        if t >= 1 and t + 1 in VIA_Z:
            k = 0 if sign < 0 else 1
            go(
                here & (z - sign >= 0) & (z - sign < NZ),
                lambda: rc(src, slab, ds.at[k, zz], dr.at[zz], (core, chip - 4 * sign)),
            )

        @pl.when(here)
        def _():
            to_sib(src, slab)

    def both(f, t):
        def run():
            f(t, 1)
            if t:
                f(t, -1)

        return run

    return [
        own,
        both(column, 1),
        both(plane, 0),
        both(column, 2),
        both(diag, 0),
        both(plane, 1),
        both(column, 3),
        both(diag, 1),
        both(plane, 2),
        both(plane, 3),
        both(diag, 2),
        both(diag, 3),
    ]


PART = 160
SHIFT = SLAB - PART
ADD = 16
ADD_UNROLL = 5
RS_BUFS = (
    ("sbuf", (16, PART, D), BF),
    ("xb", (4, PART, D), BF),
    ("yb", (4, PART, D), BF),
    ("dzb", (2, 2, PART, D), BF),
    ("czb", (2, 3, PART, D), BF),
    ("ab", (4, PART // 2, D), BF),
    ("bb", (4, PART // 2, D), BF),
    ("fin", (PART, D), F32),
)
RS_SEMS = (
    ("load", (16,)),
    ("ssend", ()),
    ("srecv", (16,)),
    ("xs", (4,)),
    ("xr", (4,)),
    ("ys", (4,)),
    ("yr", (4,)),
    ("dzs", (2, 2)),
    ("dzr", (2, 2)),
    ("czs", (2, 3)),
    ("czr", (2, 3)),
    ("as_", (4,)),
    ("ar", (4,)),
    ("bs", (4,)),
    ("br", (4,)),
    ("fsem", (2,)),
)


def rs_scratch():
    return [pltpu.VMEM(s, t) for _, s, t in RS_BUFS] + [dma(s) for _, s in RS_SEMS]


def add_rows(dst, sources, lo, size):
    def piece(i, c):
        tot = None
        for ref, at in sources:
            v = ref[pl.ds(pl.multiple_of(at + i * ADD, 16), ADD), :].astype(F32)
            tot = v if tot is None else tot + v
        dst[pl.ds(pl.multiple_of(lo + i * ADD, 16), ADD), :] = tot.astype(dst.dtype)
        return c

    lax.fori_loop(0, size // ADD, piece, 0, unroll=ADD_UNROLL)


class Sends:
    def __init__(self):
        self.kept = []

    def go(self, cond, make):
        if cond is None:
            make().start()
        else:

            @pl.when(cond)
            def _():
                make().start()

        self.kept.append((cond, make))

    def drain(self):
        for cond, make in self.kept:
            if cond is None:
                make().wait_send()
            else:

                @pl.when(cond)
                def _(make=make):
                    make().wait_send()


def sum_steps(half, g, result, obuf, refs, via):
    B = SimpleNamespace(**dict(zip([n for n, _, _ in RS_BUFS] + [n for n, _ in RS_SEMS], refs)))
    core, chip, x, y, z = place()
    flat = chip % 4
    xn = chip + 1 - 2 * x
    yn = chip + 2 - 4 * y
    sib = (1 - core, chip)
    mid = PART // 2
    top = pl.ds(0, mid)
    bottom = pl.ds(mid, mid)
    fd, fx, fy = 3 - flat, flat + 1 - 2 * x, flat + 2 - 4 * y
    sends = Sends()

    def rows_of(i, part):
        return g.at[pl.ds(pl.multiple_of((16 * half + i) * SLAB + part * SHIFT, 8), PART)]

    def each(t, f):
        if t == 0:
            f(z, 0, None)
            return
        for sign in (1, -1):
            zz = z + sign * t
            f(zz, sign, (zz >= 0) & (zz < NZ))

    def when(cond, f):
        if cond is None:
            f()
        else:
            pl.when(cond)(f)

    order = [(fd, 3), (fd, 2), (fx, 3), (fy, 3), (fx, 2), (fy, 2), (fd, 1), (flat, 3)]
    order += [(fx, 1), (fy, 1), (fd, 0), (flat, 2), (fx, 0), (fy, 0), (flat, 1), (flat, 0)]

    def start():
        for f, t in order:

            def begin(zz, sign, here, f=f):
                i = zz * 4 + f

                def go():
                    remote(rows_of(i, 1 - core), B.sbuf.at[i], B.ssend, B.srecv.at[i], sib).start()
                    pltpu.make_async_copy(rows_of(i, core), obuf(i), B.load.at[i]).start()

                when(here, go)

            each(t, begin)

    def ready(i):
        pltpu.make_async_copy(rows_of(i, core), obuf(i), B.load.at[i]).wait()
        remote(rows_of(i, core), B.sbuf.at[i], B.ssend, B.srecv.at[i], sib).wait_recv()

    def landed(dst, send, recv):
        remote(dst, dst, send, recv, sib).wait_recv()

    def up_down(sign):
        return 0 if sign > 0 else 1

    def inside(zz):
        return (zz >= 0) & (zz < NZ)

    def diag(t):
        def f(zz, sign, here):
            i = zz * 4 + fd

            def work():
                ready(i)
                src = [(obuf(i), 0), (B.sbuf.at[i], 0)]
                if t in via and t + 1 in via:
                    k = up_down(sign)
                    far = inside(z - sign)

                    @pl.when(far)
                    def _():
                        landed(B.dzb.at[k, t], B.dzs.at[k, t], B.dzr.at[k, t])
                        add_rows(obuf(i), src + [(B.dzb.at[k, t], 0)], 0, PART)

                    @pl.when(jnp.logical_not(far))
                    def _():
                        add_rows(obuf(i), src, 0, PART)

                elif t == 0 and 1 in via:
                    add_rows(obuf(i), src, 0, PART)
                    for k, s in enumerate((1, -1)):

                        @pl.when(inside(z - s))
                        def _(k=k):
                            landed(B.dzb.at[k, 0], B.dzs.at[k, 0], B.dzr.at[k, 0])
                            add_rows(obuf(i), [(obuf(i), 0), (B.dzb.at[k, 0], 0)], 0, PART)

                else:
                    add_rows(obuf(i), src, 0, PART)

            when(here, work)
            if t in via:
                k = up_down(sign)
                sends.go(
                    here,
                    lambda: remote(
                        obuf(i),
                        B.dzb.at[k, t - 1],
                        B.dzs.at[k, t - 1],
                        B.dzr.at[k, t - 1],
                        (core, chip + 4 * sign),
                    ),
                )
            else:
                sends.go(
                    here,
                    lambda: remote(
                        obuf(i).at[top], B.ab.at[zz], B.as_.at[zz], B.ar.at[zz], (core, yn)
                    ),
                )
                sends.go(
                    here,
                    lambda: remote(
                        obuf(i).at[bottom], B.bb.at[zz], B.bs.at[zz], B.br.at[zz], (core, xn)
                    ),
                )

        return lambda: each(t, f)

    def plane(t):
        def f(zz, sign, here):
            ix, iy = zz * 4 + fx, zz * 4 + fy

            def work_x():
                ready(ix)
                src = [(obuf(ix), 0), (B.sbuf.at[ix], 0)]
                if t in via:
                    add_rows(obuf(ix), src, 0, PART)
                else:
                    add_rows(obuf(ix), [(r, mid) for r, _ in src], mid, mid)
                    landed(B.ab.at[zz], B.as_.at[zz], B.ar.at[zz])
                    add_rows(obuf(ix), src + [(B.ab.at[zz], 0)], 0, mid)

            def work_y():
                ready(iy)
                src = [(obuf(iy), 0), (B.sbuf.at[iy], 0)]
                if t in via:
                    add_rows(obuf(iy), src, 0, PART)
                else:
                    add_rows(obuf(iy), src, 0, mid)
                    landed(B.bb.at[zz], B.bs.at[zz], B.br.at[zz])
                    add_rows(obuf(iy), [(r, mid) for r, _ in src] + [(B.bb.at[zz], 0)], mid, mid)

            when(here, work_x)
            sends.go(
                here, lambda: remote(obuf(ix), B.xb.at[zz], B.xs.at[zz], B.xr.at[zz], (core, xn))
            )
            when(here, work_y)
            sends.go(
                here, lambda: remote(obuf(iy), B.yb.at[zz], B.ys.at[zz], B.yr.at[zz], (core, yn))
            )

        return lambda: each(t, f)

    def column(t):
        def f(zz, sign, here):
            i = zz * 4 + flat
            k = up_down(sign)

            def work():
                ready(i)
                landed(B.xb.at[zz], B.xs.at[zz], B.xr.at[zz])
                landed(B.yb.at[zz], B.ys.at[zz], B.yr.at[zz])
                src = [(obuf(i), 0), (B.sbuf.at[i], 0), (B.xb.at[zz], 0), (B.yb.at[zz], 0)]
                if t == 3:
                    add_rows(obuf(i), src, 0, PART)
                    return
                far = inside(z - sign)

                @pl.when(far)
                def _():
                    landed(B.czb.at[k, t], B.czs.at[k, t], B.czr.at[k, t])
                    add_rows(obuf(i), src + [(B.czb.at[k, t], 0)], 0, PART)

                @pl.when(jnp.logical_not(far))
                def _():
                    add_rows(obuf(i), src, 0, PART)

            when(here, work)
            sends.go(
                here,
                lambda: remote(
                    obuf(i),
                    B.czb.at[k, t - 1],
                    B.czs.at[k, t - 1],
                    B.czr.at[k, t - 1],
                    (core, chip + 4 * sign),
                ),
            )

        return lambda: each(t, f)

    if half == 1:
        part = remote(
            B.fin.at[pl.ds(0, SHIFT)],
            result.at[pl.ds(0, SHIFT)],
            B.fsem.at[0],
            B.fsem.at[1],
            (1, chip),
        )
    else:
        part = remote(
            B.fin.at[pl.ds(PART - SHIFT, SHIFT)],
            result.at[pl.ds(PART, SHIFT)],
            B.fsem.at[0],
            B.fsem.at[1],
            (0, chip),
        )

    def final():
        i = z * 4 + flat
        ready(i)
        landed(B.xb.at[z], B.xs.at[z], B.xr.at[z])
        landed(B.yb.at[z], B.ys.at[z], B.yr.at[z])
        src = [(obuf(i), 0), (B.sbuf.at[i], 0), (B.xb.at[z], 0), (B.yb.at[z], 0)]
        add_rows(B.fin, src, 0, PART)
        for k, s in enumerate((1, -1)):

            @pl.when(inside(z - s))
            def _(k=k):
                landed(B.czb.at[k, 0], B.czs.at[k, 0], B.czr.at[k, 0])
                add_rows(B.fin, [(B.fin, 0), (B.czb.at[k, 0], 0)], 0, PART)

        @pl.when(core == half)
        def _():
            result[pl.ds(half * SHIFT, PART), :] = B.fin[...]

        @pl.when(core != half)
        def _():
            part.start()

    def drain():
        pltpu.make_async_copy(B.sbuf, B.sbuf, B.ssend).wait()
        sends.drain()

        @pl.when(core == half)
        def _():
            part.wait_recv()

        @pl.when(core != half)
        def _():
            part.wait_send()

    steps = [diag(3), diag(2), plane(3), plane(2), diag(1), column(3), plane(1), diag(0)]
    steps += [column(2), plane(0), column(1), final]
    return start, steps, drain


def last_sum(
    plen, g, vg, back, dpix, out, vout, drows, obuf, vbuf, half_rows, tall, vs, vr, vl, es, *refs
):
    core, chip = lax.axis_index("stream"), lax.axis_index("dp")
    me = core * 16 + chip
    first = core == 0
    greet_all(core, chip)
    start, steps, drain = sum_steps(0, g, out, lambda i: obuf.at[i], refs, (1, 2))
    start()

    def vsend(k, carry):
        peer = (me + k) % 32
        remote(vg.at[peer], vbuf.at[me], vs, vr, (peer // 16, peer % 16)).start()
        return carry

    lax.fori_loop(1, 32, vsend, 0)
    vcp = pltpu.make_async_copy(vg.at[me], vbuf.at[me], vl)
    vcp.start()
    steps[0]()
    steps[1]()

    row_at = lax.broadcasted_iota(jnp.int32, (PMAX, ROWS), 1)
    row_of = lax.broadcasted_iota(jnp.int32, (PMAX, ROWS), 0)
    offset = jnp.int32(0)
    total = jnp.zeros((ROWS, HALF), F32)
    for s in range(RSLOT):
        pick = (row_at == row_of + offset) & (row_of < plen[s])
        total = total + tn(pick.astype(F32).astype(BF), back[s])
        offset = offset + plen[s]
    steps[2]()
    steps[3]()
    to_text = remote(tall.at[0], tall.at[1], es.at[0], es.at[1], (1, chip))
    to_image = remote(half_rows.at[0], half_rows.at[1], es.at[0], es.at[1], (0, chip))

    @pl.when(first)
    def _():
        tall[0] = total.astype(BF)
        to_text.start()
        for i in range(OWN):
            drows[NP * i : NP * (i + 1), :] = dpix[i, 0:NP, :]

    @pl.when(core == 1)
    def _():
        for i in range(OWN):
            half_rows[0, NP * i : NP * (i + 1), :] = dpix[i, 0:NP, :]
        to_image.start()
        drows[:, HALF:] = total.astype(BF)

    steps[4]()
    steps[5]()

    @pl.when(first)
    def _():
        to_image.wait_recv()
        drows[OWN * NP :, :] = half_rows[1]

    @pl.when(core == 1)
    def _():
        to_text.wait_recv()
        drows[:, :HALF] = tall[1]

    for step in steps[6:]:
        step()
    vcp.wait()
    pltpu.make_async_copy(vbuf.at[pl.ds(0, 31)], vbuf.at[pl.ds(0, 31)], vr).wait()
    vout[...] = jnp.sum(vbuf[...], axis=0)
    pltpu.make_async_copy(vbuf.at[pl.ds(0, 31)], vbuf.at[pl.ds(0, 31)], vs).wait()

    @pl.when(first)
    def _():
        to_text.wait_send()

    @pl.when(core == 1)
    def _():
        to_image.wait_send()

    drain()


def summed(plen, g, vg, back, dpix):
    any_ = pl.BlockSpec(memory_space=pl.ANY)
    vmem = pl.BlockSpec(memory_space=pltpu.VMEM)
    smem = pl.BlockSpec(memory_space=pltpu.SMEM)
    return pl.pallas_call(
        last_sum,
        out_shape=(
            jax.ShapeDtypeStruct((SLAB, D), F32),
            jax.ShapeDtypeStruct((VEC, 128), F32),
            jax.ShapeDtypeStruct((ROWS, D), BF),
        ),
        in_specs=[smem, any_, any_, vmem, vmem],
        out_specs=(vmem, vmem, vmem),
        scratch_shapes=[
            pltpu.VMEM((16, PART, D), BF),
            pltpu.VMEM((32, VEC, 128), F32),
            pltpu.VMEM((2, OWN * NP, D), BF),
            pltpu.VMEM((2, ROWS, HALF), BF),
            dma,
            dma,
            dma,
            dma((2,)),
        ]
        + rs_scratch(),
        compiler_params=pltpu.CompilerParams(
            collective_id=2, has_side_effects=True, vmem_limit_bytes=60 * 2**20
        ),
    )(plen, g, vg, back, dpix)


X_IN = ("dest", "plen", "rows", "cot", "wsh", "vblk", "wfull")
X_OUT = ("dpix", "vgb", "g", "encm", "dprem", "wall", "r1")
X_SCRATCH = (
    ("packed", (ROWS, HALF), BF),
    ("raw", (ROWS // 2, D), BF),
    ("pmsg", (RSLOT, MSG, HALF), BF),
    ("cmsg", (RSLOT, R, HALF), BF),
    ("arp", (RSLOT, MSG, HALF), BF),
    ("arc", (RSLOT, R, HALF), BF),
    ("gvp", (OWN, MSG, HALF), BF),
    ("gtp", (OWN, MSG, HALF), BF),
    ("gvc", (OWN, R, HALF), BF),
    ("gtc", (OWN, R, HALF), BF),
    ("gvo", (OWN, R, HALF), BF),
    ("img", (IMG_DEV + 1, R, HALF), BF),
    ("pim", (IMG_DEV + 1, PMAX, HALF), BF),
    ("pback", (RSLOT, PMAX, HALF), BF),
    ("vbuf", (32, VEC, 128), BF),
    ("vec", (VEC, D), F32),
    ("bias", (1, FF), F32),
    ("vg", (VEC, D), F32),
    ("bg", (1, FF), F32),
    ("pix", (OWN, NPAD, D), BF),
    ("og", (M, D), BF),
    ("dx", (M, D), BF),
    ("stem", (PIX, D), BF),
    ("qkvw", (3 * D, D), BF),
    ("outw", (D, D), BF),
    ("wb", (8, CH, D), BF),
    ("x", (M, D), BF),
    ("nrm", (M, D), BF),
    ("qkv", (M, 3 * D), BF),
    ("prob", (2 * OWN * 6, R, R), BF),
    ("ctx", (M, D), BF),
    ("res", (M, D), F32),
    ("mlp", (M, D), BF),
    ("big", (M, D), F32),
    ("hid", (M, FF), BF),
    ("slope", (M, FF), BF),
    ("dpr", (M, CH), BF),
    ("f1", (M, CH), F32),
)
X_SEMS = (
    ("psem", (2, 4, SPAN)),
    ("gsem", (2, 6)),
    ("lsem", (8,)),
    ("vsem", (2,)),
    ("wsem", (3,)),
    ("csem", (2, 2)),
    ("osem", (2, 2)),
)


def x_kernel(near, *refs):
    names = X_IN + X_OUT + tuple(n for n, _, _ in X_SCRATCH) + tuple(n for n, _ in X_SEMS)
    K = SimpleNamespace(**dict(zip(names, refs)))
    gsems = refs[len(names) :]
    if not near:
        gsems, sum_refs = gsems[: -len(RS_BUFS) - len(RS_SEMS)], gsems[-len(RS_BUFS) - len(RS_SEMS) :]
    K.upb, K.downb = K.wb.at[pl.ds(0, 2)], K.wb.at[pl.ds(2, 2)]
    K.gub, K.gdb = K.wb.at[pl.ds(4, 2)], K.wb.at[pl.ds(6, 2)]
    core = lax.axis_index("stream")
    chip = lax.axis_index("dp")
    n_dp = lax.axis_size("dp")
    sib = (1 - core, chip)
    first = core == 0
    second = core == 1
    me = core * n_dp + chip
    if near:
        greet_near(core, chip, n_dp)
    else:
        greet_all(core, chip)
    wall = K.wfull if near else K.wall

    n_sems = len(gsems) // 2
    todo = []
    if not near:
        parts = [gather_steps(K.wsh, wall, gsems[p * n_sems : (p + 1) * n_sems], p) for p in range(2)]
        todo = [step for pair_ in zip(*parts) for step in pair_]

    def advance(n):
        for _ in range(n):
            if todo:
                todo.pop(0)()

    if not near:

        advance(2)

        K.vbuf[me] = K.vblk[...]
        own_slab = wall.at[pl.ds(pl.multiple_of(me * SLAB, 8), SLAB)]
        keep = K.upb.at[0, pl.ds(0, SLAB)]
        kin = pltpu.make_async_copy(K.wsh, keep, K.lsem.at[1])
        kout = pltpu.make_async_copy(keep, own_slab, K.lsem.at[2])
        kin.start()

    last_rows = K.rows.at[pl.ds(ROWS // 2, ROWS // 2)]
    pix_go = remote(last_rows, K.raw, K.gsem.at[0, 4], K.gsem.at[1, 4], (1, chip))
    pack_go = remote(
        K.rows.at[:, pl.ds(0, HALF)], K.packed, K.gsem.at[0, 4], K.gsem.at[1, 4], (0, chip)
    )
    pix_own = pltpu.make_async_copy(K.rows.at[pl.ds(0, ROWS // 2)], K.raw, K.lsem.at[0])
    pack_own = pltpu.make_async_copy(K.rows.at[:, pl.ds(HALF, HALF)], K.packed, K.lsem.at[0])

    @pl.when(first)
    def _():
        pix_go.start()
        pix_own.start()

    @pl.when(second)
    def _():
        pack_go.start()
        pack_own.start()

    if not near:

        def vsend(k, carry):
            peer = (me + k) % 32
            remote(K.vblk, K.vbuf.at[me], K.vsem.at[0], K.vsem.at[1], (peer // 16, peer % 16)).start()
            return carry

        lax.fori_loop(1, 32, vsend, 0)

    def pair(t):
        return pl.ds(CAP * t, CAP)

    def rc(src, dst, k, i, dev):
        return remote(src, dst, K.psem.at[0, k, i], K.psem.at[1, k, i], dev)

    down = [(core, (chip + n_dp - t - 1) % n_dp) for t in range(SPAN)]
    up = [(core, (chip + t + 1) % n_dp) for t in range(SPAN)]
    pin = [rc(K.pmsg.at[pair(t)], K.arp.at[pair(t)], 0, t, down[t]) for t in range(SPAN)]
    cin = [rc(K.cmsg.at[pair(t)], K.arc.at[pair(t)], 1, t, down[t]) for t in range(SPAN)]

    if not near:
        kin.wait()
        kout.start()

    @pl.when(first)
    def _():
        pack_go.wait_recv()
        pix_own.wait()

    @pl.when(second)
    def _():
        pix_go.wait_recv()
        pack_own.wait()

    row_at = lax.broadcasted_iota(jnp.int32, (PMAX, ROWS), 1)
    row_of = lax.broadcasted_iota(jnp.int32, (PMAX, ROWS), 0)
    offsets = [jnp.int32(0)]
    for s in range(RSLOT):
        offsets.append(offsets[s] + K.plen[s])

    def prefix_slot(s):
        size = K.plen[s]
        pick = (row_at == row_of + offsets[s]) & (row_of < size)
        K.pmsg[s, 0:PMAX, :] = nn(pick.astype(F32).astype(BF), K.packed[...]).astype(BF)
        K.pmsg[s, PMAX:MSG, :] = jnp.full((MSG - PMAX, HALF), size, jnp.int32).astype(F32).astype(BF)

    place_row = lax.broadcasted_iota(jnp.int32, (PMAX, 1), 0)
    zero = jnp.zeros((), BF)

    def cot_slot(s):
        size = K.plen[s]
        K.cmsg[s, 0:PMAX, :] = jnp.where(place_row < size, K.cot[s, NP:SEQ, :], zero)
        K.cmsg[s, PMAX : PMAX + NP, :] = jnp.where(
            jnp.full((NP, 1), size, jnp.int32) > 0, K.cot[s, 0:NP, :], zero
        )
        K.cmsg[s, PMAX + NP : R, :] = jnp.zeros((NPAD - NP, HALF), BF)

    for s in range(4):
        prefix_slot(s)
    advance(2)
    for s in range(4, RSLOT):
        prefix_slot(s)
    for t in ISSUE:
        pin[t].start()
    advance(2)
    for s in range(0, RSLOT, 2):
        cot_slot(s)
        cot_slot(s + 1)
        advance(2)
    for i in range(OWN):
        K.pix[i, 0:NP, :] = K.raw[NP * i : NP * (i + 1), :]
        K.pix[i, NP:NPAD, :] = jnp.zeros((NPAD - NP, D), BF)
    advance(2 * CIN_AT - 14)
    for t in ISSUE:
        cin[t].start()
    advance(99)
    if not near:
        for p in range(2):
            rows = (CUT, SLAB - CUT)[p] * 16
            piece = wall.at[pl.ds(0, rows)]
            pltpu.make_async_copy(piece, piece, gsems[p * n_sems + n_sems - 1]).wait()
        pltpu.make_async_copy(K.vbuf.at[pl.ds(0, 31)], K.vbuf.at[pl.ds(0, 31)], K.vsem.at[1]).wait()
    vec = jnp.zeros((VEC, D), F32)
    lane_d = lax.broadcasted_iota(jnp.int32, (1, D), 1)
    n_dev = 2 * n_dp
    width = D // n_dev
    if near:
        K.vec[...] = K.vblk[...].astype(F32)
    else:

        def spread(k, total):
            block = jnp.concatenate([K.vbuf[k].astype(F32), jnp.zeros((VEC, D - 128), F32)], axis=1)
            block = jnp.where(lane_d < width, block, 0.0)
            return total + pltpu.roll(block, k * width, 1)

        K.vec[...] = lax.fori_loop(0, n_dev, spread, vec)
    for j in range(4):
        K.bias[:, j * D : (j + 1) * D] = K.vec[5 + j : 6 + j, :]
    def load(dst, lo, n, sem):
        return pltpu.make_async_copy(wall.at[pl.ds(lo, n)], dst, sem)

    ls = load(K.stem, 0, PIX, K.wsem.at[0])
    lq = load(K.qkvw, PIX, 3 * D, K.wsem.at[1])
    lo_ = load(K.outw, PIX + 3 * D, D, K.wsem.at[2])
    if not near:
        kout.wait()
    ls.start()
    lq.start()
    lo_.start()

    def chunk(c, slot):
        at = pl.multiple_of(c * CH, 16)
        return (
            pltpu.make_async_copy(wall.at[pl.ds(UP + at, CH)], K.upb.at[slot], K.csem.at[0, slot]),
            pltpu.make_async_copy(wall.at[pl.ds(DOWN + at, CH)], K.downb.at[slot], K.csem.at[1, slot]),
        )

    def mine(k):
        return K.dest[OWN * core + k]

    def image_of(slot):
        found = jnp.int32(IMG_DEV)
        for j in range(IMG_DEV):
            found = jnp.where(K.dest[j] == slot, j, found)
        return found

    def theirs(k):
        return K.dest[OWN * (1 - core) + k]

    own_half = pl.ds(pl.multiple_of(core * HALF, 128), HALF)
    other_half = pl.ds(pl.multiple_of((1 - core) * HALF, 128), HALF)

    def swap(src, dst, k):
        return remote(src, dst, K.gsem.at[0, k], K.gsem.at[1, k], sib)

    pswap = swap(K.gvp, K.gtp, 0)
    cswap = swap(K.gvc, K.gtc, 1)
    for cp in pin:
        cp.wait_recv()
    for k in range(OWN):
        K.gvp[k] = K.arp[theirs(k)]
    lens = []
    for k in range(OWN):
        K.x[R * k : R * k + PMAX, own_half] = K.arp[mine(k), 0:PMAX, :]
        lens.append(K.arp[mine(k), PMAX:MSG, :].astype(F32)[0:1, 0:1])
    pswap.start()
    ls.wait()
    for i in range(OWN):
        K.x[R * i + PMAX : R * (i + 1), :] = nn(K.pix[i], K.stem[...]).astype(BF)
    pswap.wait_recv()
    for k in range(OWN):
        K.x[R * k : R * k + PMAX, other_half] = K.gtp[k, 0:PMAX, :]

    def norm1(rows):
        xhat, _ = norm_parts(K.x[rows, :].astype(F32))
        K.nrm[rows, :] = (xhat * K.vec[0:1, :] + K.vec[1:2, :]).astype(BF)

    rows_loop(norm1)
    lq.wait()
    for k in range(3):
        K.qkv[:, k * D : (k + 1) * D] = nt(K.nrm[...], K.qkvw[k * D : (k + 1) * D, :]).astype(BF)
    lane = lax.broadcasted_iota(jnp.int32, (1, 128), 1)
    low_half = lane < HD
    key = lax.broadcasted_iota(jnp.int32, (1, R), 1)
    scale = HD**-0.5

    def heads(i, p):
        ln = jnp.where(i == 0, lens[0], lens[1])
        ok = (key.astype(F32) < ln) | ((key >= PMAX) & (key < PMAX + NP))
        rows = pl.ds(pl.multiple_of(i * R, 16), R)

        def part(k):
            return K.qkv[rows, pl.ds(pl.multiple_of(k * D + p * 128, 128), 128)]

        return rows, ok, part(0), part(1), part(2)

    def halves(v):
        return jnp.where(low_half, v, zero), jnp.where(low_half, zero, v)

    def attend(n, c):
        i, p = n // 6, n % 6
        rows, ok, q, k, v = heads(i, p)
        outs = []
        for h, qh in enumerate(halves(q)):
            s = jnp.where(ok, nt(qh, k) * scale, MASKED)
            e = jnp.exp(s - jnp.max(s, axis=-1, keepdims=True))
            a = (e * (1.0 / jnp.sum(e, axis=-1, keepdims=True))).astype(BF)
            K.prob[2 * n + h] = a
            outs.append(nn(a, v))
        here = pl.ds(pl.multiple_of(p * 128, 128), 128)
        K.ctx[rows, here] = jnp.where(low_half, outs[0], outs[1]).astype(BF)
        return c

    lax.fori_loop(0, OWN * 6, attend, 0, unroll=3)
    lo_.wait()
    K.res[...] = nt(K.ctx[...], K.outw[...])

    def norm2(rows):
        r = K.res[rows, :] + K.x[rows, :].astype(F32)
        K.res[rows, :] = r
        xhat, _ = norm_parts(r)
        K.mlp[rows, :] = (xhat * K.vec[2:3, :] + K.vec[3:4, :]).astype(BF)
        K.big[rows, :] = r + K.vec[4:5, :]

    rows_loop(norm2)
    count = FF // CH

    def fetch(c, slot):
        for cp in chunk(c, slot):
            cp.wait()

        @pl.when(c + 1 < count)
        def _():
            for cp in chunk(c + 1, 1 - slot):
                cp.start()

    def ffn(c, carry):
        slot = lax.rem(c, 2)
        fetch(c, slot)
        cols = pl.ds(pl.multiple_of(c * CH, 128), CH)
        K.f1[...] = nt(K.mlp[...], K.upb[slot])
        b = K.bias[:, cols]

        def act(i, none):
            rows = pl.ds(pl.multiple_of(i * LNB, 16), LNB)
            h, dh = gelu_both(K.f1[rows, :] + b)
            K.hid[rows, cols] = h.astype(BF)
            K.slope[rows, cols] = dh.astype(BF)
            return none

        lax.fori_loop(0, M // LNB, act, 0, unroll=True)
        K.big[...] += nn(K.hid[:, cols], K.downb[slot])
        return carry

    for cp in chunk(0, 0):
        cp.start()
    lax.fori_loop(0, count, ffn, 0)
    for cp in chunk(0, 0):
        cp.start()
    for k in range(OWN):
        K.gvo[k] = K.big[R * k : R * (k + 1), other_half].astype(BF)
    for k in range(OWN):
        K.img[OWN * core + k] = K.big[R * k : R * (k + 1), own_half].astype(BF)
    K.img[IMG_DEV] = jnp.zeros((R, HALF), BF)
    oswap = swap(K.gvo, K.img.at[pl.ds(OWN * core, OWN)], 2)
    oswap.start()
    K.big[...] = jnp.zeros((M, D), F32)
    for cp in cin:
        cp.wait_recv()
    for k in range(OWN):
        K.gvc[k] = K.arc[theirs(k)]
    for k in range(OWN):
        K.og[R * k : R * (k + 1), own_half] = K.arc[mine(k)]
    cswap.start()
    oswap.wait()
    for cp in cin:
        cp.wait_send()
    for k in range(RSLOT):
        K.cmsg[k] = K.img[image_of(k)]
    cswap.wait_recv()
    for k in range(OWN):
        K.og[R * k : R * (k + 1), other_half] = K.gtc[k]
    eout = [rc(K.cmsg.at[pair(t)], K.encm.at[pair(t)], 2, t, up[t]) for t in range(SPAN)]
    for t in ISSUE:
        eout[t].start()

    def store(c, slot):
        at = pl.multiple_of(c * CH, 16)
        return (
            pltpu.make_async_copy(K.gub.at[slot], K.g.at[pl.ds(UP + at, CH)], K.osem.at[0, slot]),
            pltpu.make_async_copy(K.gdb.at[slot], K.g.at[pl.ds(DOWN + at, CH)], K.osem.at[1, slot]),
        )

    def ffn_back(c, carry):
        slot = lax.rem(c, 2)
        fetch(c, slot)

        @pl.when(c >= 2)
        def _():
            for cp in store(c - 2, slot):
                cp.wait()

        cols = pl.ds(pl.multiple_of(c * CH, 128), CH)
        K.f1[...] = nt(K.og[...], K.downb[slot])

        def act(i, tot):
            rows = pl.ds(pl.multiple_of(i * 16, 16), 16)
            dp = (K.f1[rows, :] * K.slope[rows, cols].astype(F32)).astype(BF)
            K.dpr[rows, :] = dp
            return tot + dp.astype(F32)

        tot = lax.fori_loop(0, M // 16, act, jnp.zeros((16, CH), F32), unroll=2)
        K.bg[:, cols] = jnp.sum(tot, axis=0, keepdims=True)
        K.big[...] += nn(K.dpr[...], K.upb[slot])
        K.gub[slot] = tn(K.dpr[...], K.mlp[...]).astype(BF)
        K.gdb[slot] = tn(K.hid[:, cols], K.og[...]).astype(BF)
        for cp in store(c, slot):
            cp.start()
        return carry

    lax.fori_loop(0, count, ffn_back, 0)
    for slot in range(2):
        for cp in store(count - 2 + slot, slot):
            cp.wait()
    late = []
    if not near:

        def obuf(i):
            return K.wb.at[i // 2, pl.ds(pl.multiple_of((i % 2) * PART, 16), PART)]

        begin, late, end_sum = sum_steps(1, K.g, K.r1, obuf, sum_refs, SUM_VIA)
        begin()

    def advance_sum(n=1):
        for _ in range(n):
            if late:
                late.pop(0)()

    def back2(i, c):
        rows = pl.ds(pl.multiple_of(i * LNB, 16), LNB)
        o = K.og[rows, :].astype(F32)
        d, dg, dc = norm_back(K.res[rows, :], K.big[rows, :], K.vec[2:3, :])
        d = d + o
        K.res[rows, :] = d
        K.dx[rows, :] = d.astype(BF)
        return (c[0] + dg, c[1] + dc, c[2] + jnp.sum(o, axis=0, keepdims=True))

    none = jnp.zeros((1, D), F32)
    dg2, dc2, dob = lax.fori_loop(0, M // LNB, back2, (none, none, none), unroll=True)
    K.vg[8:VEC, :] = jnp.zeros((VEC - 8, D), F32)
    K.vg[2:3, :] = dg2
    K.vg[3:4, :] = dc2
    K.vg[4:5, :] = dob
    for j in range(4):
        K.vg[5 + j : 6 + j, :] = K.bg[:, j * D : (j + 1) * D]

    advance_sum()

    def put(src, lo, n, sem):
        return pltpu.make_async_copy(src, K.g.at[pl.ds(lo, n)], sem)

    K.mlp[...] = nn(K.dx[...], K.outw[...]).astype(BF)
    advance_sum()
    K.outw[...] = tn(K.dx[...], K.ctx[...]).astype(BF)
    po = put(K.outw, PIX + 3 * D, D, K.wsem.at[2])
    po.start()

    def attend_back(n, c):
        i, p = n // 6, n % 6
        rows, ok, q, k, v = heads(i, p)
        here = pl.ds(pl.multiple_of(p * 128, 128), 128)
        dc = K.mlp[rows, here]
        dq = []
        dk = dv = None
        for h, (qh, dch) in enumerate(zip(halves(q), halves(dc))):
            a = K.prob[2 * n + h]
            af = a.astype(F32)
            t = af * nt(dch, v)
            dsc = (t - af * jnp.sum(t, axis=-1, keepdims=True)).astype(BF)
            dq.append(nn(dsc, k))
            dkh = tn(dsc, qh)
            dvh = tn(a, dch)
            dk = dkh if dk is None else dk + dkh
            dv = dvh if dv is None else dv + dvh

        def at(j):
            return pl.ds(pl.multiple_of(j * D + p * 128, 128), 128)

        K.qkv[rows, at(0)] = (jnp.where(low_half, dq[0], dq[1]) * scale).astype(BF)
        K.qkv[rows, at(1)] = (dk * scale).astype(BF)
        K.qkv[rows, at(2)] = dv.astype(BF)
        return c

    advance_sum()
    for group in range(6):
        lax.fori_loop(2 * group, 2 * group + 2, attend_back, 0, unroll=2)
        advance_sum()
    K.big[...] = nn(K.qkv[...], K.qkvw[...])
    advance_sum()

    def back1(i, c):
        rows = pl.ds(pl.multiple_of(i * LNB, 16), LNB)
        d, dg, dc = norm_back(K.x[rows, :].astype(F32), K.big[rows, :], K.vec[0:1, :])
        K.dx[rows, :] = (K.res[rows, :] + d).astype(BF)
        return (c[0] + dg, c[1] + dc)

    dg1, dc1 = lax.fori_loop(0, M // LNB, back1, (none, none), unroll=True)
    advance_sum()
    pswap.wait_send()
    cswap.wait_send()
    for k in range(OWN):
        K.gvp[k, 0:PMAX, :] = K.dx[R * k : R * k + PMAX, other_half]
    for k in range(OWN):
        K.pim[OWN * core + k] = K.dx[R * k : R * k + PMAX, own_half]
    K.pim[IMG_DEV] = jnp.zeros((PMAX, HALF), BF)
    dswap = swap(K.gvp.at[:, pl.ds(0, PMAX)], K.pim.at[pl.ds(OWN * core, OWN)], 3)
    dswap.start()
    K.vg[0:1, :] = dg1
    K.vg[1:2, :] = dc1

    def cut(k, c):
        K.vgb[k] = pltpu.roll(K.vg[...], lax.rem(D - k * width, D), 1)[:, 0:128]
        return c

    lax.fori_loop(0, n_dev, cut, 0)
    for k in range(3):
        K.qkvw[k * D : (k + 1) * D, :] = tn(K.qkv[:, k * D : (k + 1) * D], K.nrm[...]).astype(BF)
    pq = put(K.qkvw, PIX, 3 * D, K.wsem.at[1])
    pq.start()
    dswap.wait()
    if not near:
        advance_sum(99)
    for k in range(RSLOT):
        K.pback[k] = K.pim[image_of(k)]
    dout = [rc(K.pback.at[pair(t)], K.dprem.at[pair(t)], 3, t, up[t]) for t in range(SPAN)]
    for t in ISSUE:
        dout[t].start()
    tot = None
    for i in range(OWN):
        dp = K.dx[R * i + PMAX : R * (i + 1), :]
        K.dpix[i] = nt(dp, K.stem[...]).astype(BF)
        t = tn(K.pix[i], dp)
        tot = t if tot is None else tot + t
    K.stem[...] = tot.astype(BF)
    ps = put(K.stem, 0, PIX, K.wsem.at[0])
    ps.start()
    for cp in eout + dout:
        cp.wait()
    po.wait()
    pq.wait()
    ps.wait()
    for cp in pin:
        cp.wait_send()

    @pl.when(first)
    def _():
        pix_go.wait_send()

    @pl.when(second)
    def _():
        pack_go.wait_send()

    if not near:
        end_sum()
        for p in range(2):
            for step in gather_steps(
                K.wsh, wall, gsems[p * n_sems : (p + 1) * n_sems], p, draining=True
            ):
                step()
            rows = (CUT, SLAB - CUT)[p] * 16
            piece = wall.at[pl.ds(0, rows)]
            pltpu.make_async_copy(piece, piece, gsems[p * n_sems + n_sems - 2]).wait()
        pltpu.make_async_copy(K.vbuf.at[pl.ds(0, 31)], K.vbuf.at[pl.ds(0, 31)], K.vsem.at[0]).wait()


def whole_block(dest, plen, rows, cot, wsh, vblk, wfull, n_dev):
    near = wfull is not None
    any_ = pl.BlockSpec(memory_space=pl.ANY)
    vmem = pl.BlockSpec(memory_space=pltpu.VMEM)
    smem = pl.BlockSpec(memory_space=pltpu.SMEM)
    total = SLAB * 32 if not near else wfull.shape[0]
    if near:
        wsh = wsh[:8]
    else:
        wfull = wsh[:8]
    outs = (
        jax.ShapeDtypeStruct((OWN, NPAD, D), BF),
        jax.ShapeDtypeStruct((n_dev, VEC, 128), F32),
        jax.ShapeDtypeStruct((total, D), BF),
        jax.ShapeDtypeStruct((RSLOT, R, HALF), BF),
        jax.ShapeDtypeStruct((RSLOT, PMAX, HALF), BF),
        jax.ShapeDtypeStruct((8, D) if near else (total, D), BF),
        jax.ShapeDtypeStruct((8, D) if near else (SLAB, D), F32),
    )
    return pl.pallas_call(
        functools.partial(x_kernel, near),
        out_shape=outs,
        in_specs=[smem, smem, any_, vmem, any_, vmem, any_],
        out_specs=(vmem, vmem, any_, any_, any_, any_, vmem),
        scratch_shapes=[pltpu.VMEM(s, t) for _, s, t in X_SCRATCH]
        + [dma(s) for _, s in X_SEMS]
        + ([] if near else gather_sems() + gather_sems() + rs_scratch()),
        compiler_params=pltpu.CompilerParams(
            collective_id=3, has_side_effects=True, vmem_limit_bytes=63 * 2**20
        ),
    )(dest, plen, rows, cot, wsh, vblk, wfull)


def swapped(value):
    return lax.ppermute(value, "stream", [(0, 1), (1, 0)])


def body(
    stream_rows,
    dest,
    prefix_len,
    weights,
    momentum,
    average,
    vectors,
    vec_momentum,
    vec_average,
    cotangent,
):
    core = lax.axis_index("stream")
    first = core == 0
    n_dp = lax.axis_size("dp")
    n_dev = 2 * n_dp
    lane = vectors.shape[1]
    kernels = n_dp == 16

    rows = stream_rows[0, 0]
    half_rows = ROWS // 2
    lengths = prefix_len[0]
    slots = dest[0]
    shard = weights.astype(BF)
    if kernels:
        full = None
        block = jnp.pad(vectors.astype(BF), ((0, VEC - 9), (0, 128 - lane)))
    else:
        full = lax.all_gather(shard, ALL, axis=0, tiled=True)
        block = jnp.pad(vectors.astype(BF), ((0, VEC - 9), (0, 0)))
        block = lax.all_gather(block, ALL, axis=1, tiled=True)
    d_pixels, vec_blocks, grads, enc_back, prefix_back, _, late_grad = whole_block(
        slots, lengths, rows, cotangent[0], shard, block, full, n_dev
    )
    if kernels:
        early_grad, vec_grad, d_rows = summed(
            lengths, grads, vec_blocks, prefix_back, d_pixels
        )
        weight_grad = jnp.where(first, early_grad, late_grad)
    else:
        weight_grad = lax.psum_scatter(grads, ALL, scatter_dimension=0, tiled=True).astype(F32)
        vec_grad = lax.psum_scatter(vec_blocks, ALL, scatter_dimension=0, tiled=True)[0]
    vec_grad = vec_grad[:9, :lane]

    columns = jnp.arange(SEQ, dtype=jnp.int32)
    row_ok = (columns[None, :] < NP + lengths[:, None]) & (lengths[:, None] > 0)
    enc_out = jnp.concatenate([enc_back[:, PMAX : PMAX + NP], enc_back[:, :PMAX]], axis=1)
    enc_out = jnp.where(row_ok[:, :, None], enc_out, jnp.zeros((), BF))[None]

    if not kernels:
        offsets = jnp.cumsum(lengths) - lengths
        places = jnp.arange(PMAX, dtype=jnp.int32)
        row_index = offsets[:, None] + places[None, :]
        keep_mask = places[None, :] < lengths[:, None]
        rows_at = jnp.arange(ROWS, dtype=jnp.int32)
        pick = (
            (row_index.reshape(-1)[:, None] == rows_at[None, :]) & keep_mask.reshape(-1)[:, None]
        ).astype(BF)
        d_packed = tn(pick, prefix_back.reshape(RSLOT * PMAX, HALF)).astype(BF)
        d_pixels = d_pixels[:, :NP].reshape(half_rows, D)
        give = jnp.where(
            first, jnp.concatenate([d_packed[:half_rows], d_packed[half_rows:]], axis=1), d_pixels
        )
        got = swapped(give)
        d_image_rows = jnp.concatenate([d_pixels, got])
        d_text_rows = jnp.concatenate(
            [jnp.concatenate([got[:, :HALF], got[:, HALF:]], axis=0), d_packed], axis=1
        )
        d_rows = jnp.where(first, d_image_rows, d_text_rows)
    d_rows = d_rows.astype(F32)[None, None]

    rate = 0.5 * (D * IMG_DEV * n_dp * NP) ** (-0.5)
    new_momentum = MOMENT * momentum + weight_grad
    new_weights = weights - rate * (weight_grad + MOMENT * new_momentum)
    new_average = DECAY * average + (1.0 - DECAY) * new_weights
    vec_new_momentum = MOMENT * vec_momentum + vec_grad
    vec_new = vectors - rate * (vec_grad + MOMENT * vec_new_momentum)
    vec_new_average = DECAY * vec_average + (1.0 - DECAY) * vec_new
    return (
        enc_out,
        d_rows,
        weight_grad,
        new_momentum,
        new_average,
        new_weights,
        new_weights.astype(BF),
        vec_grad,
        vec_new_momentum,
        vec_new_average,
        vec_new,
        vec_new.astype(BF),
    )


def solution(mesh):
    both = P(ALL, None)
    lanes = P(None, ALL)
    in_specs = (
        P("stream", "dp", None, None),
        P("dp", None),
        P("dp", None),
        both,
        both,
        both,
        lanes,
        lanes,
        lanes,
        P("dp", None, None, "stream"),
    )
    out_specs = (
        P("dp", None, None, "stream"),
        P("stream", "dp", None, None),
        both,
        both,
        both,
        both,
        both,
        lanes,
        lanes,
        lanes,
        lanes,
        lanes,
    )
    return jax.shard_map(body, mesh=mesh, in_specs=in_specs, out_specs=out_specs, check_vma=False)
```

```python
import functools
from types import SimpleNamespace

import jax
import jax.numpy as jnp
from jax import lax
from jax.experimental import pallas as pl
from jax.experimental.pallas import tpu as pltpu
from jax.sharding import PartitionSpec as P

D = 768
HEADS = 12
HD = 64
FF = 3072
PIX = 768
NP = 196
PMAX = 64
SPAN = 4
IMG_DEV = 4
CAP = 2
RSLOT = 8
SEQ = 260
ROWS = 784
HALF = D // 2
OWN = IMG_DEV // 2
SLAB = 312
CUT = 160
NZ = 4

EPSILON = 1e-06
MASKED = -1e30
MOMENT = 0.5
DECAY = 0.5
BF = jnp.bfloat16
F32 = jnp.float32
ALL = ("stream", "dp")
MESH = pl.DeviceIdType.MESH


NPAD = 208
R = PMAX + NPAD
M = OWN * R
CH = 512
LNB = 32
MSG = PMAX + 16
VEC = 16
UP = PIX + 4 * D
DOWN = UP + FF
VIA_Z = (1, 2)
CIN_AT = 12
ISSUE = (1, 3, 0, 2)
SUM_VIA = (1, 2)
dma = pltpu.SemaphoreType.DMA


def nn(a, b):
    return lax.dot_general(a, b, (((1,), (0,)), ((), ())), preferred_element_type=F32)


def nt(a, b):
    return lax.dot_general(a, b, (((1,), (1,)), ((), ())), preferred_element_type=F32)


def tn(a, b):
    return lax.dot_general(a, b, (((0,), (0,)), ((), ())), preferred_element_type=F32)


def erf(v):
    v = jnp.clip(v, -3.832506856900711, 3.832506856900711)
    s = v * v
    top = 0.00022905065861350646
    for c in (0.0034082910107109506, 0.050955695062380861, 0.18520832239976145, 1.128379143519084):
        top = top * s + c
    low = -1.1791602954361697e-7
    for c in (
        0.000023547966471313185,
        0.0010179625278914885,
        0.014070470171167667,
        0.11098505178285362,
        0.49746925110067538,
        1.0,
    ):
        low = low * s + c
    return v * top / low


def gelu_both(v):
    phi = 0.5 * (1.0 + erf(v * 0.7071067811865476))
    return v * phi, phi + v * (0.3989422804014327 * jnp.exp(-0.5 * v * v))


def rows_loop(f, block=LNB, total=M):
    def run(i, c):
        f(pl.ds(pl.multiple_of(i * block, 16), block))
        return c

    lax.fori_loop(0, total // block, run, 0, unroll=True)


def norm_parts(v):
    off = v - jnp.mean(v, axis=-1, keepdims=True)
    inv = lax.rsqrt(jnp.mean(off * off, axis=-1, keepdims=True) + EPSILON)
    return off * inv, inv


def norm_back(v, dn, gain):
    xhat, inv = norm_parts(v)
    dx = dn * gain
    low = jnp.mean(dx, axis=-1, keepdims=True)
    slope = jnp.mean(dx * xhat, axis=-1, keepdims=True)
    return (
        (dx - low - xhat * slope) * inv,
        jnp.sum(dn * xhat, axis=0, keepdims=True),
        jnp.sum(dn, axis=0, keepdims=True),
    )


def slot_rows(plen, dim):
    shape = (RSLOT * PMAX, 1) if dim == 0 else (1, RSLOT * PMAX)
    at = lax.broadcasted_iota(jnp.int32, shape, dim)
    target = jnp.full(shape, -1, jnp.int32)
    offset = jnp.int32(0)
    for s in range(RSLOT):
        i = at - PMAX * s
        target = jnp.where((i >= 0) & (i < plen[s]), i + offset, target)
        offset = offset + plen[s]
    return target


def remote(src, dst, send, recv, dev):
    return pltpu.make_async_remote_copy(
        src_ref=src, dst_ref=dst, send_sem=send, recv_sem=recv, device_id=dev, device_id_type=MESH
    )


def place():
    core = lax.axis_index("stream")
    chip = lax.axis_index("dp")
    return core, chip, chip % 2, (chip // 2) % 2, chip // 4


def greet_all(core, chip):
    barrier = pltpu.get_barrier_semaphore()
    me = core * 16 + chip

    def one(k, carry):
        peer = (me + k) % 32
        pl.semaphore_signal(barrier, inc=1, device_id=(peer // 16, peer % 16), device_id_type=MESH)
        return carry

    lax.fori_loop(1, 32, one, 0)
    pl.semaphore_wait(barrier, 31)


def greet_near(core, chip, n_dp):
    barrier = pltpu.get_barrier_semaphore()
    for t in range(1, SPAN + 1):
        for peer in ((chip + t) % n_dp, (chip + n_dp - t) % n_dp):
            pl.semaphore_signal(barrier, inc=1, device_id=(core, peer), device_id_type=MESH)
    pl.semaphore_signal(barrier, inc=1, device_id=(1 - core, chip), device_id_type=MESH)
    pl.semaphore_wait(barrier, 2 * SPAN + 1)


def gather_sems():
    four = dma((4,))
    return [dma((2, 4)), four, dma((2, 4)), four] + [four] * 8 + [dma, dma]


def gather_steps(w_ref, out, sems, part, draining=False):
    core, chip, x, y, z = place()
    zs, zr, ds, dr, xs, xr, ys, yr, as_, ar, bs, br, ss, sr = sems
    base = core * 16
    me = base + chip
    flat = chip % 4
    xn = chip + 1 - 2 * x
    yn = chip + 2 - 4 * y
    start, size = ((0, CUT), (CUT, SLAB - CUT))[part]
    top = pl.ds(0, 80)
    bottom = pl.ds(80, size - 80)
    sib = (1 - core, chip)
    w_ref = w_ref.at[pl.ds(start, size)]

    def slab_of(slab, rows=None):
        whole = out.at[pl.ds(pl.multiple_of(slab * SLAB + start, 8), size)]
        return whole if rows is None else whole.at[rows]

    def rc(src, slab, ssem, rsem, dev, rows=None):
        return remote(src, slab_of(slab, rows), ssem, rsem, dev)

    def go(cond, make):
        def act():
            if draining:
                make().wait_send()
            else:
                make().start()

        if cond is None:
            act()
        else:
            pl.when(cond)(act)

    def to_sib(src, slab):
        if not draining:
            rc(src, slab, ss, sr, sib).start()

    def arrive(copy):
        if not draining:
            copy().wait_recv()

    def at(t, sign):
        zz = z + sign * t
        return zz, (zz >= 0) & (zz < NZ)

    def own():
        go(None, lambda: rc(w_ref, me, xs.at[z], xr.at[z], (core, xn)))
        go(None, lambda: rc(w_ref, me, ys.at[z], yr.at[z], (core, yn)))
        for k, s in enumerate((1, -1)):
            go(
                (z + s >= 0) & (z + s < NZ),
                lambda k=k, s=s: rc(w_ref, me, zs.at[k, z], zr.at[z], (core, chip + 4 * s)),
            )
        to_sib(w_ref, me)

    def column(t, sign):
        zz, here = at(t, sign)
        slab = base + zz * 4 + flat
        k = 0 if sign < 0 else 1

        @pl.when(here)
        def _():
            arrive(lambda: rc(w_ref, slab, ss, zr.at[zz], sib))

        src = slab_of(slab)
        go(
            here & (z - sign >= 0) & (z - sign < NZ),
            lambda: rc(src, slab, zs.at[k, zz], zr.at[zz], (core, chip - 4 * sign)),
        )
        go(here, lambda: rc(src, slab, xs.at[zz], xr.at[zz], (core, xn)))
        go(here, lambda: rc(src, slab, ys.at[zz], yr.at[zz], (core, yn)))

        @pl.when(here)
        def _():
            to_sib(src, slab)

    def plane(t, sign):
        zz, here = at(t, sign)
        xslab = base + zz * 4 + flat + 1 - 2 * x
        yslab = base + zz * 4 + flat + 2 - 4 * y

        @pl.when(here)
        def _():
            arrive(lambda: rc(w_ref, xslab, ss, xr.at[zz], sib))

        if t not in VIA_Z:
            go(
                here,
                lambda: rc(slab_of(xslab, top), xslab, as_.at[zz], ar.at[zz], (core, yn), top),
            )

        @pl.when(here)
        def _():
            arrive(lambda: rc(w_ref, yslab, ss, yr.at[zz], sib))

        if t not in VIA_Z:
            go(
                here,
                lambda: rc(slab_of(yslab, bottom), yslab, bs.at[zz], br.at[zz], (core, xn), bottom),
            )

        @pl.when(here)
        def _():
            to_sib(slab_of(xslab), xslab)
            to_sib(slab_of(yslab), yslab)

    def diag(t, sign):
        zz, here = at(t, sign)
        slab = base + zz * 4 + 3 - flat
        src = slab_of(slab)
        if t in VIA_Z:

            @pl.when(here)
            def _():
                arrive(lambda: rc(w_ref, slab, ss, dr.at[zz], sib))
        else:

            @pl.when(here)
            def _():
                arrive(lambda: rc(slab_of(slab, top), slab, ss, ar.at[zz], sib, top))
                arrive(lambda: rc(slab_of(slab, bottom), slab, ss, br.at[zz], sib, bottom))

        if t == 0 and 1 in VIA_Z:
            for k, s in enumerate((1, -1)):
                go(
                    (z + s >= 0) & (z + s < NZ),
                    lambda k=k, s=s: rc(src, slab, ds.at[k, zz], dr.at[zz], (core, chip + 4 * s)),
                )
        if t >= 1 and t + 1 in VIA_Z:
            k = 0 if sign < 0 else 1
            go(
                here & (z - sign >= 0) & (z - sign < NZ),
                lambda: rc(src, slab, ds.at[k, zz], dr.at[zz], (core, chip - 4 * sign)),
            )

        @pl.when(here)
        def _():
            to_sib(src, slab)

    def both(f, t):
        def run():
            f(t, 1)
            if t:
                f(t, -1)

        return run

    return [
        own,
        both(column, 1),
        both(plane, 0),
        both(column, 2),
        both(diag, 0),
        both(plane, 1),
        both(column, 3),
        both(diag, 1),
        both(plane, 2),
        both(plane, 3),
        both(diag, 2),
        both(diag, 3),
    ]


PART = 160
SHIFT = SLAB - PART
ADD = 16
ADD_UNROLL = 1
RS_BUFS = (
    ("sbuf", (16, PART, D), BF),
    ("xb", (4, PART, D), BF),
    ("yb", (4, PART, D), BF),
    ("dzb", (2, 2, PART, D), BF),
    ("czb", (2, 3, PART, D), BF),
    ("ab", (4, PART // 2, D), BF),
    ("bb", (4, PART // 2, D), BF),
    ("fin", (PART, D), F32),
)
RS_SEMS = (
    ("load", (16,)),
    ("ssend", ()),
    ("srecv", (16,)),
    ("xs", (4,)),
    ("xr", (4,)),
    ("ys", (4,)),
    ("yr", (4,)),
    ("dzs", (2, 2)),
    ("dzr", (2, 2)),
    ("czs", (2, 3)),
    ("czr", (2, 3)),
    ("as_", (4,)),
    ("ar", (4,)),
    ("bs", (4,)),
    ("br", (4,)),
    ("fsem", (2,)),
)


def rs_scratch():
    return [pltpu.VMEM(s, t) for _, s, t in RS_BUFS] + [dma(s) for _, s in RS_SEMS]


def add_rows(dst, sources, lo, size):
    def piece(i, c):
        tot = None
        for ref, at in sources:
            v = ref[pl.ds(pl.multiple_of(at + i * ADD, 16), ADD), :].astype(F32)
            tot = v if tot is None else tot + v
        dst[pl.ds(pl.multiple_of(lo + i * ADD, 16), ADD), :] = tot.astype(dst.dtype)
        return c

    lax.fori_loop(0, size // ADD, piece, 0, unroll=ADD_UNROLL)


class Sends:
    def __init__(self):
        self.kept = []

    def go(self, cond, make):
        if cond is None:
            make().start()
        else:

            @pl.when(cond)
            def _():
                make().start()

        self.kept.append((cond, make))

    def drain(self):
        for cond, make in self.kept:
            if cond is None:
                make().wait_send()
            else:

                @pl.when(cond)
                def _(make=make):
                    make().wait_send()


def sum_steps(half, g, result, obuf, refs, via):
    B = SimpleNamespace(**dict(zip([n for n, _, _ in RS_BUFS] + [n for n, _ in RS_SEMS], refs)))
    core, chip, x, y, z = place()
    flat = chip % 4
    xn = chip + 1 - 2 * x
    yn = chip + 2 - 4 * y
    sib = (1 - core, chip)
    mid = PART // 2
    top = pl.ds(0, mid)
    bottom = pl.ds(mid, mid)
    fd, fx, fy = 3 - flat, flat + 1 - 2 * x, flat + 2 - 4 * y
    sends = Sends()

    def rows_of(i, part):
        return g.at[pl.ds(pl.multiple_of((16 * half + i) * SLAB + part * SHIFT, 8), PART)]

    def each(t, f):
        if t == 0:
            f(z, 0, None)
            return
        for sign in (1, -1):
            zz = z + sign * t
            f(zz, sign, (zz >= 0) & (zz < NZ))

    def when(cond, f):
        if cond is None:
            f()
        else:
            pl.when(cond)(f)

    order = [(fd, 3), (fd, 2), (fx, 3), (fy, 3), (fx, 2), (fy, 2), (fd, 1), (flat, 3)]
    order += [(fx, 1), (fy, 1), (fd, 0), (flat, 2), (fx, 0), (fy, 0), (flat, 1), (flat, 0)]

    def start():
        for f, t in order:

            def begin(zz, sign, here, f=f):
                i = zz * 4 + f

                def go():
                    remote(rows_of(i, 1 - core), B.sbuf.at[i], B.ssend, B.srecv.at[i], sib).start()
                    pltpu.make_async_copy(rows_of(i, core), obuf(i), B.load.at[i]).start()

                when(here, go)

            each(t, begin)

    def ready(i):
        pltpu.make_async_copy(rows_of(i, core), obuf(i), B.load.at[i]).wait()
        remote(rows_of(i, core), B.sbuf.at[i], B.ssend, B.srecv.at[i], sib).wait_recv()

    def landed(dst, send, recv):
        remote(dst, dst, send, recv, sib).wait_recv()

    def up_down(sign):
        return 0 if sign > 0 else 1

    def inside(zz):
        return (zz >= 0) & (zz < NZ)

    def diag(t):
        def f(zz, sign, here):
            i = zz * 4 + fd

            def work():
                ready(i)
                src = [(obuf(i), 0), (B.sbuf.at[i], 0)]
                if t in via and t + 1 in via:
                    k = up_down(sign)
                    far = inside(z - sign)

                    @pl.when(far)
                    def _():
                        landed(B.dzb.at[k, t], B.dzs.at[k, t], B.dzr.at[k, t])
                        add_rows(obuf(i), src + [(B.dzb.at[k, t], 0)], 0, PART)

                    @pl.when(jnp.logical_not(far))
                    def _():
                        add_rows(obuf(i), src, 0, PART)

                elif t == 0 and 1 in via:
                    add_rows(obuf(i), src, 0, PART)
                    for k, s in enumerate((1, -1)):

                        @pl.when(inside(z - s))
                        def _(k=k):
                            landed(B.dzb.at[k, 0], B.dzs.at[k, 0], B.dzr.at[k, 0])
                            add_rows(obuf(i), [(obuf(i), 0), (B.dzb.at[k, 0], 0)], 0, PART)

                else:
                    add_rows(obuf(i), src, 0, PART)

            when(here, work)
            if t in via:
                k = up_down(sign)
                sends.go(
                    here,
                    lambda: remote(
                        obuf(i),
                        B.dzb.at[k, t - 1],
                        B.dzs.at[k, t - 1],
                        B.dzr.at[k, t - 1],
                        (core, chip + 4 * sign),
                    ),
                )
            else:
                sends.go(
                    here,
                    lambda: remote(
                        obuf(i).at[top], B.ab.at[zz], B.as_.at[zz], B.ar.at[zz], (core, yn)
                    ),
                )
                sends.go(
                    here,
                    lambda: remote(
                        obuf(i).at[bottom], B.bb.at[zz], B.bs.at[zz], B.br.at[zz], (core, xn)
                    ),
                )

        return lambda: each(t, f)

    def plane(t):
        def f(zz, sign, here):
            ix, iy = zz * 4 + fx, zz * 4 + fy

            def work_x():
                ready(ix)
                src = [(obuf(ix), 0), (B.sbuf.at[ix], 0)]
                if t in via:
                    add_rows(obuf(ix), src, 0, PART)
                else:
                    add_rows(obuf(ix), [(r, mid) for r, _ in src], mid, mid)
                    landed(B.ab.at[zz], B.as_.at[zz], B.ar.at[zz])
                    add_rows(obuf(ix), src + [(B.ab.at[zz], 0)], 0, mid)

            def work_y():
                ready(iy)
                src = [(obuf(iy), 0), (B.sbuf.at[iy], 0)]
                if t in via:
                    add_rows(obuf(iy), src, 0, PART)
                else:
                    add_rows(obuf(iy), src, 0, mid)
                    landed(B.bb.at[zz], B.bs.at[zz], B.br.at[zz])
                    add_rows(obuf(iy), [(r, mid) for r, _ in src] + [(B.bb.at[zz], 0)], mid, mid)

            when(here, work_x)
            sends.go(
                here, lambda: remote(obuf(ix), B.xb.at[zz], B.xs.at[zz], B.xr.at[zz], (core, xn))
            )
            when(here, work_y)
            sends.go(
                here, lambda: remote(obuf(iy), B.yb.at[zz], B.ys.at[zz], B.yr.at[zz], (core, yn))
            )

        return lambda: each(t, f)

    def column(t):
        def f(zz, sign, here):
            i = zz * 4 + flat
            k = up_down(sign)

            def work():
                ready(i)
                landed(B.xb.at[zz], B.xs.at[zz], B.xr.at[zz])
                landed(B.yb.at[zz], B.ys.at[zz], B.yr.at[zz])
                src = [(obuf(i), 0), (B.sbuf.at[i], 0), (B.xb.at[zz], 0), (B.yb.at[zz], 0)]
                if t == 3:
                    add_rows(obuf(i), src, 0, PART)
                    return
                far = inside(z - sign)

                @pl.when(far)
                def _():
                    landed(B.czb.at[k, t], B.czs.at[k, t], B.czr.at[k, t])
                    add_rows(obuf(i), src + [(B.czb.at[k, t], 0)], 0, PART)

                @pl.when(jnp.logical_not(far))
                def _():
                    add_rows(obuf(i), src, 0, PART)

            when(here, work)
            sends.go(
                here,
                lambda: remote(
                    obuf(i),
                    B.czb.at[k, t - 1],
                    B.czs.at[k, t - 1],
                    B.czr.at[k, t - 1],
                    (core, chip + 4 * sign),
                ),
            )

        return lambda: each(t, f)

    if half == 1:
        part = remote(
            B.fin.at[pl.ds(0, SHIFT)],
            result.at[pl.ds(0, SHIFT)],
            B.fsem.at[0],
            B.fsem.at[1],
            (1, chip),
        )
    else:
        part = remote(
            B.fin.at[pl.ds(PART - SHIFT, SHIFT)],
            result.at[pl.ds(PART, SHIFT)],
            B.fsem.at[0],
            B.fsem.at[1],
            (0, chip),
        )

    def final():
        i = z * 4 + flat
        ready(i)
        landed(B.xb.at[z], B.xs.at[z], B.xr.at[z])
        landed(B.yb.at[z], B.ys.at[z], B.yr.at[z])
        src = [(obuf(i), 0), (B.sbuf.at[i], 0), (B.xb.at[z], 0), (B.yb.at[z], 0)]
        add_rows(B.fin, src, 0, PART)
        for k, s in enumerate((1, -1)):

            @pl.when(inside(z - s))
            def _(k=k):
                landed(B.czb.at[k, 0], B.czs.at[k, 0], B.czr.at[k, 0])
                add_rows(B.fin, [(B.fin, 0), (B.czb.at[k, 0], 0)], 0, PART)

        @pl.when(core == half)
        def _():
            result[pl.ds(half * SHIFT, PART), :] = B.fin[...]

        @pl.when(core != half)
        def _():
            part.start()

    def drain():
        pltpu.make_async_copy(B.sbuf, B.sbuf, B.ssend).wait()
        sends.drain()

        @pl.when(core == half)
        def _():
            part.wait_recv()

        @pl.when(core != half)
        def _():
            part.wait_send()

    steps = [diag(3), diag(2), plane(3), plane(2), diag(1), column(3), plane(1), diag(0)]
    steps += [column(2), plane(0), column(1), final]
    return start, steps, drain


def last_sum(
    plen, g, vg, back, dpix, out, vout, drows, obuf, vbuf, half_rows, tall, vs, vr, vl, es, *refs
):
    core, chip = lax.axis_index("stream"), lax.axis_index("dp")
    me = core * 16 + chip
    first = core == 0
    greet_all(core, chip)
    start, steps, drain = sum_steps(0, g, out, lambda i: obuf.at[i], refs, (1, 2))
    start()

    def vsend(k, carry):
        peer = (me + k) % 32
        remote(vg.at[peer], vbuf.at[me], vs, vr, (peer // 16, peer % 16)).start()
        return carry

    lax.fori_loop(1, 32, vsend, 0)
    vcp = pltpu.make_async_copy(vg.at[me], vbuf.at[me], vl)
    vcp.start()
    steps[0]()
    steps[1]()

    pick = lax.broadcasted_iota(jnp.int32, (ROWS, RSLOT * PMAX), 0) == slot_rows(plen, 1)
    total = nn(pick.astype(F32).astype(BF), back[...].reshape(RSLOT * PMAX, HALF))
    steps[2]()
    steps[3]()
    to_text = remote(tall.at[0], tall.at[1], es.at[0], es.at[1], (1, chip))
    to_image = remote(half_rows.at[0], half_rows.at[1], es.at[0], es.at[1], (0, chip))

    @pl.when(first)
    def _():
        tall[0] = total.astype(BF)
        to_text.start()
        for i in range(OWN):
            drows[NP * i : NP * (i + 1), :] = dpix[i, 0:NP, :]

    @pl.when(core == 1)
    def _():
        for i in range(OWN):
            half_rows[0, NP * i : NP * (i + 1), :] = dpix[i, 0:NP, :]
        to_image.start()
        drows[:, HALF:] = total.astype(BF)

    steps[4]()
    steps[5]()

    @pl.when(first)
    def _():
        to_image.wait_recv()
        drows[OWN * NP :, :] = half_rows[1]

    @pl.when(core == 1)
    def _():
        to_text.wait_recv()
        drows[:, :HALF] = tall[1]

    for step in steps[6:]:
        step()
    vcp.wait()
    pltpu.make_async_copy(vbuf.at[pl.ds(0, 31)], vbuf.at[pl.ds(0, 31)], vr).wait()
    vout[...] = jnp.sum(vbuf[...], axis=0)
    pltpu.make_async_copy(vbuf.at[pl.ds(0, 31)], vbuf.at[pl.ds(0, 31)], vs).wait()

    @pl.when(first)
    def _():
        to_text.wait_send()

    @pl.when(core == 1)
    def _():
        to_image.wait_send()

    drain()


def summed(plen, g, vg, back, dpix):
    any_ = pl.BlockSpec(memory_space=pl.ANY)
    vmem = pl.BlockSpec(memory_space=pltpu.VMEM)
    smem = pl.BlockSpec(memory_space=pltpu.SMEM)
    return pl.pallas_call(
        last_sum,
        out_shape=(
            jax.ShapeDtypeStruct((SLAB, D), F32),
            jax.ShapeDtypeStruct((VEC, 128), F32),
            jax.ShapeDtypeStruct((ROWS, D), BF),
        ),
        in_specs=[smem, any_, any_, vmem, vmem],
        out_specs=(vmem, vmem, vmem),
        scratch_shapes=[
            pltpu.VMEM((16, PART, D), BF),
            pltpu.VMEM((32, VEC, 128), F32),
            pltpu.VMEM((2, OWN * NP, D), BF),
            pltpu.VMEM((2, ROWS, HALF), BF),
            dma,
            dma,
            dma,
            dma((2,)),
        ]
        + rs_scratch(),
        compiler_params=pltpu.CompilerParams(
            collective_id=2, has_side_effects=True, vmem_limit_bytes=60 * 2**20
        ),
    )(plen, g, vg, back, dpix)


X_IN = ("dest", "plen", "rows", "cot", "wsh", "vblk", "wfull")
X_OUT = ("dpix", "vgb", "g", "encm", "dprem", "wall", "r1")
X_SCRATCH = (
    ("packed", (ROWS, HALF), BF),
    ("raw", (ROWS // 2, D), BF),
    ("pmsg", (RSLOT, MSG, HALF), BF),
    ("cmsg", (RSLOT, R, HALF), BF),
    ("arp", (RSLOT, MSG, HALF), BF),
    ("arc", (RSLOT, R, HALF), BF),
    ("gvp", (OWN, MSG, HALF), BF),
    ("gtp", (OWN, MSG, HALF), BF),
    ("gvc", (OWN, R, HALF), BF),
    ("gtc", (OWN, R, HALF), BF),
    ("gvo", (OWN, R, HALF), BF),
    ("img", (IMG_DEV + 1, R, HALF), BF),
    ("pim", (IMG_DEV + 1, PMAX, HALF), BF),
    ("pback", (RSLOT, PMAX, HALF), BF),
    ("vbuf", (32, VEC, 128), BF),
    ("vec", (VEC, D), F32),
    ("bias", (1, FF), F32),
    ("vg", (VEC, D), F32),
    ("bg", (1, FF), F32),
    ("pix", (OWN, NPAD, D), BF),
    ("og", (M, D), BF),
    ("dx", (M, D), BF),
    ("stem", (PIX, D), BF),
    ("qkvw", (3 * D, D), BF),
    ("outw", (D, D), BF),
    ("wb", (8, CH, D), BF),
    ("x", (M, D), BF),
    ("nrm", (M, D), BF),
    ("qkv", (M, 3 * D), BF),
    ("prob", (2 * OWN * 6, R, R), BF),
    ("ctx", (M, D), BF),
    ("res", (M, D), F32),
    ("mlp", (M, D), BF),
    ("big", (M, D), F32),
    ("hid", (M, FF), BF),
    ("slope", (M, FF), BF),
    ("dpr", (M, CH), BF),
    ("f1", (M, CH), F32),
)
X_SEMS = (
    ("psem", (2, 4, SPAN)),
    ("gsem", (2, 6)),
    ("lsem", (8,)),
    ("vsem", (2,)),
    ("wsem", (3,)),
    ("csem", (2, 2)),
    ("osem", (2, 2)),
)


def x_kernel(near, *refs):
    names = X_IN + X_OUT + tuple(n for n, _, _ in X_SCRATCH) + tuple(n for n, _ in X_SEMS)
    K = SimpleNamespace(**dict(zip(names, refs)))
    gsems = refs[len(names) :]
    if not near:
        gsems, sum_refs = gsems[: -len(RS_BUFS) - len(RS_SEMS)], gsems[-len(RS_BUFS) - len(RS_SEMS) :]
    K.upb, K.downb = K.wb.at[pl.ds(0, 2)], K.wb.at[pl.ds(2, 2)]
    K.gub, K.gdb = K.wb.at[pl.ds(4, 2)], K.wb.at[pl.ds(6, 2)]
    core = lax.axis_index("stream")
    chip = lax.axis_index("dp")
    n_dp = lax.axis_size("dp")
    sib = (1 - core, chip)
    first = core == 0
    second = core == 1
    me = core * n_dp + chip
    if near:
        greet_near(core, chip, n_dp)
    else:
        greet_all(core, chip)
    wall = K.wfull if near else K.wall

    n_sems = len(gsems) // 2
    todo = []
    if not near:
        parts = [gather_steps(K.wsh, wall, gsems[p * n_sems : (p + 1) * n_sems], p) for p in range(2)]
        todo = [step for pair_ in zip(*parts) for step in pair_]

    def advance(n):
        for _ in range(n):
            if todo:
                todo.pop(0)()

    if not near:

        advance(2)

        K.vbuf[me] = K.vblk[...]
        own_slab = wall.at[pl.ds(pl.multiple_of(me * SLAB, 8), SLAB)]
        keep = K.upb.at[0, pl.ds(0, SLAB)]
        kin = pltpu.make_async_copy(K.wsh, keep, K.lsem.at[1])
        kout = pltpu.make_async_copy(keep, own_slab, K.lsem.at[2])
        kin.start()

    last_rows = K.rows.at[pl.ds(ROWS // 2, ROWS // 2)]
    pix_go = remote(last_rows, K.raw, K.gsem.at[0, 4], K.gsem.at[1, 4], (1, chip))
    pack_go = remote(
        K.rows.at[:, pl.ds(0, HALF)], K.packed, K.gsem.at[0, 4], K.gsem.at[1, 4], (0, chip)
    )
    pix_own = pltpu.make_async_copy(K.rows.at[pl.ds(0, ROWS // 2)], K.raw, K.lsem.at[0])
    pack_own = pltpu.make_async_copy(K.rows.at[:, pl.ds(HALF, HALF)], K.packed, K.lsem.at[0])

    @pl.when(first)
    def _():
        pix_go.start()
        pix_own.start()

    @pl.when(second)
    def _():
        pack_go.start()
        pack_own.start()

    if not near:

        def vsend(k, carry):
            peer = (me + k) % 32
            remote(K.vblk, K.vbuf.at[me], K.vsem.at[0], K.vsem.at[1], (peer // 16, peer % 16)).start()
            return carry

        lax.fori_loop(1, 32, vsend, 0)

    def pair(t):
        return pl.ds(CAP * t, CAP)

    def rc(src, dst, k, i, dev):
        return remote(src, dst, K.psem.at[0, k, i], K.psem.at[1, k, i], dev)

    down = [(core, (chip + n_dp - t - 1) % n_dp) for t in range(SPAN)]
    up = [(core, (chip + t + 1) % n_dp) for t in range(SPAN)]
    pin = [rc(K.pmsg.at[pair(t)], K.arp.at[pair(t)], 0, t, down[t]) for t in range(SPAN)]
    cin = [rc(K.cmsg.at[pair(t)], K.arc.at[pair(t)], 1, t, down[t]) for t in range(SPAN)]

    if not near:
        kin.wait()
        kout.start()

    @pl.when(first)
    def _():
        pack_go.wait_recv()
        pix_own.wait()

    @pl.when(second)
    def _():
        pix_go.wait_recv()
        pack_own.wait()

    def prefix_slots():
        target = slot_rows(K.plen, 0)
        pick = lax.broadcasted_iota(jnp.int32, (RSLOT * PMAX, ROWS), 1) == target
        rows = nn(pick.astype(F32).astype(BF), K.packed[...]).astype(BF)
        for s in range(RSLOT):
            K.pmsg[s, 0:PMAX, :] = rows[PMAX * s : PMAX * (s + 1), :]
            size = jnp.full((MSG - PMAX, HALF), K.plen[s], jnp.int32)
            K.pmsg[s, PMAX:MSG, :] = size.astype(F32).astype(BF)

    place_row = lax.broadcasted_iota(jnp.int32, (PMAX, 1), 0)
    zero = jnp.zeros((), BF)

    def cot_slot(s, none):
        size = K.plen[s]
        K.cmsg[s, 0:PMAX, :] = jnp.where(place_row < size, K.cot[s, NP:SEQ, :], zero)
        K.cmsg[s, PMAX : PMAX + NP, :] = jnp.where(
            jnp.full((NP, 1), size, jnp.int32) > 0, K.cot[s, 0:NP, :], zero
        )
        K.cmsg[s, PMAX + NP : R, :] = jnp.zeros((NPAD - NP, HALF), BF)
        return none

    prefix_slots()
    for t in ISSUE:
        pin[t].start()
    advance(4)
    for s in range(0, RSLOT, 2):
        lax.fori_loop(s, s + 2, cot_slot, 0)
        advance(2)
    for i in range(OWN):
        K.pix[i, 0:NP, :] = K.raw[NP * i : NP * (i + 1), :]
        K.pix[i, NP:NPAD, :] = jnp.zeros((NPAD - NP, D), BF)
    advance(2 * CIN_AT - 14)
    for t in ISSUE:
        cin[t].start()
    advance(99)
    if not near:
        for p in range(2):
            rows = (CUT, SLAB - CUT)[p] * 16
            piece = wall.at[pl.ds(0, rows)]
            pltpu.make_async_copy(piece, piece, gsems[p * n_sems + n_sems - 1]).wait()
        pltpu.make_async_copy(K.vbuf.at[pl.ds(0, 31)], K.vbuf.at[pl.ds(0, 31)], K.vsem.at[1]).wait()
    vec = jnp.zeros((VEC, D), F32)
    lane_d = lax.broadcasted_iota(jnp.int32, (1, D), 1)
    n_dev = 2 * n_dp
    width = D // n_dev
    if near:
        K.vec[...] = K.vblk[...].astype(F32)
    else:

        def spread(k, total):
            block = jnp.concatenate([K.vbuf[k].astype(F32), jnp.zeros((VEC, D - 128), F32)], axis=1)
            block = jnp.where(lane_d < width, block, 0.0)
            return total + pltpu.roll(block, k * width, 1)

        K.vec[...] = lax.fori_loop(0, n_dev, spread, vec)
    for j in range(4):
        K.bias[:, j * D : (j + 1) * D] = K.vec[5 + j : 6 + j, :]
    def load(dst, lo, n, sem):
        return pltpu.make_async_copy(wall.at[pl.ds(lo, n)], dst, sem)

    ls = load(K.stem, 0, PIX, K.wsem.at[0])
    lq = load(K.qkvw, PIX, 3 * D, K.wsem.at[1])
    lo_ = load(K.outw, PIX + 3 * D, D, K.wsem.at[2])
    if not near:
        kout.wait()
    ls.start()
    lq.start()
    lo_.start()

    def chunk(c, slot):
        at = pl.multiple_of(c * CH, 16)
        return (
            pltpu.make_async_copy(wall.at[pl.ds(UP + at, CH)], K.upb.at[slot], K.csem.at[0, slot]),
            pltpu.make_async_copy(wall.at[pl.ds(DOWN + at, CH)], K.downb.at[slot], K.csem.at[1, slot]),
        )

    def mine(k):
        return K.dest[OWN * core + k]

    def image_of(slot):
        found = jnp.int32(IMG_DEV)
        for j in range(IMG_DEV):
            found = jnp.where(K.dest[j] == slot, j, found)
        return found

    def theirs(k):
        return K.dest[OWN * (1 - core) + k]

    own_half = pl.ds(pl.multiple_of(core * HALF, 128), HALF)
    other_half = pl.ds(pl.multiple_of((1 - core) * HALF, 128), HALF)

    def swap(src, dst, k):
        return remote(src, dst, K.gsem.at[0, k], K.gsem.at[1, k], sib)

    pswap = swap(K.gvp, K.gtp, 0)
    cswap = swap(K.gvc, K.gtc, 1)
    for cp in pin:
        cp.wait_recv()
    for k in range(OWN):
        K.gvp[k] = K.arp[theirs(k)]
    lens = []
    for k in range(OWN):
        K.x[R * k : R * k + PMAX, own_half] = K.arp[mine(k), 0:PMAX, :]
        lens.append(K.arp[mine(k), PMAX:MSG, :].astype(F32)[0:1, 0:1])
    pswap.start()
    ls.wait()
    for i in range(OWN):
        K.x[R * i + PMAX : R * (i + 1), :] = nn(K.pix[i], K.stem[...]).astype(BF)
    pswap.wait_recv()
    for k in range(OWN):
        K.x[R * k : R * k + PMAX, other_half] = K.gtp[k, 0:PMAX, :]

    def norm1(rows):
        xhat, _ = norm_parts(K.x[rows, :].astype(F32))
        K.nrm[rows, :] = (xhat * K.vec[0:1, :] + K.vec[1:2, :]).astype(BF)

    rows_loop(norm1)
    lq.wait()
    for k in range(3):
        K.qkv[:, k * D : (k + 1) * D] = nt(K.nrm[...], K.qkvw[k * D : (k + 1) * D, :]).astype(BF)
    lane = lax.broadcasted_iota(jnp.int32, (1, 128), 1)
    low_half = lane < HD
    key = lax.broadcasted_iota(jnp.int32, (1, R), 1)
    scale = HD**-0.5

    def heads(i, p):
        ln = jnp.where(i == 0, lens[0], lens[1])
        ok = (key.astype(F32) < ln) | ((key >= PMAX) & (key < PMAX + NP))
        rows = pl.ds(pl.multiple_of(i * R, 16), R)

        def part(k):
            return K.qkv[rows, pl.ds(pl.multiple_of(k * D + p * 128, 128), 128)]

        return rows, ok, part(0), part(1), part(2)

    def halves(v):
        return jnp.where(low_half, v, zero), jnp.where(low_half, zero, v)

    def attend(n, c):
        i, p = n // 6, n % 6
        rows, ok, q, k, v = heads(i, p)
        outs = []
        for h, qh in enumerate(halves(q)):
            s = jnp.where(ok, nt(qh, k) * scale, MASKED)
            e = jnp.exp(s - jnp.max(s, axis=-1, keepdims=True))
            a = (e * (1.0 / jnp.sum(e, axis=-1, keepdims=True))).astype(BF)
            K.prob[2 * n + h] = a
            outs.append(nn(a, v))
        here = pl.ds(pl.multiple_of(p * 128, 128), 128)
        K.ctx[rows, here] = jnp.where(low_half, outs[0], outs[1]).astype(BF)
        return c

    lax.fori_loop(0, OWN * 6, attend, 0, unroll=3)
    lo_.wait()
    K.res[...] = nt(K.ctx[...], K.outw[...])

    def norm2(rows):
        r = K.res[rows, :] + K.x[rows, :].astype(F32)
        K.res[rows, :] = r
        xhat, _ = norm_parts(r)
        K.mlp[rows, :] = (xhat * K.vec[2:3, :] + K.vec[3:4, :]).astype(BF)
        K.big[rows, :] = r + K.vec[4:5, :]

    rows_loop(norm2)
    count = FF // CH

    def fetch(c, slot):
        for cp in chunk(c, slot):
            cp.wait()

        @pl.when(c + 1 < count)
        def _():
            for cp in chunk(c + 1, 1 - slot):
                cp.start()

    def ffn(c, carry):
        slot = lax.rem(c, 2)
        fetch(c, slot)
        cols = pl.ds(pl.multiple_of(c * CH, 128), CH)
        K.f1[...] = nt(K.mlp[...], K.upb[slot])
        b = K.bias[:, cols]

        def act(i, none):
            rows = pl.ds(pl.multiple_of(i * LNB, 16), LNB)
            h, dh = gelu_both(K.f1[rows, :] + b)
            K.hid[rows, cols] = h.astype(BF)
            K.slope[rows, cols] = dh.astype(BF)
            return none

        lax.fori_loop(0, M // LNB, act, 0, unroll=True)
        K.big[...] += nn(K.hid[:, cols], K.downb[slot])
        return carry

    for cp in chunk(0, 0):
        cp.start()
    lax.fori_loop(0, count, ffn, 0)
    for cp in chunk(0, 0):
        cp.start()
    for k in range(OWN):
        K.gvo[k] = K.big[R * k : R * (k + 1), other_half].astype(BF)
    for k in range(OWN):
        K.img[OWN * core + k] = K.big[R * k : R * (k + 1), own_half].astype(BF)
    K.img[IMG_DEV] = jnp.zeros((R, HALF), BF)
    oswap = swap(K.gvo, K.img.at[pl.ds(OWN * core, OWN)], 2)
    oswap.start()
    K.big[...] = jnp.zeros((M, D), F32)
    for cp in cin:
        cp.wait_recv()
    for k in range(OWN):
        K.gvc[k] = K.arc[theirs(k)]
    for k in range(OWN):
        K.og[R * k : R * (k + 1), own_half] = K.arc[mine(k)]
    cswap.start()
    oswap.wait()
    for cp in cin:
        cp.wait_send()
    for k in range(RSLOT):
        K.cmsg[k] = K.img[image_of(k)]
    cswap.wait_recv()
    for k in range(OWN):
        K.og[R * k : R * (k + 1), other_half] = K.gtc[k]
    eout = [rc(K.cmsg.at[pair(t)], K.encm.at[pair(t)], 2, t, up[t]) for t in range(SPAN)]
    for t in ISSUE:
        eout[t].start()

    def store(c, slot):
        at = pl.multiple_of(c * CH, 16)
        return (
            pltpu.make_async_copy(K.gub.at[slot], K.g.at[pl.ds(UP + at, CH)], K.osem.at[0, slot]),
            pltpu.make_async_copy(K.gdb.at[slot], K.g.at[pl.ds(DOWN + at, CH)], K.osem.at[1, slot]),
        )

    def ffn_back(c, carry):
        slot = lax.rem(c, 2)
        fetch(c, slot)

        @pl.when(c >= 2)
        def _():
            for cp in store(c - 2, slot):
                cp.wait()

        cols = pl.ds(pl.multiple_of(c * CH, 128), CH)
        K.f1[...] = nt(K.og[...], K.downb[slot])

        def act(i, tot):
            rows = pl.ds(pl.multiple_of(i * 16, 16), 16)
            dp = (K.f1[rows, :] * K.slope[rows, cols].astype(F32)).astype(BF)
            K.dpr[rows, :] = dp
            return tot + dp.astype(F32)

        tot = lax.fori_loop(0, M // 16, act, jnp.zeros((16, CH), F32), unroll=2)
        K.bg[:, cols] = jnp.sum(tot, axis=0, keepdims=True)
        K.big[...] += nn(K.dpr[...], K.upb[slot])
        K.gub[slot] = tn(K.dpr[...], K.mlp[...]).astype(BF)
        K.gdb[slot] = tn(K.hid[:, cols], K.og[...]).astype(BF)
        for cp in store(c, slot):
            cp.start()
        return carry

    lax.fori_loop(0, count, ffn_back, 0)
    for slot in range(2):
        for cp in store(count - 2 + slot, slot):
            cp.wait()
    late = []
    if not near:

        def obuf(i):
            return K.wb.at[i // 2, pl.ds(pl.multiple_of((i % 2) * PART, 16), PART)]

        begin, late, end_sum = sum_steps(1, K.g, K.r1, obuf, sum_refs, SUM_VIA)
        begin()

    def advance_sum(n=1):
        for _ in range(n):
            if late:
                late.pop(0)()

    def back2(i, c):
        rows = pl.ds(pl.multiple_of(i * LNB, 16), LNB)
        o = K.og[rows, :].astype(F32)
        d, dg, dc = norm_back(K.res[rows, :], K.big[rows, :], K.vec[2:3, :])
        d = d + o
        K.res[rows, :] = d
        K.dx[rows, :] = d.astype(BF)
        return (c[0] + dg, c[1] + dc, c[2] + jnp.sum(o, axis=0, keepdims=True))

    none = jnp.zeros((1, D), F32)
    dg2, dc2, dob = lax.fori_loop(0, M // LNB, back2, (none, none, none), unroll=True)
    K.vg[8:VEC, :] = jnp.zeros((VEC - 8, D), F32)
    K.vg[2:3, :] = dg2
    K.vg[3:4, :] = dc2
    K.vg[4:5, :] = dob
    for j in range(4):
        K.vg[5 + j : 6 + j, :] = K.bg[:, j * D : (j + 1) * D]

    advance_sum()

    def put(src, lo, n, sem):
        return pltpu.make_async_copy(src, K.g.at[pl.ds(lo, n)], sem)

    K.mlp[...] = nn(K.dx[...], K.outw[...]).astype(BF)
    advance_sum()
    K.outw[...] = tn(K.dx[...], K.ctx[...]).astype(BF)
    po = put(K.outw, PIX + 3 * D, D, K.wsem.at[2])
    po.start()

    def attend_back(n, c):
        i, p = n // 6, n % 6
        rows, ok, q, k, v = heads(i, p)
        here = pl.ds(pl.multiple_of(p * 128, 128), 128)
        dc = K.mlp[rows, here]
        dq = []
        dk = dv = None
        for h, (qh, dch) in enumerate(zip(halves(q), halves(dc))):
            a = K.prob[2 * n + h]
            af = a.astype(F32)
            t = af * nt(dch, v)
            dsc = (t - af * jnp.sum(t, axis=-1, keepdims=True)).astype(BF)
            dq.append(nn(dsc, k))
            dkh = tn(dsc, qh)
            dvh = tn(a, dch)
            dk = dkh if dk is None else dk + dkh
            dv = dvh if dv is None else dv + dvh

        def at(j):
            return pl.ds(pl.multiple_of(j * D + p * 128, 128), 128)

        K.qkv[rows, at(0)] = (jnp.where(low_half, dq[0], dq[1]) * scale).astype(BF)
        K.qkv[rows, at(1)] = (dk * scale).astype(BF)
        K.qkv[rows, at(2)] = dv.astype(BF)
        return c

    advance_sum()
    for group in range(6):
        lax.fori_loop(2 * group, 2 * group + 2, attend_back, 0)
        advance_sum()
    K.big[...] = nn(K.qkv[...], K.qkvw[...])
    advance_sum()

    def back1(i, c):
        rows = pl.ds(pl.multiple_of(i * LNB, 16), LNB)
        d, dg, dc = norm_back(K.x[rows, :].astype(F32), K.big[rows, :], K.vec[0:1, :])
        K.dx[rows, :] = (K.res[rows, :] + d).astype(BF)
        return (c[0] + dg, c[1] + dc)

    dg1, dc1 = lax.fori_loop(0, M // LNB, back1, (none, none), unroll=True)
    advance_sum()
    pswap.wait_send()
    cswap.wait_send()
    for k in range(OWN):
        K.gvp[k, 0:PMAX, :] = K.dx[R * k : R * k + PMAX, other_half]
    for k in range(OWN):
        K.pim[OWN * core + k] = K.dx[R * k : R * k + PMAX, own_half]
    K.pim[IMG_DEV] = jnp.zeros((PMAX, HALF), BF)
    dswap = swap(K.gvp.at[:, pl.ds(0, PMAX)], K.pim.at[pl.ds(OWN * core, OWN)], 3)
    dswap.start()
    K.vg[0:1, :] = dg1
    K.vg[1:2, :] = dc1

    def cut(k, c):
        K.vgb[k] = pltpu.roll(K.vg[...], lax.rem(D - k * width, D), 1)[:, 0:128]
        return c

    lax.fori_loop(0, n_dev, cut, 0)
    for k in range(3):
        K.qkvw[k * D : (k + 1) * D, :] = tn(K.qkv[:, k * D : (k + 1) * D], K.nrm[...]).astype(BF)
    pq = put(K.qkvw, PIX, 3 * D, K.wsem.at[1])
    pq.start()
    dswap.wait()
    if not near:
        advance_sum(99)
    for k in range(RSLOT):
        K.pback[k] = K.pim[image_of(k)]
    dout = [rc(K.pback.at[pair(t)], K.dprem.at[pair(t)], 3, t, up[t]) for t in range(SPAN)]
    for t in ISSUE:
        dout[t].start()
    tot = None
    for i in range(OWN):
        dp = K.dx[R * i + PMAX : R * (i + 1), :]
        K.dpix[i] = nt(dp, K.stem[...]).astype(BF)
        t = tn(K.pix[i], dp)
        tot = t if tot is None else tot + t
    K.stem[...] = tot.astype(BF)
    ps = put(K.stem, 0, PIX, K.wsem.at[0])
    ps.start()
    for cp in eout + dout:
        cp.wait()
    po.wait()
    pq.wait()
    ps.wait()
    for cp in pin:
        cp.wait_send()

    @pl.when(first)
    def _():
        pix_go.wait_send()

    @pl.when(second)
    def _():
        pack_go.wait_send()

    if not near:
        end_sum()
        for p in range(2):
            for step in gather_steps(
                K.wsh, wall, gsems[p * n_sems : (p + 1) * n_sems], p, draining=True
            ):
                step()
            rows = (CUT, SLAB - CUT)[p] * 16
            piece = wall.at[pl.ds(0, rows)]
            pltpu.make_async_copy(piece, piece, gsems[p * n_sems + n_sems - 2]).wait()
        pltpu.make_async_copy(K.vbuf.at[pl.ds(0, 31)], K.vbuf.at[pl.ds(0, 31)], K.vsem.at[0]).wait()


def whole_block(dest, plen, rows, cot, wsh, vblk, wfull, n_dev):
    near = wfull is not None
    any_ = pl.BlockSpec(memory_space=pl.ANY)
    vmem = pl.BlockSpec(memory_space=pltpu.VMEM)
    smem = pl.BlockSpec(memory_space=pltpu.SMEM)
    total = SLAB * 32 if not near else wfull.shape[0]
    if near:
        wsh = wsh[:8]
    else:
        wfull = wsh[:8]
    outs = (
        jax.ShapeDtypeStruct((OWN, NPAD, D), BF),
        jax.ShapeDtypeStruct((n_dev, VEC, 128), F32),
        jax.ShapeDtypeStruct((total, D), BF),
        jax.ShapeDtypeStruct((RSLOT, R, HALF), BF),
        jax.ShapeDtypeStruct((RSLOT, PMAX, HALF), BF),
        jax.ShapeDtypeStruct((8, D) if near else (total, D), BF),
        jax.ShapeDtypeStruct((8, D) if near else (SLAB, D), F32),
    )
    return pl.pallas_call(
        functools.partial(x_kernel, near),
        out_shape=outs,
        in_specs=[smem, smem, any_, vmem, any_, vmem, any_],
        out_specs=(vmem, vmem, any_, any_, any_, any_, vmem),
        scratch_shapes=[pltpu.VMEM(s, t) for _, s, t in X_SCRATCH]
        + [dma(s) for _, s in X_SEMS]
        + ([] if near else gather_sems() + gather_sems() + rs_scratch()),
        compiler_params=pltpu.CompilerParams(
            collective_id=3, has_side_effects=True, vmem_limit_bytes=63 * 2**20
        ),
    )(dest, plen, rows, cot, wsh, vblk, wfull)


def swapped(value):
    return lax.ppermute(value, "stream", [(0, 1), (1, 0)])


def body(
    stream_rows,
    dest,
    prefix_len,
    weights,
    momentum,
    average,
    vectors,
    vec_momentum,
    vec_average,
    cotangent,
):
    core = lax.axis_index("stream")
    first = core == 0
    n_dp = lax.axis_size("dp")
    n_dev = 2 * n_dp
    lane = vectors.shape[1]
    kernels = n_dp == 16

    rows = stream_rows[0, 0]
    half_rows = ROWS // 2
    lengths = prefix_len[0]
    slots = dest[0]
    shard = weights.astype(BF)
    if kernels:
        full = None
        block = jnp.pad(vectors.astype(BF), ((0, VEC - 9), (0, 128 - lane)))
    else:
        full = lax.all_gather(shard, ALL, axis=0, tiled=True)
        block = jnp.pad(vectors.astype(BF), ((0, VEC - 9), (0, 0)))
        block = lax.all_gather(block, ALL, axis=1, tiled=True)
    d_pixels, vec_blocks, grads, enc_back, prefix_back, _, late_grad = whole_block(
        slots, lengths, rows, cotangent[0], shard, block, full, n_dev
    )
    if kernels:
        early_grad, vec_grad, d_rows = summed(
            lengths, grads, vec_blocks, prefix_back, d_pixels
        )
        weight_grad = jnp.where(first, early_grad, late_grad)
    else:
        weight_grad = lax.psum_scatter(grads, ALL, scatter_dimension=0, tiled=True).astype(F32)
        vec_grad = lax.psum_scatter(vec_blocks, ALL, scatter_dimension=0, tiled=True)[0]
    vec_grad = vec_grad[:9, :lane]

    columns = jnp.arange(SEQ, dtype=jnp.int32)
    row_ok = (columns[None, :] < NP + lengths[:, None]) & (lengths[:, None] > 0)
    enc_out = jnp.concatenate([enc_back[:, PMAX : PMAX + NP], enc_back[:, :PMAX]], axis=1)
    enc_out = jnp.where(row_ok[:, :, None], enc_out, jnp.zeros((), BF))[None]

    if not kernels:
        offsets = jnp.cumsum(lengths) - lengths
        places = jnp.arange(PMAX, dtype=jnp.int32)
        row_index = offsets[:, None] + places[None, :]
        keep_mask = places[None, :] < lengths[:, None]
        rows_at = jnp.arange(ROWS, dtype=jnp.int32)
        pick = (
            (row_index.reshape(-1)[:, None] == rows_at[None, :]) & keep_mask.reshape(-1)[:, None]
        ).astype(BF)
        d_packed = tn(pick, prefix_back.reshape(RSLOT * PMAX, HALF)).astype(BF)
        d_pixels = d_pixels[:, :NP].reshape(half_rows, D)
        give = jnp.where(
            first, jnp.concatenate([d_packed[:half_rows], d_packed[half_rows:]], axis=1), d_pixels
        )
        got = swapped(give)
        d_image_rows = jnp.concatenate([d_pixels, got])
        d_text_rows = jnp.concatenate(
            [jnp.concatenate([got[:, :HALF], got[:, HALF:]], axis=0), d_packed], axis=1
        )
        d_rows = jnp.where(first, d_image_rows, d_text_rows)
    d_rows = d_rows.astype(F32)[None, None]

    rate = 0.5 * (D * IMG_DEV * n_dp * NP) ** (-0.5)
    new_momentum = MOMENT * momentum + weight_grad
    new_weights = weights - rate * (weight_grad + MOMENT * new_momentum)
    new_average = DECAY * average + (1.0 - DECAY) * new_weights
    vec_new_momentum = MOMENT * vec_momentum + vec_grad
    vec_new = vectors - rate * (vec_grad + MOMENT * vec_new_momentum)
    vec_new_average = DECAY * vec_average + (1.0 - DECAY) * vec_new
    return (
        enc_out,
        d_rows,
        weight_grad,
        new_momentum,
        new_average,
        new_weights,
        new_weights.astype(BF),
        vec_grad,
        vec_new_momentum,
        vec_new_average,
        vec_new,
        vec_new.astype(BF),
    )


def solution(mesh):
    both = P(ALL, None)
    lanes = P(None, ALL)
    in_specs = (
        P("stream", "dp", None, None),
        P("dp", None),
        P("dp", None),
        both,
        both,
        both,
        lanes,
        lanes,
        lanes,
        P("dp", None, None, "stream"),
    )
    out_specs = (
        P("dp", None, None, "stream"),
        P("stream", "dp", None, None),
        both,
        both,
        both,
        both,
        both,
        lanes,
        lanes,
        lanes,
        lanes,
        lanes,
    )
    return jax.shard_map(body, mesh=mesh, in_specs=in_specs, out_specs=out_specs, check_vma=False)
```

```python
import functools
from types import SimpleNamespace

import jax
import jax.numpy as jnp
from jax import lax
from jax.experimental import pallas as pl
from jax.experimental.pallas import tpu as pltpu
from jax.sharding import PartitionSpec as P

D = 768
HEADS = 12
HD = 64
FF = 3072
PIX = 768
NP = 196
PMAX = 64
SPAN = 4
IMG_DEV = 4
CAP = 2
RSLOT = 8
SEQ = 260
ROWS = 784
HALF = D // 2
OWN = IMG_DEV // 2
SLAB = 312
CUT = 160
NZ = 4

EPSILON = 1e-06
MASKED = -1e30
MOMENT = 0.5
DECAY = 0.5
BF = jnp.bfloat16
F32 = jnp.float32
ALL = ("stream", "dp")
MESH = pl.DeviceIdType.MESH


NPAD = 208
R = PMAX + NPAD
M = OWN * R
CH = 512
LNB = 32
MSG = PMAX + 16
VEC = 16
UP = PIX + 4 * D
DOWN = UP + FF
VIA_Z = (1, 2)
CIN_AT = 12
ISSUE = (1, 3, 0, 2)
SUM_VIA = (1, 2)
dma = pltpu.SemaphoreType.DMA


def nn(a, b):
    return lax.dot_general(a, b, (((1,), (0,)), ((), ())), preferred_element_type=F32)


def nt(a, b):
    return lax.dot_general(a, b, (((1,), (1,)), ((), ())), preferred_element_type=F32)


def tn(a, b):
    return lax.dot_general(a, b, (((0,), (0,)), ((), ())), preferred_element_type=F32)


def erf(v):
    v = jnp.clip(v, -3.832506856900711, 3.832506856900711)
    s = v * v
    top = 0.00022905065861350646
    for c in (0.0034082910107109506, 0.050955695062380861, 0.18520832239976145, 1.128379143519084):
        top = top * s + c
    low = -1.1791602954361697e-7
    for c in (
        0.000023547966471313185,
        0.0010179625278914885,
        0.014070470171167667,
        0.11098505178285362,
        0.49746925110067538,
        1.0,
    ):
        low = low * s + c
    return v * top / low


def gelu_both(v):
    phi = 0.5 * (1.0 + erf(v * 0.7071067811865476))
    return v * phi, phi + v * (0.3989422804014327 * jnp.exp(-0.5 * v * v))


def rows_loop(f, block=LNB, total=M):
    def run(i, c):
        f(pl.ds(pl.multiple_of(i * block, 16), block))
        return c

    lax.fori_loop(0, total // block, run, 0, unroll=True)


def norm_parts(v):
    off = v - jnp.mean(v, axis=-1, keepdims=True)
    inv = lax.rsqrt(jnp.mean(off * off, axis=-1, keepdims=True) + EPSILON)
    return off * inv, inv


def norm_back(v, dn, gain):
    xhat, inv = norm_parts(v)
    dx = dn * gain
    low = jnp.mean(dx, axis=-1, keepdims=True)
    slope = jnp.mean(dx * xhat, axis=-1, keepdims=True)
    return (
        (dx - low - xhat * slope) * inv,
        jnp.sum(dn * xhat, axis=0, keepdims=True),
        jnp.sum(dn, axis=0, keepdims=True),
    )


def slot_rows(plen, dim):
    shape = (RSLOT * PMAX, 1) if dim == 0 else (1, RSLOT * PMAX)
    at = lax.broadcasted_iota(jnp.int32, shape, dim)
    target = jnp.full(shape, -1, jnp.int32)
    offset = jnp.int32(0)
    for s in range(RSLOT):
        i = at - PMAX * s
        target = jnp.where((i >= 0) & (i < plen[s]), i + offset, target)
        offset = offset + plen[s]
    return target


def remote(src, dst, send, recv, dev):
    return pltpu.make_async_remote_copy(
        src_ref=src, dst_ref=dst, send_sem=send, recv_sem=recv, device_id=dev, device_id_type=MESH
    )


def place():
    core = lax.axis_index("stream")
    chip = lax.axis_index("dp")
    return core, chip, chip % 2, (chip // 2) % 2, chip // 4


def greet_all(core, chip):
    barrier = pltpu.get_barrier_semaphore()
    me = core * 16 + chip

    def one(k, carry):
        peer = (me + k) % 32
        pl.semaphore_signal(barrier, inc=1, device_id=(peer // 16, peer % 16), device_id_type=MESH)
        return carry

    lax.fori_loop(1, 32, one, 0)
    pl.semaphore_wait(barrier, 31)


def greet_near(core, chip, n_dp):
    barrier = pltpu.get_barrier_semaphore()
    for t in range(1, SPAN + 1):
        for peer in ((chip + t) % n_dp, (chip + n_dp - t) % n_dp):
            pl.semaphore_signal(barrier, inc=1, device_id=(core, peer), device_id_type=MESH)
    pl.semaphore_signal(barrier, inc=1, device_id=(1 - core, chip), device_id_type=MESH)
    pl.semaphore_wait(barrier, 2 * SPAN + 1)


def gather_sems():
    four = dma((4,))
    return [dma((2, 4)), four, dma((2, 4)), four] + [four] * 8 + [dma, dma]


def gather_steps(w_ref, out, sems, part, draining=False):
    core, chip, x, y, z = place()
    zs, zr, ds, dr, xs, xr, ys, yr, as_, ar, bs, br, ss, sr = sems
    base = core * 16
    me = base + chip
    flat = chip % 4
    xn = chip + 1 - 2 * x
    yn = chip + 2 - 4 * y
    start, size = ((0, CUT), (CUT, SLAB - CUT))[part]
    top = pl.ds(0, 80)
    bottom = pl.ds(80, size - 80)
    sib = (1 - core, chip)
    w_ref = w_ref.at[pl.ds(start, size)]

    def slab_of(slab, rows=None):
        whole = out.at[pl.ds(pl.multiple_of(slab * SLAB + start, 8), size)]
        return whole if rows is None else whole.at[rows]

    def rc(src, slab, ssem, rsem, dev, rows=None):
        return remote(src, slab_of(slab, rows), ssem, rsem, dev)

    def go(cond, make):
        def act():
            if draining:
                make().wait_send()
            else:
                make().start()

        if cond is None:
            act()
        else:
            pl.when(cond)(act)

    def to_sib(src, slab):
        if not draining:
            rc(src, slab, ss, sr, sib).start()

    def arrive(copy):
        if not draining:
            copy().wait_recv()

    def at(t, sign):
        zz = z + sign * t
        return zz, (zz >= 0) & (zz < NZ)

    def own():
        go(None, lambda: rc(w_ref, me, xs.at[z], xr.at[z], (core, xn)))
        go(None, lambda: rc(w_ref, me, ys.at[z], yr.at[z], (core, yn)))
        for k, s in enumerate((1, -1)):
            go(
                (z + s >= 0) & (z + s < NZ),
                lambda k=k, s=s: rc(w_ref, me, zs.at[k, z], zr.at[z], (core, chip + 4 * s)),
            )
        to_sib(w_ref, me)

    def column(t, sign):
        zz, here = at(t, sign)
        slab = base + zz * 4 + flat
        k = 0 if sign < 0 else 1

        @pl.when(here)
        def _():
            arrive(lambda: rc(w_ref, slab, ss, zr.at[zz], sib))

        src = slab_of(slab)
        go(
            here & (z - sign >= 0) & (z - sign < NZ),
            lambda: rc(src, slab, zs.at[k, zz], zr.at[zz], (core, chip - 4 * sign)),
        )
        go(here, lambda: rc(src, slab, xs.at[zz], xr.at[zz], (core, xn)))
        go(here, lambda: rc(src, slab, ys.at[zz], yr.at[zz], (core, yn)))

        @pl.when(here)
        def _():
            to_sib(src, slab)

    def plane(t, sign):
        zz, here = at(t, sign)
        xslab = base + zz * 4 + flat + 1 - 2 * x
        yslab = base + zz * 4 + flat + 2 - 4 * y

        @pl.when(here)
        def _():
            arrive(lambda: rc(w_ref, xslab, ss, xr.at[zz], sib))

        if t not in VIA_Z:
            go(
                here,
                lambda: rc(slab_of(xslab, top), xslab, as_.at[zz], ar.at[zz], (core, yn), top),
            )

        @pl.when(here)
        def _():
            arrive(lambda: rc(w_ref, yslab, ss, yr.at[zz], sib))

        if t not in VIA_Z:
            go(
                here,
                lambda: rc(slab_of(yslab, bottom), yslab, bs.at[zz], br.at[zz], (core, xn), bottom),
            )

        @pl.when(here)
        def _():
            to_sib(slab_of(xslab), xslab)
            to_sib(slab_of(yslab), yslab)

    def diag(t, sign):
        zz, here = at(t, sign)
        slab = base + zz * 4 + 3 - flat
        src = slab_of(slab)
        if t in VIA_Z:

            @pl.when(here)
            def _():
                arrive(lambda: rc(w_ref, slab, ss, dr.at[zz], sib))
        else:

            @pl.when(here)
            def _():
                arrive(lambda: rc(slab_of(slab, top), slab, ss, ar.at[zz], sib, top))
                arrive(lambda: rc(slab_of(slab, bottom), slab, ss, br.at[zz], sib, bottom))

        if t == 0 and 1 in VIA_Z:
            for k, s in enumerate((1, -1)):
                go(
                    (z + s >= 0) & (z + s < NZ),
                    lambda k=k, s=s: rc(src, slab, ds.at[k, zz], dr.at[zz], (core, chip + 4 * s)),
                )
        if t >= 1 and t + 1 in VIA_Z:
            k = 0 if sign < 0 else 1
            go(
                here & (z - sign >= 0) & (z - sign < NZ),
                lambda: rc(src, slab, ds.at[k, zz], dr.at[zz], (core, chip - 4 * sign)),
            )

        @pl.when(here)
        def _():
            to_sib(src, slab)

    def both(f, t):
        def run():
            f(t, 1)
            if t:
                f(t, -1)

        return run

    return [
        own,
        both(column, 1),
        both(plane, 0),
        both(column, 2),
        both(diag, 0),
        both(plane, 1),
        both(column, 3),
        both(diag, 1),
        both(plane, 2),
        both(plane, 3),
        both(diag, 2),
        both(diag, 3),
    ]


PART = 160
SHIFT = SLAB - PART
ADD = 16
ADD_UNROLL = 1
WAYS_AT = 11
RS_BUFS = (
    ("sbuf", (16, PART, D), BF),
    ("xb", (4, PART, D), BF),
    ("yb", (4, PART, D), BF),
    ("dzb", (2, 2, PART, D), BF),
    ("czb", (2, 3, PART, D), BF),
    ("ab", (4, PART // 2, D), BF),
    ("bb", (4, PART // 2, D), BF),
    ("fin", (PART, D), F32),
)
RS_SEMS = (
    ("load", (16,)),
    ("ssend", ()),
    ("srecv", (16,)),
    ("xs", (4,)),
    ("xr", (4,)),
    ("ys", (4,)),
    ("yr", (4,)),
    ("dzs", (2, 2)),
    ("dzr", (2, 2)),
    ("czs", (2, 3)),
    ("czr", (2, 3)),
    ("as_", (4,)),
    ("ar", (4,)),
    ("bs", (4,)),
    ("br", (4,)),
    ("fsem", (2,)),
)


def rs_scratch():
    return [pltpu.VMEM(s, t) for _, s, t in RS_BUFS] + [dma(s) for _, s in RS_SEMS]


def add_rows(dst, sources, lo, size):
    def piece(i, c):
        tot = None
        for ref, at in sources:
            v = ref[pl.ds(pl.multiple_of(at + i * ADD, 16), ADD), :].astype(F32)
            tot = v if tot is None else tot + v
        dst[pl.ds(pl.multiple_of(lo + i * ADD, 16), ADD), :] = tot.astype(dst.dtype)
        return c

    lax.fori_loop(0, size // ADD, piece, 0, unroll=ADD_UNROLL)


class Sends:
    def __init__(self):
        self.kept = []

    def go(self, cond, make):
        if cond is None:
            make().start()
        else:

            @pl.when(cond)
            def _():
                make().start()

        self.kept.append((cond, make))

    def drain(self):
        for cond, make in self.kept:
            if cond is None:
                make().wait_send()
            else:

                @pl.when(cond)
                def _(make=make):
                    make().wait_send()


def sum_steps(half, g, result, obuf, refs, via):
    B = SimpleNamespace(**dict(zip([n for n, _, _ in RS_BUFS] + [n for n, _ in RS_SEMS], refs)))
    core, chip, x, y, z = place()
    flat = chip % 4
    xn = chip + 1 - 2 * x
    yn = chip + 2 - 4 * y
    sib = (1 - core, chip)
    mid = PART // 2
    top = pl.ds(0, mid)
    bottom = pl.ds(mid, mid)
    fd, fx, fy = 3 - flat, flat + 1 - 2 * x, flat + 2 - 4 * y
    sends = Sends()

    def rows_of(i, part):
        return g.at[pl.ds(pl.multiple_of((16 * half + i) * SLAB + part * SHIFT, 8), PART)]

    def each(t, f):
        if t == 0:
            f(z, 0, None)
            return
        for sign in (1, -1):
            zz = z + sign * t
            f(zz, sign, (zz >= 0) & (zz < NZ))

    def when(cond, f):
        if cond is None:
            f()
        else:
            pl.when(cond)(f)

    order = [(fd, 3), (fd, 2), (fx, 3), (fy, 3), (fx, 2), (fy, 2), (fd, 1), (flat, 3)]
    order += [(fx, 1), (fy, 1), (fd, 0), (flat, 2), (fx, 0), (fy, 0), (flat, 1), (flat, 0)]

    def start():
        for f, t in order:

            def begin(zz, sign, here, f=f):
                i = zz * 4 + f

                def go():
                    remote(rows_of(i, 1 - core), B.sbuf.at[i], B.ssend, B.srecv.at[i], sib).start()
                    pltpu.make_async_copy(rows_of(i, core), obuf(i), B.load.at[i]).start()

                when(here, go)

            each(t, begin)

    def ready(i):
        pltpu.make_async_copy(rows_of(i, core), obuf(i), B.load.at[i]).wait()
        remote(rows_of(i, core), B.sbuf.at[i], B.ssend, B.srecv.at[i], sib).wait_recv()

    def landed(dst, send, recv):
        remote(dst, dst, send, recv, sib).wait_recv()

    def up_down(sign):
        return 0 if sign > 0 else 1

    def inside(zz):
        return (zz >= 0) & (zz < NZ)

    def diag(t):
        def f(zz, sign, here):
            i = zz * 4 + fd

            def work():
                ready(i)
                src = [(obuf(i), 0), (B.sbuf.at[i], 0)]
                if t in via and t + 1 in via:
                    k = up_down(sign)
                    far = inside(z - sign)

                    @pl.when(far)
                    def _():
                        landed(B.dzb.at[k, t], B.dzs.at[k, t], B.dzr.at[k, t])
                        add_rows(obuf(i), src + [(B.dzb.at[k, t], 0)], 0, PART)

                    @pl.when(jnp.logical_not(far))
                    def _():
                        add_rows(obuf(i), src, 0, PART)

                elif t == 0 and 1 in via:
                    add_rows(obuf(i), src, 0, PART)
                    for k, s in enumerate((1, -1)):

                        @pl.when(inside(z - s))
                        def _(k=k):
                            landed(B.dzb.at[k, 0], B.dzs.at[k, 0], B.dzr.at[k, 0])
                            add_rows(obuf(i), [(obuf(i), 0), (B.dzb.at[k, 0], 0)], 0, PART)

                else:
                    add_rows(obuf(i), src, 0, PART)

            when(here, work)
            if t in via:
                k = up_down(sign)
                sends.go(
                    here,
                    lambda: remote(
                        obuf(i),
                        B.dzb.at[k, t - 1],
                        B.dzs.at[k, t - 1],
                        B.dzr.at[k, t - 1],
                        (core, chip + 4 * sign),
                    ),
                )
            else:
                sends.go(
                    here,
                    lambda: remote(
                        obuf(i).at[top], B.ab.at[zz], B.as_.at[zz], B.ar.at[zz], (core, yn)
                    ),
                )
                sends.go(
                    here,
                    lambda: remote(
                        obuf(i).at[bottom], B.bb.at[zz], B.bs.at[zz], B.br.at[zz], (core, xn)
                    ),
                )

        return lambda: each(t, f)

    def plane(t):
        def f(zz, sign, here):
            ix, iy = zz * 4 + fx, zz * 4 + fy

            def work_x():
                ready(ix)
                src = [(obuf(ix), 0), (B.sbuf.at[ix], 0)]
                if t in via:
                    add_rows(obuf(ix), src, 0, PART)
                else:
                    add_rows(obuf(ix), [(r, mid) for r, _ in src], mid, mid)
                    landed(B.ab.at[zz], B.as_.at[zz], B.ar.at[zz])
                    add_rows(obuf(ix), src + [(B.ab.at[zz], 0)], 0, mid)

            def work_y():
                ready(iy)
                src = [(obuf(iy), 0), (B.sbuf.at[iy], 0)]
                if t in via:
                    add_rows(obuf(iy), src, 0, PART)
                else:
                    add_rows(obuf(iy), src, 0, mid)
                    landed(B.bb.at[zz], B.bs.at[zz], B.br.at[zz])
                    add_rows(obuf(iy), [(r, mid) for r, _ in src] + [(B.bb.at[zz], 0)], mid, mid)

            when(here, work_x)
            sends.go(
                here, lambda: remote(obuf(ix), B.xb.at[zz], B.xs.at[zz], B.xr.at[zz], (core, xn))
            )
            when(here, work_y)
            sends.go(
                here, lambda: remote(obuf(iy), B.yb.at[zz], B.ys.at[zz], B.yr.at[zz], (core, yn))
            )

        return lambda: each(t, f)

    def column(t):
        def f(zz, sign, here):
            i = zz * 4 + flat
            k = up_down(sign)

            def work():
                ready(i)
                landed(B.xb.at[zz], B.xs.at[zz], B.xr.at[zz])
                landed(B.yb.at[zz], B.ys.at[zz], B.yr.at[zz])
                src = [(obuf(i), 0), (B.sbuf.at[i], 0), (B.xb.at[zz], 0), (B.yb.at[zz], 0)]
                if t == 3:
                    add_rows(obuf(i), src, 0, PART)
                    return
                far = inside(z - sign)

                @pl.when(far)
                def _():
                    landed(B.czb.at[k, t], B.czs.at[k, t], B.czr.at[k, t])
                    add_rows(obuf(i), src + [(B.czb.at[k, t], 0)], 0, PART)

                @pl.when(jnp.logical_not(far))
                def _():
                    add_rows(obuf(i), src, 0, PART)

            when(here, work)
            sends.go(
                here,
                lambda: remote(
                    obuf(i),
                    B.czb.at[k, t - 1],
                    B.czs.at[k, t - 1],
                    B.czr.at[k, t - 1],
                    (core, chip + 4 * sign),
                ),
            )

        return lambda: each(t, f)

    if half == 1:
        part = remote(
            B.fin.at[pl.ds(0, SHIFT)],
            result.at[pl.ds(0, SHIFT)],
            B.fsem.at[0],
            B.fsem.at[1],
            (1, chip),
        )
    else:
        part = remote(
            B.fin.at[pl.ds(PART - SHIFT, SHIFT)],
            result.at[pl.ds(PART, SHIFT)],
            B.fsem.at[0],
            B.fsem.at[1],
            (0, chip),
        )

    def final():
        i = z * 4 + flat
        ready(i)
        landed(B.xb.at[z], B.xs.at[z], B.xr.at[z])
        landed(B.yb.at[z], B.ys.at[z], B.yr.at[z])
        src = [(obuf(i), 0), (B.sbuf.at[i], 0), (B.xb.at[z], 0), (B.yb.at[z], 0)]
        add_rows(B.fin, src, 0, PART)
        for k, s in enumerate((1, -1)):

            @pl.when(inside(z - s))
            def _(k=k):
                landed(B.czb.at[k, 0], B.czs.at[k, 0], B.czr.at[k, 0])
                add_rows(B.fin, [(B.fin, 0), (B.czb.at[k, 0], 0)], 0, PART)

        @pl.when(core == half)
        def _():
            result[pl.ds(half * SHIFT, PART), :] = B.fin[...]

        @pl.when(core != half)
        def _():
            part.start()

    def drain():
        pltpu.make_async_copy(B.sbuf, B.sbuf, B.ssend).wait()
        sends.drain()

        @pl.when(core == half)
        def _():
            part.wait_recv()

        @pl.when(core != half)
        def _():
            part.wait_send()

    steps = [diag(3), diag(2), plane(3), plane(2), diag(1), column(3), plane(1), diag(0)]
    steps += [column(2), plane(0), column(1), final]
    return start, steps, drain


def last_sum(
    plen,
    g,
    vg,
    sent,
    dpix,
    out,
    vout,
    drows,
    obuf,
    vbuf,
    half_rows,
    tall,
    back,
    vs,
    vr,
    vl,
    es,
    bs,
    *refs,
):
    core, chip = lax.axis_index("stream"), lax.axis_index("dp")
    me = core * 16 + chip
    first = core == 0
    greet_all(core, chip)
    start, steps, drain = sum_steps(0, g, out, lambda i: obuf.at[i], refs, (1, 2))
    start()

    def vsend(k, carry):
        peer = (me + k) % 32
        remote(vg.at[peer], vbuf.at[me], vs, vr, (peer // 16, peer % 16)).start()
        return carry

    ways = []
    for t in range(SPAN):
        two = pl.ds(CAP * t, CAP)
        to = (core, (chip + t + 1) % 16)
        ways.append(remote(sent.at[two], back.at[two], bs.at[0, t], bs.at[1, t], to))
    lax.fori_loop(1, 32, vsend, 0)
    vcp = pltpu.make_async_copy(vg.at[me], vbuf.at[me], vl)
    vcp.start()
    for step in steps[:7]:
        step()
    for t in ISSUE:
        ways[t].start()
    for step in steps[7:WAYS_AT]:
        step()
    for way in ways:
        way.wait()

    pick = lax.broadcasted_iota(jnp.int32, (ROWS, RSLOT * PMAX), 0) == slot_rows(plen, 1)
    total = nn(pick.astype(F32).astype(BF), back[...].reshape(RSLOT * PMAX, HALF))
    to_text = remote(tall.at[0], tall.at[1], es.at[0], es.at[1], (1, chip))
    to_image = remote(half_rows.at[0], half_rows.at[1], es.at[0], es.at[1], (0, chip))

    @pl.when(first)
    def _():
        tall[0] = total.astype(BF)
        to_text.start()
        for i in range(OWN):
            drows[NP * i : NP * (i + 1), :] = dpix[i, 0:NP, :]

    @pl.when(core == 1)
    def _():
        for i in range(OWN):
            half_rows[0, NP * i : NP * (i + 1), :] = dpix[i, 0:NP, :]
        to_image.start()
        drows[:, HALF:] = total.astype(BF)

    for step in steps[WAYS_AT : WAYS_AT + 2]:
        step()

    @pl.when(first)
    def _():
        to_image.wait_recv()
        drows[OWN * NP :, :] = half_rows[1]

    @pl.when(core == 1)
    def _():
        to_text.wait_recv()
        drows[:, :HALF] = tall[1]

    for step in steps[WAYS_AT + 2 :]:
        step()
    vcp.wait()
    pltpu.make_async_copy(vbuf.at[pl.ds(0, 31)], vbuf.at[pl.ds(0, 31)], vr).wait()
    vout[...] = jnp.sum(vbuf[...], axis=0)
    pltpu.make_async_copy(vbuf.at[pl.ds(0, 31)], vbuf.at[pl.ds(0, 31)], vs).wait()

    @pl.when(first)
    def _():
        to_text.wait_send()

    @pl.when(core == 1)
    def _():
        to_image.wait_send()

    drain()


def summed(plen, g, vg, back, dpix):
    any_ = pl.BlockSpec(memory_space=pl.ANY)
    vmem = pl.BlockSpec(memory_space=pltpu.VMEM)
    smem = pl.BlockSpec(memory_space=pltpu.SMEM)
    return pl.pallas_call(
        last_sum,
        out_shape=(
            jax.ShapeDtypeStruct((SLAB, D), F32),
            jax.ShapeDtypeStruct((VEC, 128), F32),
            jax.ShapeDtypeStruct((ROWS, D), BF),
        ),
        in_specs=[smem, any_, any_, vmem, vmem],
        out_specs=(vmem, vmem, vmem),
        scratch_shapes=[
            pltpu.VMEM((16, PART, D), BF),
            pltpu.VMEM((32, VEC, 128), F32),
            pltpu.VMEM((2, OWN * NP, D), BF),
            pltpu.VMEM((2, ROWS, HALF), BF),
            pltpu.VMEM((RSLOT, PMAX, HALF), BF),
            dma,
            dma,
            dma,
            dma((2,)),
            dma((2, SPAN)),
        ]
        + rs_scratch(),
        compiler_params=pltpu.CompilerParams(
            collective_id=2, has_side_effects=True, vmem_limit_bytes=60 * 2**20
        ),
    )(plen, g, vg, back, dpix)


X_IN = ("dest", "plen", "rows", "cot", "wsh", "vblk", "wfull")
X_OUT = ("dpix", "vgb", "g", "encm", "dprem", "wall", "r1")
X_SCRATCH = (
    ("packed", (ROWS, HALF), BF),
    ("raw", (ROWS // 2, D), BF),
    ("pmsg", (RSLOT, MSG, HALF), BF),
    ("cmsg", (RSLOT, R, HALF), BF),
    ("arp", (RSLOT, MSG, HALF), BF),
    ("arc", (RSLOT, R, HALF), BF),
    ("gvp", (OWN, MSG, HALF), BF),
    ("gtp", (OWN, MSG, HALF), BF),
    ("gvc", (OWN, R, HALF), BF),
    ("gtc", (OWN, R, HALF), BF),
    ("gvo", (OWN, R, HALF), BF),
    ("img", (IMG_DEV + 1, R, HALF), BF),
    ("pim", (IMG_DEV + 1, PMAX, HALF), BF),
    ("vbuf", (32, VEC, 128), BF),
    ("vec", (VEC, D), F32),
    ("bias", (1, FF), F32),
    ("vg", (VEC, D), F32),
    ("bg", (1, FF), F32),
    ("pix", (OWN, NPAD, D), BF),
    ("og", (M, D), BF),
    ("dx", (M, D), BF),
    ("stem", (PIX, D), BF),
    ("qkvw", (3 * D, D), BF),
    ("outw", (D, D), BF),
    ("wb", (8, CH, D), BF),
    ("x", (M, D), BF),
    ("nrm", (M, D), BF),
    ("qkv", (M, 3 * D), BF),
    ("prob", (2 * OWN * 6, R, R), BF),
    ("ctx", (M, D), BF),
    ("res", (M, D), F32),
    ("mlp", (M, D), BF),
    ("big", (M, D), F32),
    ("hid", (M, FF), BF),
    ("slope", (M, FF), BF),
    ("dpr", (M, CH), BF),
    ("f1", (M, CH), F32),
)
X_SEMS = (
    ("psem", (2, 4, SPAN)),
    ("gsem", (2, 6)),
    ("lsem", (8,)),
    ("vsem", (2,)),
    ("wsem", (3,)),
    ("csem", (2, 2)),
    ("osem", (2, 2)),
)


def x_kernel(near, *refs):
    names = X_IN + X_OUT + tuple(n for n, _, _ in X_SCRATCH) + tuple(n for n, _ in X_SEMS)
    K = SimpleNamespace(**dict(zip(names, refs)))
    gsems = refs[len(names) :]
    if not near:
        gsems, sum_refs = gsems[: -len(RS_BUFS) - len(RS_SEMS)], gsems[-len(RS_BUFS) - len(RS_SEMS) :]
    K.upb, K.downb = K.wb.at[pl.ds(0, 2)], K.wb.at[pl.ds(2, 2)]
    K.gub, K.gdb = K.wb.at[pl.ds(4, 2)], K.wb.at[pl.ds(6, 2)]
    core = lax.axis_index("stream")
    chip = lax.axis_index("dp")
    n_dp = lax.axis_size("dp")
    sib = (1 - core, chip)
    first = core == 0
    second = core == 1
    me = core * n_dp + chip
    if near:
        greet_near(core, chip, n_dp)
    else:
        greet_all(core, chip)
    wall = K.wfull if near else K.wall

    n_sems = len(gsems) // 2
    todo = []
    if not near:
        parts = [gather_steps(K.wsh, wall, gsems[p * n_sems : (p + 1) * n_sems], p) for p in range(2)]
        todo = [step for pair_ in zip(*parts) for step in pair_]

    def advance(n):
        for _ in range(n):
            if todo:
                todo.pop(0)()

    if not near:

        advance(2)

        K.vbuf[me] = K.vblk[...]
        own_slab = wall.at[pl.ds(pl.multiple_of(me * SLAB, 8), SLAB)]
        keep = K.upb.at[0, pl.ds(0, SLAB)]
        kin = pltpu.make_async_copy(K.wsh, keep, K.lsem.at[1])
        kout = pltpu.make_async_copy(keep, own_slab, K.lsem.at[2])
        kin.start()

    last_rows = K.rows.at[pl.ds(ROWS // 2, ROWS // 2)]
    pix_go = remote(last_rows, K.raw, K.gsem.at[0, 4], K.gsem.at[1, 4], (1, chip))
    pack_go = remote(
        K.rows.at[:, pl.ds(0, HALF)], K.packed, K.gsem.at[0, 4], K.gsem.at[1, 4], (0, chip)
    )
    pix_own = pltpu.make_async_copy(K.rows.at[pl.ds(0, ROWS // 2)], K.raw, K.lsem.at[0])
    pack_own = pltpu.make_async_copy(K.rows.at[:, pl.ds(HALF, HALF)], K.packed, K.lsem.at[0])

    @pl.when(first)
    def _():
        pix_go.start()
        pix_own.start()

    @pl.when(second)
    def _():
        pack_go.start()
        pack_own.start()

    if not near:

        def vsend(k, carry):
            peer = (me + k) % 32
            remote(K.vblk, K.vbuf.at[me], K.vsem.at[0], K.vsem.at[1], (peer // 16, peer % 16)).start()
            return carry

        lax.fori_loop(1, 32, vsend, 0)

    def pair(t):
        return pl.ds(CAP * t, CAP)

    def rc(src, dst, k, i, dev):
        return remote(src, dst, K.psem.at[0, k, i], K.psem.at[1, k, i], dev)

    down = [(core, (chip + n_dp - t - 1) % n_dp) for t in range(SPAN)]
    up = [(core, (chip + t + 1) % n_dp) for t in range(SPAN)]
    pin = [rc(K.pmsg.at[pair(t)], K.arp.at[pair(t)], 0, t, down[t]) for t in range(SPAN)]
    cin = [rc(K.cmsg.at[pair(t)], K.arc.at[pair(t)], 1, t, down[t]) for t in range(SPAN)]

    if not near:
        kin.wait()
        kout.start()

    @pl.when(first)
    def _():
        pack_go.wait_recv()
        pix_own.wait()

    @pl.when(second)
    def _():
        pix_go.wait_recv()
        pack_own.wait()

    def prefix_slots():
        target = slot_rows(K.plen, 0)
        pick = lax.broadcasted_iota(jnp.int32, (RSLOT * PMAX, ROWS), 1) == target
        rows = nn(pick.astype(F32).astype(BF), K.packed[...]).astype(BF)
        for s in range(RSLOT):
            K.pmsg[s, 0:PMAX, :] = rows[PMAX * s : PMAX * (s + 1), :]
            size = jnp.full((MSG - PMAX, HALF), K.plen[s], jnp.int32)
            K.pmsg[s, PMAX:MSG, :] = size.astype(F32).astype(BF)

    place_row = lax.broadcasted_iota(jnp.int32, (PMAX, 1), 0)
    zero = jnp.zeros((), BF)

    def cot_slot(s, none):
        size = K.plen[s]
        K.cmsg[s, 0:PMAX, :] = jnp.where(place_row < size, K.cot[s, NP:SEQ, :], zero)
        K.cmsg[s, PMAX : PMAX + NP, :] = jnp.where(
            jnp.full((NP, 1), size, jnp.int32) > 0, K.cot[s, 0:NP, :], zero
        )
        K.cmsg[s, PMAX + NP : R, :] = jnp.zeros((NPAD - NP, HALF), BF)
        return none

    prefix_slots()
    for t in ISSUE:
        pin[t].start()
    advance(4)
    for s in range(0, RSLOT, 2):
        lax.fori_loop(s, s + 2, cot_slot, 0)
        advance(2)
    for i in range(OWN):
        K.pix[i, 0:NP, :] = K.raw[NP * i : NP * (i + 1), :]
        K.pix[i, NP:NPAD, :] = jnp.zeros((NPAD - NP, D), BF)
    advance(2 * CIN_AT - 14)
    for t in ISSUE:
        cin[t].start()
    advance(99)
    if not near:
        for p in range(2):
            rows = (CUT, SLAB - CUT)[p] * 16
            piece = wall.at[pl.ds(0, rows)]
            pltpu.make_async_copy(piece, piece, gsems[p * n_sems + n_sems - 1]).wait()
        pltpu.make_async_copy(K.vbuf.at[pl.ds(0, 31)], K.vbuf.at[pl.ds(0, 31)], K.vsem.at[1]).wait()
    vec = jnp.zeros((VEC, D), F32)
    lane_d = lax.broadcasted_iota(jnp.int32, (1, D), 1)
    n_dev = 2 * n_dp
    width = D // n_dev
    if near:
        K.vec[...] = K.vblk[...].astype(F32)
    else:

        def spread(k, total):
            block = jnp.concatenate([K.vbuf[k].astype(F32), jnp.zeros((VEC, D - 128), F32)], axis=1)
            block = jnp.where(lane_d < width, block, 0.0)
            return total + pltpu.roll(block, k * width, 1)

        K.vec[...] = lax.fori_loop(0, n_dev, spread, vec)
    for j in range(4):
        K.bias[:, j * D : (j + 1) * D] = K.vec[5 + j : 6 + j, :]
    def load(dst, lo, n, sem):
        return pltpu.make_async_copy(wall.at[pl.ds(lo, n)], dst, sem)

    ls = load(K.stem, 0, PIX, K.wsem.at[0])
    lq = load(K.qkvw, PIX, 3 * D, K.wsem.at[1])
    lo_ = load(K.outw, PIX + 3 * D, D, K.wsem.at[2])
    if not near:
        kout.wait()
    ls.start()
    lq.start()
    lo_.start()

    def chunk(c, slot):
        at = pl.multiple_of(c * CH, 16)
        return (
            pltpu.make_async_copy(wall.at[pl.ds(UP + at, CH)], K.upb.at[slot], K.csem.at[0, slot]),
            pltpu.make_async_copy(wall.at[pl.ds(DOWN + at, CH)], K.downb.at[slot], K.csem.at[1, slot]),
        )

    def mine(k):
        return K.dest[OWN * core + k]

    def image_of(slot):
        found = jnp.int32(IMG_DEV)
        for j in range(IMG_DEV):
            found = jnp.where(K.dest[j] == slot, j, found)
        return found

    def theirs(k):
        return K.dest[OWN * (1 - core) + k]

    own_half = pl.ds(pl.multiple_of(core * HALF, 128), HALF)
    other_half = pl.ds(pl.multiple_of((1 - core) * HALF, 128), HALF)

    def swap(src, dst, k):
        return remote(src, dst, K.gsem.at[0, k], K.gsem.at[1, k], sib)

    pswap = swap(K.gvp, K.gtp, 0)
    cswap = swap(K.gvc, K.gtc, 1)
    for cp in pin:
        cp.wait_recv()
    for k in range(OWN):
        K.gvp[k] = K.arp[theirs(k)]
    lens = []
    for k in range(OWN):
        K.x[R * k : R * k + PMAX, own_half] = K.arp[mine(k), 0:PMAX, :]
        lens.append(K.arp[mine(k), PMAX:MSG, :].astype(F32)[0:1, 0:1])
    pswap.start()
    ls.wait()
    for i in range(OWN):
        K.x[R * i + PMAX : R * (i + 1), :] = nn(K.pix[i], K.stem[...]).astype(BF)
    pswap.wait_recv()
    for k in range(OWN):
        K.x[R * k : R * k + PMAX, other_half] = K.gtp[k, 0:PMAX, :]

    def norm1(rows):
        xhat, _ = norm_parts(K.x[rows, :].astype(F32))
        K.nrm[rows, :] = (xhat * K.vec[0:1, :] + K.vec[1:2, :]).astype(BF)

    rows_loop(norm1)
    lq.wait()
    for k in range(3):
        K.qkv[:, k * D : (k + 1) * D] = nt(K.nrm[...], K.qkvw[k * D : (k + 1) * D, :]).astype(BF)
    lane = lax.broadcasted_iota(jnp.int32, (1, 128), 1)
    low_half = lane < HD
    key = lax.broadcasted_iota(jnp.int32, (1, R), 1)
    scale = HD**-0.5

    def heads(i, p):
        ln = jnp.where(i == 0, lens[0], lens[1])
        ok = (key.astype(F32) < ln) | ((key >= PMAX) & (key < PMAX + NP))
        rows = pl.ds(pl.multiple_of(i * R, 16), R)

        def part(k):
            return K.qkv[rows, pl.ds(pl.multiple_of(k * D + p * 128, 128), 128)]

        return rows, ok, part(0), part(1), part(2)

    def halves(v):
        return jnp.where(low_half, v, zero), jnp.where(low_half, zero, v)

    def attend(n, c):
        i, p = n // 6, n % 6
        rows, ok, q, k, v = heads(i, p)
        outs = []
        for h, qh in enumerate(halves(q)):
            s = jnp.where(ok, nt(qh, k) * scale, MASKED)
            e = jnp.exp(s - jnp.max(s, axis=-1, keepdims=True))
            a = (e * (1.0 / jnp.sum(e, axis=-1, keepdims=True))).astype(BF)
            K.prob[2 * n + h] = a
            outs.append(nn(a, v))
        here = pl.ds(pl.multiple_of(p * 128, 128), 128)
        K.ctx[rows, here] = jnp.where(low_half, outs[0], outs[1]).astype(BF)
        return c

    lax.fori_loop(0, OWN * 6, attend, 0, unroll=3)
    lo_.wait()
    K.res[...] = nt(K.ctx[...], K.outw[...])

    def norm2(rows):
        r = K.res[rows, :] + K.x[rows, :].astype(F32)
        K.res[rows, :] = r
        xhat, _ = norm_parts(r)
        K.mlp[rows, :] = (xhat * K.vec[2:3, :] + K.vec[3:4, :]).astype(BF)
        K.big[rows, :] = r + K.vec[4:5, :]

    rows_loop(norm2)
    count = FF // CH

    def fetch(c, slot):
        for cp in chunk(c, slot):
            cp.wait()

        @pl.when(c + 1 < count)
        def _():
            for cp in chunk(c + 1, 1 - slot):
                cp.start()

    def ffn(c, carry):
        slot = lax.rem(c, 2)
        fetch(c, slot)
        cols = pl.ds(pl.multiple_of(c * CH, 128), CH)
        K.f1[...] = nt(K.mlp[...], K.upb[slot])
        b = K.bias[:, cols]

        def act(i, none):
            rows = pl.ds(pl.multiple_of(i * LNB, 16), LNB)
            h, dh = gelu_both(K.f1[rows, :] + b)
            K.hid[rows, cols] = h.astype(BF)
            K.slope[rows, cols] = dh.astype(BF)
            return none

        lax.fori_loop(0, M // LNB, act, 0, unroll=True)
        K.big[...] += nn(K.hid[:, cols], K.downb[slot])
        return carry

    for cp in chunk(0, 0):
        cp.start()
    lax.fori_loop(0, count, ffn, 0)
    for cp in chunk(0, 0):
        cp.start()
    for k in range(OWN):
        K.gvo[k] = K.big[R * k : R * (k + 1), other_half].astype(BF)
    for k in range(OWN):
        K.img[OWN * core + k] = K.big[R * k : R * (k + 1), own_half].astype(BF)
    K.img[IMG_DEV] = jnp.zeros((R, HALF), BF)
    oswap = swap(K.gvo, K.img.at[pl.ds(OWN * core, OWN)], 2)
    oswap.start()
    K.big[...] = jnp.zeros((M, D), F32)
    oswap.wait()
    for cp in cin:
        cp.wait_send()
    for k in range(RSLOT):
        K.cmsg[k] = K.img[image_of(k)]
    eout = [rc(K.cmsg.at[pair(t)], K.encm.at[pair(t)], 2, t, up[t]) for t in range(SPAN)]
    for t in ISSUE:
        eout[t].start()
    for cp in cin:
        cp.wait_recv()
    for k in range(OWN):
        K.gvc[k] = K.arc[theirs(k)]
    for k in range(OWN):
        K.og[R * k : R * (k + 1), own_half] = K.arc[mine(k)]
    cswap.start()
    cswap.wait_recv()
    for k in range(OWN):
        K.og[R * k : R * (k + 1), other_half] = K.gtc[k]

    def store(c, slot):
        at = pl.multiple_of(c * CH, 16)
        return (
            pltpu.make_async_copy(K.gub.at[slot], K.g.at[pl.ds(UP + at, CH)], K.osem.at[0, slot]),
            pltpu.make_async_copy(K.gdb.at[slot], K.g.at[pl.ds(DOWN + at, CH)], K.osem.at[1, slot]),
        )

    def ffn_back(c, carry):
        slot = lax.rem(c, 2)
        fetch(c, slot)

        @pl.when(c >= 2)
        def _():
            for cp in store(c - 2, slot):
                cp.wait()

        cols = pl.ds(pl.multiple_of(c * CH, 128), CH)
        K.f1[...] = nt(K.og[...], K.downb[slot])

        def act(i, tot):
            rows = pl.ds(pl.multiple_of(i * 16, 16), 16)
            dp = (K.f1[rows, :] * K.slope[rows, cols].astype(F32)).astype(BF)
            K.dpr[rows, :] = dp
            return tot + dp.astype(F32)

        tot = lax.fori_loop(0, M // 16, act, jnp.zeros((16, CH), F32), unroll=2)
        K.bg[:, cols] = jnp.sum(tot, axis=0, keepdims=True)
        K.big[...] += nn(K.dpr[...], K.upb[slot])
        K.gub[slot] = tn(K.dpr[...], K.mlp[...]).astype(BF)
        K.gdb[slot] = tn(K.hid[:, cols], K.og[...]).astype(BF)
        for cp in store(c, slot):
            cp.start()
        return carry

    lax.fori_loop(0, count, ffn_back, 0)
    for slot in range(2):
        for cp in store(count - 2 + slot, slot):
            cp.wait()
    late = []
    if not near:

        def obuf(i):
            return K.wb.at[i // 2, pl.ds(pl.multiple_of((i % 2) * PART, 16), PART)]

        begin, late, end_sum = sum_steps(1, K.g, K.r1, obuf, sum_refs, SUM_VIA)
        begin()

    def advance_sum(n=1):
        for _ in range(n):
            if late:
                late.pop(0)()

    def back2(i, c):
        rows = pl.ds(pl.multiple_of(i * LNB, 16), LNB)
        o = K.og[rows, :].astype(F32)
        d, dg, dc = norm_back(K.res[rows, :], K.big[rows, :], K.vec[2:3, :])
        d = d + o
        K.res[rows, :] = d
        K.dx[rows, :] = d.astype(BF)
        return (c[0] + dg, c[1] + dc, c[2] + jnp.sum(o, axis=0, keepdims=True))

    none = jnp.zeros((1, D), F32)
    dg2, dc2, dob = lax.fori_loop(0, M // LNB, back2, (none, none, none), unroll=True)
    K.vg[8:VEC, :] = jnp.zeros((VEC - 8, D), F32)
    K.vg[2:3, :] = dg2
    K.vg[3:4, :] = dc2
    K.vg[4:5, :] = dob
    for j in range(4):
        K.vg[5 + j : 6 + j, :] = K.bg[:, j * D : (j + 1) * D]

    advance_sum()

    def put(src, lo, n, sem):
        return pltpu.make_async_copy(src, K.g.at[pl.ds(lo, n)], sem)

    K.mlp[...] = nn(K.dx[...], K.outw[...]).astype(BF)
    advance_sum()
    K.outw[...] = tn(K.dx[...], K.ctx[...]).astype(BF)
    po = put(K.outw, PIX + 3 * D, D, K.wsem.at[2])
    po.start()

    def attend_back(n, c):
        i, p = n // 6, n % 6
        rows, ok, q, k, v = heads(i, p)
        here = pl.ds(pl.multiple_of(p * 128, 128), 128)
        dc = K.mlp[rows, here]
        dq = []
        dk = dv = None
        for h, (qh, dch) in enumerate(zip(halves(q), halves(dc))):
            a = K.prob[2 * n + h]
            af = a.astype(F32)
            t = af * nt(dch, v)
            dsc = (t - af * jnp.sum(t, axis=-1, keepdims=True)).astype(BF)
            dq.append(nn(dsc, k))
            dkh = tn(dsc, qh)
            dvh = tn(a, dch)
            dk = dkh if dk is None else dk + dkh
            dv = dvh if dv is None else dv + dvh

        def at(j):
            return pl.ds(pl.multiple_of(j * D + p * 128, 128), 128)

        K.qkv[rows, at(0)] = (jnp.where(low_half, dq[0], dq[1]) * scale).astype(BF)
        K.qkv[rows, at(1)] = (dk * scale).astype(BF)
        K.qkv[rows, at(2)] = dv.astype(BF)
        return c

    advance_sum()
    for group in range(6):
        lax.fori_loop(2 * group, 2 * group + 2, attend_back, 0)
        advance_sum()
    K.big[...] = nn(K.qkv[...], K.qkvw[...])
    advance_sum()

    def back1(i, c):
        rows = pl.ds(pl.multiple_of(i * LNB, 16), LNB)
        d, dg, dc = norm_back(K.x[rows, :].astype(F32), K.big[rows, :], K.vec[0:1, :])
        K.dx[rows, :] = (K.res[rows, :] + d).astype(BF)
        return (c[0] + dg, c[1] + dc)

    dg1, dc1 = lax.fori_loop(0, M // LNB, back1, (none, none), unroll=True)
    advance_sum()
    pswap.wait_send()
    cswap.wait_send()
    for k in range(OWN):
        K.gvp[k, 0:PMAX, :] = K.dx[R * k : R * k + PMAX, other_half]
    for k in range(OWN):
        K.pim[OWN * core + k] = K.dx[R * k : R * k + PMAX, own_half]
    K.pim[IMG_DEV] = jnp.zeros((PMAX, HALF), BF)
    dswap = swap(K.gvp.at[:, pl.ds(0, PMAX)], K.pim.at[pl.ds(OWN * core, OWN)], 3)
    dswap.start()
    K.vg[0:1, :] = dg1
    K.vg[1:2, :] = dc1

    def cut(k, c):
        K.vgb[k] = pltpu.roll(K.vg[...], lax.rem(D - k * width, D), 1)[:, 0:128]
        return c

    lax.fori_loop(0, n_dev, cut, 0)
    for k in range(3):
        K.qkvw[k * D : (k + 1) * D, :] = tn(K.qkv[:, k * D : (k + 1) * D], K.nrm[...]).astype(BF)
    pq = put(K.qkvw, PIX, 3 * D, K.wsem.at[1])
    pq.start()
    dswap.wait()
    if not near:
        advance_sum(99)
    dout = []
    if near:
        for k in range(RSLOT):
            K.arp[k, 0:PMAX, :] = K.pim[image_of(k)]
        dout = [
            rc(K.arp.at[pair(t), pl.ds(0, PMAX)], K.dprem.at[pair(t)], 3, t, up[t])
            for t in range(SPAN)
        ]
        for t in ISSUE:
            dout[t].start()
    else:
        for k in range(RSLOT):
            K.dprem[k] = K.pim[image_of(k)]
    tot = None
    for i in range(OWN):
        dp = K.dx[R * i + PMAX : R * (i + 1), :]
        K.dpix[i] = nt(dp, K.stem[...]).astype(BF)
        t = tn(K.pix[i], dp)
        tot = t if tot is None else tot + t
    K.stem[...] = tot.astype(BF)
    ps = put(K.stem, 0, PIX, K.wsem.at[0])
    ps.start()
    for cp in eout + dout:
        cp.wait()
    po.wait()
    pq.wait()
    ps.wait()
    for cp in pin:
        cp.wait_send()

    @pl.when(first)
    def _():
        pix_go.wait_send()

    @pl.when(second)
    def _():
        pack_go.wait_send()

    if not near:
        end_sum()
        for p in range(2):
            for step in gather_steps(
                K.wsh, wall, gsems[p * n_sems : (p + 1) * n_sems], p, draining=True
            ):
                step()
            rows = (CUT, SLAB - CUT)[p] * 16
            piece = wall.at[pl.ds(0, rows)]
            pltpu.make_async_copy(piece, piece, gsems[p * n_sems + n_sems - 2]).wait()
        pltpu.make_async_copy(K.vbuf.at[pl.ds(0, 31)], K.vbuf.at[pl.ds(0, 31)], K.vsem.at[0]).wait()


def whole_block(dest, plen, rows, cot, wsh, vblk, wfull, n_dev):
    near = wfull is not None
    any_ = pl.BlockSpec(memory_space=pl.ANY)
    vmem = pl.BlockSpec(memory_space=pltpu.VMEM)
    smem = pl.BlockSpec(memory_space=pltpu.SMEM)
    total = SLAB * 32 if not near else wfull.shape[0]
    if near:
        wsh = wsh[:8]
    else:
        wfull = wsh[:8]
    outs = (
        jax.ShapeDtypeStruct((OWN, NPAD, D), BF),
        jax.ShapeDtypeStruct((n_dev, VEC, 128), F32),
        jax.ShapeDtypeStruct((total, D), BF),
        jax.ShapeDtypeStruct((RSLOT, R, HALF), BF),
        jax.ShapeDtypeStruct((RSLOT, PMAX, HALF), BF),
        jax.ShapeDtypeStruct((8, D) if near else (total, D), BF),
        jax.ShapeDtypeStruct((8, D) if near else (SLAB, D), F32),
    )
    return pl.pallas_call(
        functools.partial(x_kernel, near),
        out_shape=outs,
        in_specs=[smem, smem, any_, vmem, any_, vmem, any_],
        out_specs=(vmem, vmem, any_, any_, vmem, any_, vmem),
        scratch_shapes=[pltpu.VMEM(s, t) for _, s, t in X_SCRATCH]
        + [dma(s) for _, s in X_SEMS]
        + ([] if near else gather_sems() + gather_sems() + rs_scratch()),
        compiler_params=pltpu.CompilerParams(
            collective_id=3, has_side_effects=True, vmem_limit_bytes=63 * 2**20
        ),
    )(dest, plen, rows, cot, wsh, vblk, wfull)


def swapped(value):
    return lax.ppermute(value, "stream", [(0, 1), (1, 0)])


def body(
    stream_rows,
    dest,
    prefix_len,
    weights,
    momentum,
    average,
    vectors,
    vec_momentum,
    vec_average,
    cotangent,
):
    core = lax.axis_index("stream")
    first = core == 0
    n_dp = lax.axis_size("dp")
    n_dev = 2 * n_dp
    lane = vectors.shape[1]
    kernels = n_dp == 16

    rows = stream_rows[0, 0]
    half_rows = ROWS // 2
    lengths = prefix_len[0]
    slots = dest[0]
    shard = weights.astype(BF)
    if kernels:
        full = None
        block = jnp.pad(vectors.astype(BF), ((0, VEC - 9), (0, 128 - lane)))
    else:
        full = lax.all_gather(shard, ALL, axis=0, tiled=True)
        block = jnp.pad(vectors.astype(BF), ((0, VEC - 9), (0, 0)))
        block = lax.all_gather(block, ALL, axis=1, tiled=True)
    d_pixels, vec_blocks, grads, enc_back, prefix_back, _, late_grad = whole_block(
        slots, lengths, rows, cotangent[0], shard, block, full, n_dev
    )
    if kernels:
        early_grad, vec_grad, d_rows = summed(
            lengths, grads, vec_blocks, prefix_back, d_pixels
        )
        weight_grad = jnp.where(first, early_grad, late_grad)
    else:
        weight_grad = lax.psum_scatter(grads, ALL, scatter_dimension=0, tiled=True).astype(F32)
        vec_grad = lax.psum_scatter(vec_blocks, ALL, scatter_dimension=0, tiled=True)[0]
    vec_grad = vec_grad[:9, :lane]

    columns = jnp.arange(SEQ, dtype=jnp.int32)
    row_ok = (columns[None, :] < NP + lengths[:, None]) & (lengths[:, None] > 0)
    enc_out = jnp.concatenate([enc_back[:, PMAX : PMAX + NP], enc_back[:, :PMAX]], axis=1)
    enc_out = jnp.where(row_ok[:, :, None], enc_out, jnp.zeros((), BF))[None]

    if not kernels:
        offsets = jnp.cumsum(lengths) - lengths
        places = jnp.arange(PMAX, dtype=jnp.int32)
        row_index = offsets[:, None] + places[None, :]
        keep_mask = places[None, :] < lengths[:, None]
        rows_at = jnp.arange(ROWS, dtype=jnp.int32)
        pick = (
            (row_index.reshape(-1)[:, None] == rows_at[None, :]) & keep_mask.reshape(-1)[:, None]
        ).astype(BF)
        d_packed = tn(pick, prefix_back.reshape(RSLOT * PMAX, HALF)).astype(BF)
        d_pixels = d_pixels[:, :NP].reshape(half_rows, D)
        give = jnp.where(
            first, jnp.concatenate([d_packed[:half_rows], d_packed[half_rows:]], axis=1), d_pixels
        )
        got = swapped(give)
        d_image_rows = jnp.concatenate([d_pixels, got])
        d_text_rows = jnp.concatenate(
            [jnp.concatenate([got[:, :HALF], got[:, HALF:]], axis=0), d_packed], axis=1
        )
        d_rows = jnp.where(first, d_image_rows, d_text_rows)
    d_rows = d_rows.astype(F32)[None, None]

    rate = 0.5 * (D * IMG_DEV * n_dp * NP) ** (-0.5)
    new_momentum = MOMENT * momentum + weight_grad
    new_weights = weights - rate * (weight_grad + MOMENT * new_momentum)
    new_average = DECAY * average + (1.0 - DECAY) * new_weights
    vec_new_momentum = MOMENT * vec_momentum + vec_grad
    vec_new = vectors - rate * (vec_grad + MOMENT * vec_new_momentum)
    vec_new_average = DECAY * vec_average + (1.0 - DECAY) * vec_new
    return (
        enc_out,
        d_rows,
        weight_grad,
        new_momentum,
        new_average,
        new_weights,
        new_weights.astype(BF),
        vec_grad,
        vec_new_momentum,
        vec_new_average,
        vec_new,
        vec_new.astype(BF),
    )


def solution(mesh):
    both = P(ALL, None)
    lanes = P(None, ALL)
    in_specs = (
        P("stream", "dp", None, None),
        P("dp", None),
        P("dp", None),
        both,
        both,
        both,
        lanes,
        lanes,
        lanes,
        P("dp", None, None, "stream"),
    )
    out_specs = (
        P("dp", None, None, "stream"),
        P("stream", "dp", None, None),
        both,
        both,
        both,
        both,
        both,
        lanes,
        lanes,
        lanes,
        lanes,
        lanes,
    )
    return jax.shard_map(body, mesh=mesh, in_specs=in_specs, out_specs=out_specs, check_vma=False)
```

```python
import functools
from types import SimpleNamespace

import jax
import jax.numpy as jnp
from jax import lax
from jax.experimental import pallas as pl
from jax.experimental.pallas import tpu as pltpu
from jax.sharding import PartitionSpec as P

D = 768
HEADS = 12
HD = 64
FF = 3072
PIX = 768
NP = 196
PMAX = 64
SPAN = 4
IMG_DEV = 4
CAP = 2
RSLOT = 8
SEQ = 260
ROWS = 784
HALF = D // 2
OWN = IMG_DEV // 2
SLAB = 312
CUT = 160
NZ = 4

EPSILON = 1e-06
MASKED = -1e30
MOMENT = 0.5
DECAY = 0.5
BF = jnp.bfloat16
F32 = jnp.float32
ALL = ("stream", "dp")
MESH = pl.DeviceIdType.MESH


NPAD = 208
R = PMAX + NPAD
M = OWN * R
CH = 512
LNB = 32
MSG = PMAX + 16
VEC = 16
UP = PIX + 4 * D
DOWN = UP + FF
VIA_Z = (1, 2)
CIN_AT = 12
ISSUE = (1, 3, 0, 2)
SUM_VIA = (1, 2)
dma = pltpu.SemaphoreType.DMA


def nn(a, b):
    return lax.dot_general(a, b, (((1,), (0,)), ((), ())), preferred_element_type=F32)


def nt(a, b):
    return lax.dot_general(a, b, (((1,), (1,)), ((), ())), preferred_element_type=F32)


def tn(a, b):
    return lax.dot_general(a, b, (((0,), (0,)), ((), ())), preferred_element_type=F32)


def erf(v):
    v = jnp.clip(v, -3.832506856900711, 3.832506856900711)
    s = v * v
    top = 0.00022905065861350646
    for c in (0.0034082910107109506, 0.050955695062380861, 0.18520832239976145, 1.128379143519084):
        top = top * s + c
    low = -1.1791602954361697e-7
    for c in (
        0.000023547966471313185,
        0.0010179625278914885,
        0.014070470171167667,
        0.11098505178285362,
        0.49746925110067538,
        1.0,
    ):
        low = low * s + c
    return v * top / low


def gelu_both(v):
    phi = 0.5 * (1.0 + erf(v * 0.7071067811865476))
    return v * phi, phi + v * (0.3989422804014327 * jnp.exp(-0.5 * v * v))


def rows_loop(f, block=LNB, total=M):
    def run(i, c):
        f(pl.ds(pl.multiple_of(i * block, 16), block))
        return c

    lax.fori_loop(0, total // block, run, 0, unroll=True)


def norm_parts(v):
    off = v - jnp.mean(v, axis=-1, keepdims=True)
    inv = lax.rsqrt(jnp.mean(off * off, axis=-1, keepdims=True) + EPSILON)
    return off * inv, inv


def norm_back(v, dn, gain):
    xhat, inv = norm_parts(v)
    dx = dn * gain
    low = jnp.mean(dx, axis=-1, keepdims=True)
    slope = jnp.mean(dx * xhat, axis=-1, keepdims=True)
    return (
        (dx - low - xhat * slope) * inv,
        jnp.sum(dn * xhat, axis=0, keepdims=True),
        jnp.sum(dn, axis=0, keepdims=True),
    )


def slot_rows(plen, dim):
    shape = (RSLOT * PMAX, 1) if dim == 0 else (1, RSLOT * PMAX)
    at = lax.broadcasted_iota(jnp.int32, shape, dim)
    target = jnp.full(shape, -1, jnp.int32)
    offset = jnp.int32(0)
    for s in range(RSLOT):
        i = at - PMAX * s
        target = jnp.where((i >= 0) & (i < plen[s]), i + offset, target)
        offset = offset + plen[s]
    return target


def remote(src, dst, send, recv, dev):
    return pltpu.make_async_remote_copy(
        src_ref=src, dst_ref=dst, send_sem=send, recv_sem=recv, device_id=dev, device_id_type=MESH
    )


def place():
    core = lax.axis_index("stream")
    chip = lax.axis_index("dp")
    return core, chip, chip % 2, (chip // 2) % 2, chip // 4


def greet_all(core, chip):
    barrier = pltpu.get_barrier_semaphore()
    me = core * 16 + chip

    def one(k, carry):
        peer = (me + k) % 32
        pl.semaphore_signal(barrier, inc=1, device_id=(peer // 16, peer % 16), device_id_type=MESH)
        return carry

    lax.fori_loop(1, 32, one, 0)
    pl.semaphore_wait(barrier, 31)


def greet_near(core, chip, n_dp):
    barrier = pltpu.get_barrier_semaphore()
    for t in range(1, SPAN + 1):
        for peer in ((chip + t) % n_dp, (chip + n_dp - t) % n_dp):
            pl.semaphore_signal(barrier, inc=1, device_id=(core, peer), device_id_type=MESH)
    pl.semaphore_signal(barrier, inc=1, device_id=(1 - core, chip), device_id_type=MESH)
    pl.semaphore_wait(barrier, 2 * SPAN + 1)


def gather_sems():
    four = dma((4,))
    return [dma((2, 4)), four, dma((2, 4)), four] + [four] * 8 + [dma, dma]


def gather_steps(w_ref, out, sems, part, draining=False):
    core, chip, x, y, z = place()
    zs, zr, ds, dr, xs, xr, ys, yr, as_, ar, bs, br, ss, sr = sems
    base = core * 16
    me = base + chip
    flat = chip % 4
    xn = chip + 1 - 2 * x
    yn = chip + 2 - 4 * y
    start, size = ((0, CUT), (CUT, SLAB - CUT))[part]
    top = pl.ds(0, 80)
    bottom = pl.ds(80, size - 80)
    sib = (1 - core, chip)
    w_ref = w_ref.at[pl.ds(start, size)]

    def slab_of(slab, rows=None):
        whole = out.at[pl.ds(pl.multiple_of(slab * SLAB + start, 8), size)]
        return whole if rows is None else whole.at[rows]

    def rc(src, slab, ssem, rsem, dev, rows=None):
        return remote(src, slab_of(slab, rows), ssem, rsem, dev)

    def go(cond, make):
        def act():
            if draining:
                make().wait_send()
            else:
                make().start()

        if cond is None:
            act()
        else:
            pl.when(cond)(act)

    def to_sib(src, slab):
        if not draining:
            rc(src, slab, ss, sr, sib).start()

    def arrive(copy):
        if not draining:
            copy().wait_recv()

    def at(t, sign):
        zz = z + sign * t
        return zz, (zz >= 0) & (zz < NZ)

    def own():
        go(None, lambda: rc(w_ref, me, xs.at[z], xr.at[z], (core, xn)))
        go(None, lambda: rc(w_ref, me, ys.at[z], yr.at[z], (core, yn)))
        for k, s in enumerate((1, -1)):
            go(
                (z + s >= 0) & (z + s < NZ),
                lambda k=k, s=s: rc(w_ref, me, zs.at[k, z], zr.at[z], (core, chip + 4 * s)),
            )
        to_sib(w_ref, me)

    def column(t, sign):
        zz, here = at(t, sign)
        slab = base + zz * 4 + flat
        k = 0 if sign < 0 else 1

        @pl.when(here)
        def _():
            arrive(lambda: rc(w_ref, slab, ss, zr.at[zz], sib))

        src = slab_of(slab)
        go(
            here & (z - sign >= 0) & (z - sign < NZ),
            lambda: rc(src, slab, zs.at[k, zz], zr.at[zz], (core, chip - 4 * sign)),
        )
        go(here, lambda: rc(src, slab, xs.at[zz], xr.at[zz], (core, xn)))
        go(here, lambda: rc(src, slab, ys.at[zz], yr.at[zz], (core, yn)))

        @pl.when(here)
        def _():
            to_sib(src, slab)

    def plane(t, sign):
        zz, here = at(t, sign)
        xslab = base + zz * 4 + flat + 1 - 2 * x
        yslab = base + zz * 4 + flat + 2 - 4 * y

        @pl.when(here)
        def _():
            arrive(lambda: rc(w_ref, xslab, ss, xr.at[zz], sib))

        if t not in VIA_Z:
            go(
                here,
                lambda: rc(slab_of(xslab, top), xslab, as_.at[zz], ar.at[zz], (core, yn), top),
            )

        @pl.when(here)
        def _():
            arrive(lambda: rc(w_ref, yslab, ss, yr.at[zz], sib))

        if t not in VIA_Z:
            go(
                here,
                lambda: rc(slab_of(yslab, bottom), yslab, bs.at[zz], br.at[zz], (core, xn), bottom),
            )

        @pl.when(here)
        def _():
            to_sib(slab_of(xslab), xslab)
            to_sib(slab_of(yslab), yslab)

    def diag(t, sign):
        zz, here = at(t, sign)
        slab = base + zz * 4 + 3 - flat
        src = slab_of(slab)
        if t in VIA_Z:

            @pl.when(here)
            def _():
                arrive(lambda: rc(w_ref, slab, ss, dr.at[zz], sib))
        else:

            @pl.when(here)
            def _():
                arrive(lambda: rc(slab_of(slab, top), slab, ss, ar.at[zz], sib, top))
                arrive(lambda: rc(slab_of(slab, bottom), slab, ss, br.at[zz], sib, bottom))

        if t == 0 and 1 in VIA_Z:
            for k, s in enumerate((1, -1)):
                go(
                    (z + s >= 0) & (z + s < NZ),
                    lambda k=k, s=s: rc(src, slab, ds.at[k, zz], dr.at[zz], (core, chip + 4 * s)),
                )
        if t >= 1 and t + 1 in VIA_Z:
            k = 0 if sign < 0 else 1
            go(
                here & (z - sign >= 0) & (z - sign < NZ),
                lambda: rc(src, slab, ds.at[k, zz], dr.at[zz], (core, chip - 4 * sign)),
            )

        @pl.when(here)
        def _():
            to_sib(src, slab)

    def both(f, t):
        def run():
            f(t, 1)
            if t:
                f(t, -1)

        return run

    return [
        own,
        both(column, 1),
        both(plane, 0),
        both(column, 2),
        both(diag, 0),
        both(plane, 1),
        both(column, 3),
        both(diag, 1),
        both(plane, 2),
        both(plane, 3),
        both(diag, 2),
        both(diag, 3),
    ]


PART = 160
SHIFT = SLAB - PART
ADD = 16
ADD_UNROLL = 1
WAYS_AT = 11
RS_BUFS = (
    ("sbuf", (16, PART, D), BF),
    ("xb", (4, PART, D), BF),
    ("yb", (4, PART, D), BF),
    ("dzb", (2, 2, PART, D), BF),
    ("czb", (2, 3, PART, D), BF),
    ("ab", (4, PART // 2, D), BF),
    ("bb", (4, PART // 2, D), BF),
    ("fin", (PART, D), F32),
)
RS_SEMS = (
    ("load", (16,)),
    ("ssend", ()),
    ("srecv", (16,)),
    ("xs", (4,)),
    ("xr", (4,)),
    ("ys", (4,)),
    ("yr", (4,)),
    ("dzs", (2, 2)),
    ("dzr", (2, 2)),
    ("czs", (2, 3)),
    ("czr", (2, 3)),
    ("as_", (4,)),
    ("ar", (4,)),
    ("bs", (4,)),
    ("br", (4,)),
    ("fsem", (2,)),
)


def rs_scratch():
    return [pltpu.VMEM(s, t) for _, s, t in RS_BUFS] + [dma(s) for _, s in RS_SEMS]


def add_rows(dst, sources, lo, size):
    def piece(i, c):
        tot = None
        for ref, at in sources:
            v = ref[pl.ds(pl.multiple_of(at + i * ADD, 16), ADD), :].astype(F32)
            tot = v if tot is None else tot + v
        dst[pl.ds(pl.multiple_of(lo + i * ADD, 16), ADD), :] = tot.astype(dst.dtype)
        return c

    lax.fori_loop(0, size // ADD, piece, 0, unroll=ADD_UNROLL)


class Sends:
    def __init__(self):
        self.kept = []

    def go(self, cond, make):
        if cond is None:
            make().start()
        else:

            @pl.when(cond)
            def _():
                make().start()

        self.kept.append((cond, make))

    def drain(self):
        for cond, make in self.kept:
            if cond is None:
                make().wait_send()
            else:

                @pl.when(cond)
                def _(make=make):
                    make().wait_send()


def sum_steps(half, g, result, obuf, refs, via):
    B = SimpleNamespace(**dict(zip([n for n, _, _ in RS_BUFS] + [n for n, _ in RS_SEMS], refs)))
    core, chip, x, y, z = place()
    flat = chip % 4
    xn = chip + 1 - 2 * x
    yn = chip + 2 - 4 * y
    sib = (1 - core, chip)
    mid = PART // 2
    top = pl.ds(0, mid)
    bottom = pl.ds(mid, mid)
    fd, fx, fy = 3 - flat, flat + 1 - 2 * x, flat + 2 - 4 * y
    sends = Sends()

    def rows_of(i, part):
        return g.at[pl.ds(pl.multiple_of((16 * half + i) * SLAB + part * SHIFT, 8), PART)]

    def each(t, f):
        if t == 0:
            f(z, 0, None)
            return
        for sign in (1, -1):
            zz = z + sign * t
            f(zz, sign, (zz >= 0) & (zz < NZ))

    def when(cond, f):
        if cond is None:
            f()
        else:
            pl.when(cond)(f)

    order = [(fd, 3), (fd, 2), (fx, 3), (fy, 3), (fx, 2), (fy, 2), (fd, 1), (flat, 3)]
    order += [(fx, 1), (fy, 1), (fd, 0), (flat, 2), (fx, 0), (fy, 0), (flat, 1), (flat, 0)]

    def start():
        for f, t in order:

            def begin(zz, sign, here, f=f):
                i = zz * 4 + f

                def go():
                    remote(rows_of(i, 1 - core), B.sbuf.at[i], B.ssend, B.srecv.at[i], sib).start()
                    pltpu.make_async_copy(rows_of(i, core), obuf(i), B.load.at[i]).start()

                when(here, go)

            each(t, begin)

    def ready(i):
        pltpu.make_async_copy(rows_of(i, core), obuf(i), B.load.at[i]).wait()
        remote(rows_of(i, core), B.sbuf.at[i], B.ssend, B.srecv.at[i], sib).wait_recv()

    def landed(dst, send, recv):
        remote(dst, dst, send, recv, sib).wait_recv()

    def up_down(sign):
        return 0 if sign > 0 else 1

    def inside(zz):
        return (zz >= 0) & (zz < NZ)

    def diag(t):
        def f(zz, sign, here):
            i = zz * 4 + fd

            def work():
                ready(i)
                src = [(obuf(i), 0), (B.sbuf.at[i], 0)]
                if t in via and t + 1 in via:
                    k = up_down(sign)
                    far = inside(z - sign)

                    @pl.when(far)
                    def _():
                        landed(B.dzb.at[k, t], B.dzs.at[k, t], B.dzr.at[k, t])
                        add_rows(obuf(i), src + [(B.dzb.at[k, t], 0)], 0, PART)

                    @pl.when(jnp.logical_not(far))
                    def _():
                        add_rows(obuf(i), src, 0, PART)

                elif t == 0 and 1 in via:
                    add_rows(obuf(i), src, 0, PART)
                    for k, s in enumerate((1, -1)):

                        @pl.when(inside(z - s))
                        def _(k=k):
                            landed(B.dzb.at[k, 0], B.dzs.at[k, 0], B.dzr.at[k, 0])
                            add_rows(obuf(i), [(obuf(i), 0), (B.dzb.at[k, 0], 0)], 0, PART)

                else:
                    add_rows(obuf(i), src, 0, PART)

            when(here, work)
            if t in via:
                k = up_down(sign)
                sends.go(
                    here,
                    lambda: remote(
                        obuf(i),
                        B.dzb.at[k, t - 1],
                        B.dzs.at[k, t - 1],
                        B.dzr.at[k, t - 1],
                        (core, chip + 4 * sign),
                    ),
                )
            else:
                sends.go(
                    here,
                    lambda: remote(
                        obuf(i).at[top], B.ab.at[zz], B.as_.at[zz], B.ar.at[zz], (core, yn)
                    ),
                )
                sends.go(
                    here,
                    lambda: remote(
                        obuf(i).at[bottom], B.bb.at[zz], B.bs.at[zz], B.br.at[zz], (core, xn)
                    ),
                )

        return lambda: each(t, f)

    def plane(t):
        def f(zz, sign, here):
            ix, iy = zz * 4 + fx, zz * 4 + fy

            def work_x():
                ready(ix)
                src = [(obuf(ix), 0), (B.sbuf.at[ix], 0)]
                if t in via:
                    add_rows(obuf(ix), src, 0, PART)
                else:
                    add_rows(obuf(ix), [(r, mid) for r, _ in src], mid, mid)
                    landed(B.ab.at[zz], B.as_.at[zz], B.ar.at[zz])
                    add_rows(obuf(ix), src + [(B.ab.at[zz], 0)], 0, mid)

            def work_y():
                ready(iy)
                src = [(obuf(iy), 0), (B.sbuf.at[iy], 0)]
                if t in via:
                    add_rows(obuf(iy), src, 0, PART)
                else:
                    add_rows(obuf(iy), src, 0, mid)
                    landed(B.bb.at[zz], B.bs.at[zz], B.br.at[zz])
                    add_rows(obuf(iy), [(r, mid) for r, _ in src] + [(B.bb.at[zz], 0)], mid, mid)

            when(here, work_x)
            sends.go(
                here, lambda: remote(obuf(ix), B.xb.at[zz], B.xs.at[zz], B.xr.at[zz], (core, xn))
            )
            when(here, work_y)
            sends.go(
                here, lambda: remote(obuf(iy), B.yb.at[zz], B.ys.at[zz], B.yr.at[zz], (core, yn))
            )

        return lambda: each(t, f)

    def column(t):
        def f(zz, sign, here):
            i = zz * 4 + flat
            k = up_down(sign)

            def work():
                ready(i)
                landed(B.xb.at[zz], B.xs.at[zz], B.xr.at[zz])
                landed(B.yb.at[zz], B.ys.at[zz], B.yr.at[zz])
                src = [(obuf(i), 0), (B.sbuf.at[i], 0), (B.xb.at[zz], 0), (B.yb.at[zz], 0)]
                if t == 3:
                    add_rows(obuf(i), src, 0, PART)
                    return
                far = inside(z - sign)

                @pl.when(far)
                def _():
                    landed(B.czb.at[k, t], B.czs.at[k, t], B.czr.at[k, t])
                    add_rows(obuf(i), src + [(B.czb.at[k, t], 0)], 0, PART)

                @pl.when(jnp.logical_not(far))
                def _():
                    add_rows(obuf(i), src, 0, PART)

            when(here, work)
            sends.go(
                here,
                lambda: remote(
                    obuf(i),
                    B.czb.at[k, t - 1],
                    B.czs.at[k, t - 1],
                    B.czr.at[k, t - 1],
                    (core, chip + 4 * sign),
                ),
            )

        return lambda: each(t, f)

    if half == 1:
        part = remote(
            B.fin.at[pl.ds(0, SHIFT)],
            result.at[pl.ds(0, SHIFT)],
            B.fsem.at[0],
            B.fsem.at[1],
            (1, chip),
        )
    else:
        part = remote(
            B.fin.at[pl.ds(PART - SHIFT, SHIFT)],
            result.at[pl.ds(PART, SHIFT)],
            B.fsem.at[0],
            B.fsem.at[1],
            (0, chip),
        )

    def final():
        i = z * 4 + flat
        ready(i)
        landed(B.xb.at[z], B.xs.at[z], B.xr.at[z])
        landed(B.yb.at[z], B.ys.at[z], B.yr.at[z])
        src = [(obuf(i), 0), (B.sbuf.at[i], 0), (B.xb.at[z], 0), (B.yb.at[z], 0)]
        add_rows(B.fin, src, 0, PART)
        for k, s in enumerate((1, -1)):

            @pl.when(inside(z - s))
            def _(k=k):
                landed(B.czb.at[k, 0], B.czs.at[k, 0], B.czr.at[k, 0])
                add_rows(B.fin, [(B.fin, 0), (B.czb.at[k, 0], 0)], 0, PART)

        @pl.when(core == half)
        def _():
            result[pl.ds(half * SHIFT, PART), :] = B.fin[...]

        @pl.when(core != half)
        def _():
            part.start()

    def drain():
        pltpu.make_async_copy(B.sbuf, B.sbuf, B.ssend).wait()
        sends.drain()

        @pl.when(core == half)
        def _():
            part.wait_recv()

        @pl.when(core != half)
        def _():
            part.wait_send()

    steps = [diag(3), diag(2), plane(3), plane(2), diag(1), column(3), plane(1), diag(0)]
    steps += [column(2), plane(0), column(1), final]
    return start, steps, drain


def last_sum(
    plen,
    g,
    vg,
    sent,
    dpix,
    out,
    vout,
    drows,
    obuf,
    vbuf,
    half_rows,
    tall,
    back,
    vs,
    vr,
    vl,
    es,
    bs,
    *refs,
):
    core, chip = lax.axis_index("stream"), lax.axis_index("dp")
    me = core * 16 + chip
    first = core == 0
    greet_all(core, chip)
    start, steps, drain = sum_steps(0, g, out, lambda i: obuf.at[i], refs, (1, 2))
    start()

    def vsend(k, carry):
        peer = (me + k) % 32
        remote(vg.at[peer], vbuf.at[me], vs, vr, (peer // 16, peer % 16)).start()
        return carry

    ways = []
    for t in range(SPAN):
        two = pl.ds(CAP * t, CAP)
        to = (core, (chip + t + 1) % 16)
        ways.append(remote(sent.at[two], back.at[two], bs.at[0, t], bs.at[1, t], to))
    lax.fori_loop(1, 32, vsend, 0)
    vcp = pltpu.make_async_copy(vg.at[me], vbuf.at[me], vl)
    vcp.start()
    for step in steps[:7]:
        step()
    for t in ISSUE:
        ways[t].start()
    for step in steps[7:WAYS_AT]:
        step()
    for way in ways:
        way.wait()

    pick = lax.broadcasted_iota(jnp.int32, (ROWS, RSLOT * PMAX), 0) == slot_rows(plen, 1)
    total = nn(pick.astype(F32).astype(BF), back[...].reshape(RSLOT * PMAX, HALF))
    to_text = remote(tall.at[0], tall.at[1], es.at[0], es.at[1], (1, chip))
    to_image = remote(half_rows.at[0], half_rows.at[1], es.at[0], es.at[1], (0, chip))

    @pl.when(first)
    def _():
        tall[0] = total.astype(BF)
        to_text.start()
        for i in range(OWN):
            drows[NP * i : NP * (i + 1), :] = dpix[i, 0:NP, :]

    @pl.when(core == 1)
    def _():
        for i in range(OWN):
            half_rows[0, NP * i : NP * (i + 1), :] = dpix[i, 0:NP, :]
        to_image.start()
        drows[:, HALF:] = total.astype(BF)

    for step in steps[WAYS_AT : WAYS_AT + 2]:
        step()

    @pl.when(first)
    def _():
        to_image.wait_recv()
        drows[OWN * NP :, :] = half_rows[1]

    @pl.when(core == 1)
    def _():
        to_text.wait_recv()
        drows[:, :HALF] = tall[1]

    for step in steps[WAYS_AT + 2 :]:
        step()
    vcp.wait()
    pltpu.make_async_copy(vbuf.at[pl.ds(0, 31)], vbuf.at[pl.ds(0, 31)], vr).wait()
    vout[...] = jnp.sum(vbuf[...], axis=0)
    pltpu.make_async_copy(vbuf.at[pl.ds(0, 31)], vbuf.at[pl.ds(0, 31)], vs).wait()

    @pl.when(first)
    def _():
        to_text.wait_send()

    @pl.when(core == 1)
    def _():
        to_image.wait_send()

    drain()


def summed(plen, g, vg, back, dpix):
    any_ = pl.BlockSpec(memory_space=pl.ANY)
    vmem = pl.BlockSpec(memory_space=pltpu.VMEM)
    smem = pl.BlockSpec(memory_space=pltpu.SMEM)
    return pl.pallas_call(
        last_sum,
        out_shape=(
            jax.ShapeDtypeStruct((SLAB, D), F32),
            jax.ShapeDtypeStruct((VEC, 128), F32),
            jax.ShapeDtypeStruct((ROWS, D), BF),
        ),
        in_specs=[smem, any_, any_, vmem, vmem],
        out_specs=(vmem, vmem, vmem),
        scratch_shapes=[
            pltpu.VMEM((16, PART, D), BF),
            pltpu.VMEM((32, VEC, 128), F32),
            pltpu.VMEM((2, OWN * NP, D), BF),
            pltpu.VMEM((2, ROWS, HALF), BF),
            pltpu.VMEM((RSLOT, PMAX, HALF), BF),
            dma,
            dma,
            dma,
            dma((2,)),
            dma((2, SPAN)),
        ]
        + rs_scratch(),
        compiler_params=pltpu.CompilerParams(
            collective_id=2, has_side_effects=True, vmem_limit_bytes=60 * 2**20
        ),
    )(plen, g, vg, back, dpix)


X_IN = ("dest", "plen", "rows", "cot", "wsh", "vblk", "wfull")
X_OUT = ("dpix", "vgb", "g", "encm", "dprem", "wall", "r1")
X_SCRATCH = (
    ("packed", (ROWS, HALF), BF),
    ("raw", (ROWS // 2, D), BF),
    ("pmsg", (RSLOT, MSG, HALF), BF),
    ("cmsg", (RSLOT, R, HALF), BF),
    ("arp", (RSLOT, MSG, HALF), BF),
    ("arc", (RSLOT, R, HALF), BF),
    ("gvp", (OWN, MSG, HALF), BF),
    ("gtp", (OWN, MSG, HALF), BF),
    ("gvc", (OWN, R, HALF), BF),
    ("gtc", (OWN, R, HALF), BF),
    ("gvo", (OWN, R, HALF), BF),
    ("img", (IMG_DEV + 1, R, HALF), BF),
    ("pim", (IMG_DEV + 1, PMAX, HALF), BF),
    ("vbuf", (32, VEC, 128), BF),
    ("vec", (VEC, D), F32),
    ("bias", (1, FF), F32),
    ("vg", (VEC, D), F32),
    ("bg", (1, FF), F32),
    ("pix", (OWN, NPAD, D), BF),
    ("og", (M, D), BF),
    ("dx", (M, D), BF),
    ("stem", (PIX, D), BF),
    ("qkvw", (3 * D, D), BF),
    ("outw", (D, D), BF),
    ("wb", (8, CH, D), BF),
    ("x", (M, D), BF),
    ("nrm", (M, D), BF),
    ("qkv", (M, 3 * D), BF),
    ("prob", (2 * OWN * 6, R, R), BF),
    ("ctx", (M, D), BF),
    ("res", (M, D), F32),
    ("mlp", (M, D), BF),
    ("big", (M, D), F32),
    ("hid", (M, FF), BF),
    ("slope", (M, FF), BF),
    ("dpr", (M, CH), BF),
    ("f1", (M, CH), F32),
)
X_SEMS = (
    ("psem", (2, 4, SPAN)),
    ("gsem", (2, 6)),
    ("lsem", (8,)),
    ("vsem", (2,)),
    ("wsem", (3,)),
    ("csem", (2, 2)),
    ("osem", (2, 2)),
)


def x_kernel(near, *refs):
    names = X_IN + X_OUT + tuple(n for n, _, _ in X_SCRATCH) + tuple(n for n, _ in X_SEMS)
    K = SimpleNamespace(**dict(zip(names, refs)))
    gsems = refs[len(names) :]
    if not near:
        gsems, sum_refs = gsems[: -len(RS_BUFS) - len(RS_SEMS)], gsems[-len(RS_BUFS) - len(RS_SEMS) :]
    K.upb, K.downb = K.wb.at[pl.ds(0, 2)], K.wb.at[pl.ds(2, 2)]
    K.gub, K.gdb = K.wb.at[pl.ds(4, 2)], K.wb.at[pl.ds(6, 2)]
    core = lax.axis_index("stream")
    chip = lax.axis_index("dp")
    n_dp = lax.axis_size("dp")
    sib = (1 - core, chip)
    first = core == 0
    second = core == 1
    me = core * n_dp + chip
    if near:
        greet_near(core, chip, n_dp)
    else:
        greet_all(core, chip)
    wall = K.wfull if near else K.wall

    n_sems = len(gsems) // 2
    todo = []
    if not near:
        parts = [gather_steps(K.wsh, wall, gsems[p * n_sems : (p + 1) * n_sems], p) for p in range(2)]
        todo = [step for pair_ in zip(*parts) for step in pair_]

    def advance(n):
        for _ in range(n):
            if todo:
                todo.pop(0)()

    if not near:

        advance(2)

        K.vbuf[me] = K.vblk[...]
        own_slab = wall.at[pl.ds(pl.multiple_of(me * SLAB, 8), SLAB)]
        keep = K.upb.at[0, pl.ds(0, SLAB)]
        kin = pltpu.make_async_copy(K.wsh, keep, K.lsem.at[1])
        kout = pltpu.make_async_copy(keep, own_slab, K.lsem.at[2])
        kin.start()

    last_rows = K.rows.at[pl.ds(ROWS // 2, ROWS // 2)]
    pix_go = remote(last_rows, K.raw, K.gsem.at[0, 4], K.gsem.at[1, 4], (1, chip))
    pack_go = remote(
        K.rows.at[:, pl.ds(0, HALF)], K.packed, K.gsem.at[0, 4], K.gsem.at[1, 4], (0, chip)
    )
    pix_own = pltpu.make_async_copy(K.rows.at[pl.ds(0, ROWS // 2)], K.raw, K.lsem.at[0])
    pack_own = pltpu.make_async_copy(K.rows.at[:, pl.ds(HALF, HALF)], K.packed, K.lsem.at[0])

    @pl.when(first)
    def _():
        pix_go.start()
        pix_own.start()

    @pl.when(second)
    def _():
        pack_go.start()
        pack_own.start()

    if not near:

        def vsend(k, carry):
            peer = (me + k) % 32
            remote(K.vblk, K.vbuf.at[me], K.vsem.at[0], K.vsem.at[1], (peer // 16, peer % 16)).start()
            return carry

        lax.fori_loop(1, 32, vsend, 0)

    def pair(t):
        return pl.ds(CAP * t, CAP)

    def rc(src, dst, k, i, dev):
        return remote(src, dst, K.psem.at[0, k, i], K.psem.at[1, k, i], dev)

    down = [(core, (chip + n_dp - t - 1) % n_dp) for t in range(SPAN)]
    up = [(core, (chip + t + 1) % n_dp) for t in range(SPAN)]
    pin = [rc(K.pmsg.at[pair(t)], K.arp.at[pair(t)], 0, t, down[t]) for t in range(SPAN)]
    cin = [rc(K.cmsg.at[pair(t)], K.arc.at[pair(t)], 1, t, down[t]) for t in range(SPAN)]

    if not near:
        kin.wait()
        kout.start()

    @pl.when(first)
    def _():
        pack_go.wait_recv()
        pix_own.wait()

    @pl.when(second)
    def _():
        pix_go.wait_recv()
        pack_own.wait()

    def prefix_slots():
        target = slot_rows(K.plen, 0)
        pick = lax.broadcasted_iota(jnp.int32, (RSLOT * PMAX, ROWS), 1) == target
        rows = nn(pick.astype(F32).astype(BF), K.packed[...]).astype(BF)
        for s in range(RSLOT):
            K.pmsg[s, 0:PMAX, :] = rows[PMAX * s : PMAX * (s + 1), :]
            size = jnp.full((MSG - PMAX, HALF), K.plen[s], jnp.int32)
            K.pmsg[s, PMAX:MSG, :] = size.astype(F32).astype(BF)

    place_row = lax.broadcasted_iota(jnp.int32, (PMAX, 1), 0)
    zero = jnp.zeros((), BF)

    def cot_slot(s, none):
        size = K.plen[s]
        K.cmsg[s, 0:PMAX, :] = jnp.where(place_row < size, K.cot[s, NP:SEQ, :], zero)
        K.cmsg[s, PMAX : PMAX + NP, :] = jnp.where(
            jnp.full((NP, 1), size, jnp.int32) > 0, K.cot[s, 0:NP, :], zero
        )
        K.cmsg[s, PMAX + NP : R, :] = jnp.zeros((NPAD - NP, HALF), BF)
        return none

    prefix_slots()
    for t in ISSUE:
        pin[t].start()
    advance(4)
    for s in range(0, RSLOT, 2):
        lax.fori_loop(s, s + 2, cot_slot, 0)
        advance(2)
    for i in range(OWN):
        K.pix[i, 0:NP, :] = K.raw[NP * i : NP * (i + 1), :]
        K.pix[i, NP:NPAD, :] = jnp.zeros((NPAD - NP, D), BF)
    advance(2 * CIN_AT - 14)
    for t in ISSUE:
        cin[t].start()
    advance(99)
    if not near:
        for p in range(2):
            rows = (CUT, SLAB - CUT)[p] * 16
            piece = wall.at[pl.ds(0, rows)]
            pltpu.make_async_copy(piece, piece, gsems[p * n_sems + n_sems - 1]).wait()
        pltpu.make_async_copy(K.vbuf.at[pl.ds(0, 31)], K.vbuf.at[pl.ds(0, 31)], K.vsem.at[1]).wait()
    vec = jnp.zeros((VEC, D), F32)
    lane_d = lax.broadcasted_iota(jnp.int32, (1, D), 1)
    n_dev = 2 * n_dp
    width = D // n_dev
    if near:
        K.vec[...] = K.vblk[...].astype(F32)
    else:

        def spread(k, total):
            block = jnp.concatenate([K.vbuf[k].astype(F32), jnp.zeros((VEC, D - 128), F32)], axis=1)
            block = jnp.where(lane_d < width, block, 0.0)
            return total + pltpu.roll(block, k * width, 1)

        K.vec[...] = lax.fori_loop(0, n_dev, spread, vec)
    for j in range(4):
        K.bias[:, j * D : (j + 1) * D] = K.vec[5 + j : 6 + j, :]
    def load(dst, lo, n, sem):
        return pltpu.make_async_copy(wall.at[pl.ds(lo, n)], dst, sem)

    ls = load(K.stem, 0, PIX, K.wsem.at[0])
    lq = load(K.qkvw, PIX, 3 * D, K.wsem.at[1])
    lo_ = load(K.outw, PIX + 3 * D, D, K.wsem.at[2])
    if not near:
        kout.wait()
    ls.start()
    lq.start()
    lo_.start()

    def chunk(c, slot):
        at = pl.multiple_of(c * CH, 16)
        return (
            pltpu.make_async_copy(wall.at[pl.ds(UP + at, CH)], K.upb.at[slot], K.csem.at[0, slot]),
            pltpu.make_async_copy(wall.at[pl.ds(DOWN + at, CH)], K.downb.at[slot], K.csem.at[1, slot]),
        )

    def mine(k):
        return K.dest[OWN * core + k]

    def image_of(slot):
        found = jnp.int32(IMG_DEV)
        for j in range(IMG_DEV):
            found = jnp.where(K.dest[j] == slot, j, found)
        return found

    def theirs(k):
        return K.dest[OWN * (1 - core) + k]

    own_half = pl.ds(pl.multiple_of(core * HALF, 128), HALF)
    other_half = pl.ds(pl.multiple_of((1 - core) * HALF, 128), HALF)

    def swap(src, dst, k):
        return remote(src, dst, K.gsem.at[0, k], K.gsem.at[1, k], sib)

    pswap = swap(K.gvp, K.gtp, 0)
    cswap = swap(K.gvc, K.gtc, 1)
    for cp in pin:
        cp.wait_recv()
    for k in range(OWN):
        K.gvp[k] = K.arp[theirs(k)]
    lens = []
    for k in range(OWN):
        K.x[R * k : R * k + PMAX, own_half] = K.arp[mine(k), 0:PMAX, :]
        lens.append(K.arp[mine(k), PMAX:MSG, :].astype(F32)[0:1, 0:1])
    pswap.start()
    ls.wait()
    for i in range(OWN):
        K.x[R * i + PMAX : R * (i + 1), :] = nn(K.pix[i], K.stem[...]).astype(BF)
    pswap.wait_recv()
    for k in range(OWN):
        K.x[R * k : R * k + PMAX, other_half] = K.gtp[k, 0:PMAX, :]

    def norm1(rows):
        xhat, _ = norm_parts(K.x[rows, :].astype(F32))
        K.nrm[rows, :] = (xhat * K.vec[0:1, :] + K.vec[1:2, :]).astype(BF)

    rows_loop(norm1)
    lq.wait()
    for k in range(3):
        K.qkv[:, k * D : (k + 1) * D] = nt(K.nrm[...], K.qkvw[k * D : (k + 1) * D, :]).astype(BF)
    lane = lax.broadcasted_iota(jnp.int32, (1, 128), 1)
    low_half = lane < HD
    key = lax.broadcasted_iota(jnp.int32, (1, R), 1)
    scale = HD**-0.5

    def heads(i, p):
        ln = jnp.where(i == 0, lens[0], lens[1])
        ok = (key.astype(F32) < ln) | ((key >= PMAX) & (key < PMAX + NP))
        rows = pl.ds(pl.multiple_of(i * R, 16), R)

        def part(k):
            return K.qkv[rows, pl.ds(pl.multiple_of(k * D + p * 128, 128), 128)]

        return rows, ok, part(0), part(1), part(2)

    def halves(v):
        return jnp.where(low_half, v, zero), jnp.where(low_half, zero, v)

    def attend(n, c):
        i, p = n // 6, n % 6
        rows, ok, q, k, v = heads(i, p)
        outs = []
        for h, qh in enumerate(halves(q)):
            s = jnp.where(ok, nt(qh, k) * scale, MASKED)
            e = jnp.exp(s - jnp.max(s, axis=-1, keepdims=True))
            a = (e * (1.0 / jnp.sum(e, axis=-1, keepdims=True))).astype(BF)
            K.prob[2 * n + h] = a
            outs.append(nn(a, v))
        here = pl.ds(pl.multiple_of(p * 128, 128), 128)
        K.ctx[rows, here] = jnp.where(low_half, outs[0], outs[1]).astype(BF)
        return c

    lax.fori_loop(0, OWN * 6, attend, 0, unroll=3)
    lo_.wait()
    K.res[...] = nt(K.ctx[...], K.outw[...])

    def norm2(rows):
        r = K.res[rows, :] + K.x[rows, :].astype(F32)
        K.res[rows, :] = r
        xhat, _ = norm_parts(r)
        K.mlp[rows, :] = (xhat * K.vec[2:3, :] + K.vec[3:4, :]).astype(BF)
        K.big[rows, :] = r + K.vec[4:5, :]

    rows_loop(norm2)
    count = FF // CH

    def fetch(c, slot):
        for cp in chunk(c, slot):
            cp.wait()

        @pl.when(c + 1 < count)
        def _():
            for cp in chunk(c + 1, 1 - slot):
                cp.start()

    def ffn(c, carry):
        slot = lax.rem(c, 2)
        fetch(c, slot)
        cols = pl.ds(pl.multiple_of(c * CH, 128), CH)
        K.f1[...] = nt(K.mlp[...], K.upb[slot])
        b = K.bias[:, cols]

        def act(i, none):
            rows = pl.ds(pl.multiple_of(i * LNB, 16), LNB)
            h, dh = gelu_both(K.f1[rows, :] + b)
            K.hid[rows, cols] = h.astype(BF)
            K.slope[rows, cols] = dh.astype(BF)
            return none

        lax.fori_loop(0, M // LNB, act, 0, unroll=True)
        K.big[...] += nn(K.hid[:, cols], K.downb[slot])
        return carry

    for cp in chunk(0, 0):
        cp.start()
    lax.fori_loop(0, count, ffn, 0)
    for cp in chunk(0, 0):
        cp.start()
    for k in range(OWN):
        K.gvo[k] = K.big[R * k : R * (k + 1), other_half].astype(BF)
    for k in range(OWN):
        K.img[OWN * core + k] = K.big[R * k : R * (k + 1), own_half].astype(BF)
    K.img[IMG_DEV] = jnp.zeros((R, HALF), BF)
    oswap = swap(K.gvo, K.img.at[pl.ds(OWN * core, OWN)], 2)
    oswap.start()
    K.big[...] = jnp.zeros((M, D), F32)
    oswap.wait()
    for cp in cin:
        cp.wait_send()
    for k in range(RSLOT):
        K.cmsg[k] = K.img[image_of(k)]
    eout = [rc(K.cmsg.at[pair(t)], K.encm.at[pair(t)], 2, t, up[t]) for t in range(SPAN)]
    for t in (3, 2, 1, 0):
        eout[t].start()
    for cp in cin:
        cp.wait_recv()
    for k in range(OWN):
        K.gvc[k] = K.arc[theirs(k)]
    for k in range(OWN):
        K.og[R * k : R * (k + 1), own_half] = K.arc[mine(k)]
    cswap.start()
    cswap.wait_recv()
    for k in range(OWN):
        K.og[R * k : R * (k + 1), other_half] = K.gtc[k]

    def store(c, slot):
        at = pl.multiple_of(c * CH, 16)
        return (
            pltpu.make_async_copy(K.gub.at[slot], K.g.at[pl.ds(UP + at, CH)], K.osem.at[0, slot]),
            pltpu.make_async_copy(K.gdb.at[slot], K.g.at[pl.ds(DOWN + at, CH)], K.osem.at[1, slot]),
        )

    def ffn_back(c, carry):
        slot = lax.rem(c, 2)
        fetch(c, slot)

        @pl.when(c >= 2)
        def _():
            for cp in store(c - 2, slot):
                cp.wait()

        cols = pl.ds(pl.multiple_of(c * CH, 128), CH)
        K.f1[...] = nt(K.og[...], K.downb[slot])

        def act(i, tot):
            rows = pl.ds(pl.multiple_of(i * 16, 16), 16)
            dp = (K.f1[rows, :] * K.slope[rows, cols].astype(F32)).astype(BF)
            K.dpr[rows, :] = dp
            return tot + dp.astype(F32)

        tot = lax.fori_loop(0, M // 16, act, jnp.zeros((16, CH), F32), unroll=2)
        K.bg[:, cols] = jnp.sum(tot, axis=0, keepdims=True)
        K.big[...] += nn(K.dpr[...], K.upb[slot])
        K.gub[slot] = tn(K.dpr[...], K.mlp[...]).astype(BF)
        K.gdb[slot] = tn(K.hid[:, cols], K.og[...]).astype(BF)
        for cp in store(c, slot):
            cp.start()
        return carry

    lax.fori_loop(0, count, ffn_back, 0)
    for slot in range(2):
        for cp in store(count - 2 + slot, slot):
            cp.wait()
    late = []
    if not near:

        def obuf(i):
            return K.wb.at[i // 2, pl.ds(pl.multiple_of((i % 2) * PART, 16), PART)]

        begin, late, end_sum = sum_steps(1, K.g, K.r1, obuf, sum_refs, SUM_VIA)
        begin()

    def advance_sum(n=1):
        for _ in range(n):
            if late:
                late.pop(0)()

    def back2(i, c):
        rows = pl.ds(pl.multiple_of(i * LNB, 16), LNB)
        o = K.og[rows, :].astype(F32)
        d, dg, dc = norm_back(K.res[rows, :], K.big[rows, :], K.vec[2:3, :])
        d = d + o
        K.res[rows, :] = d
        K.dx[rows, :] = d.astype(BF)
        return (c[0] + dg, c[1] + dc, c[2] + jnp.sum(o, axis=0, keepdims=True))

    none = jnp.zeros((1, D), F32)
    dg2, dc2, dob = lax.fori_loop(0, M // LNB, back2, (none, none, none), unroll=True)
    K.vg[8:VEC, :] = jnp.zeros((VEC - 8, D), F32)
    K.vg[2:3, :] = dg2
    K.vg[3:4, :] = dc2
    K.vg[4:5, :] = dob
    for j in range(4):
        K.vg[5 + j : 6 + j, :] = K.bg[:, j * D : (j + 1) * D]

    advance_sum()

    def put(src, lo, n, sem):
        return pltpu.make_async_copy(src, K.g.at[pl.ds(lo, n)], sem)

    K.mlp[...] = nn(K.dx[...], K.outw[...]).astype(BF)
    advance_sum()
    K.outw[...] = tn(K.dx[...], K.ctx[...]).astype(BF)
    po = put(K.outw, PIX + 3 * D, D, K.wsem.at[2])
    po.start()

    def attend_back(n, c):
        i, p = n // 6, n % 6
        rows, ok, q, k, v = heads(i, p)
        here = pl.ds(pl.multiple_of(p * 128, 128), 128)
        dc = K.mlp[rows, here]
        dq = []
        dk = dv = None
        for h, (qh, dch) in enumerate(zip(halves(q), halves(dc))):
            a = K.prob[2 * n + h]
            af = a.astype(F32)
            t = af * nt(dch, v)
            dsc = (t - af * jnp.sum(t, axis=-1, keepdims=True)).astype(BF)
            dq.append(nn(dsc, k))
            dkh = tn(dsc, qh)
            dvh = tn(a, dch)
            dk = dkh if dk is None else dk + dkh
            dv = dvh if dv is None else dv + dvh

        def at(j):
            return pl.ds(pl.multiple_of(j * D + p * 128, 128), 128)

        K.qkv[rows, at(0)] = (jnp.where(low_half, dq[0], dq[1]) * scale).astype(BF)
        K.qkv[rows, at(1)] = (dk * scale).astype(BF)
        K.qkv[rows, at(2)] = dv.astype(BF)
        return c

    advance_sum()
    for group in range(6):
        lax.fori_loop(2 * group, 2 * group + 2, attend_back, 0)
        advance_sum()
    K.big[...] = nn(K.qkv[...], K.qkvw[...])
    advance_sum()

    def back1(i, c):
        rows = pl.ds(pl.multiple_of(i * LNB, 16), LNB)
        d, dg, dc = norm_back(K.x[rows, :].astype(F32), K.big[rows, :], K.vec[0:1, :])
        K.dx[rows, :] = (K.res[rows, :] + d).astype(BF)
        return (c[0] + dg, c[1] + dc)

    dg1, dc1 = lax.fori_loop(0, M // LNB, back1, (none, none), unroll=True)
    advance_sum()
    pswap.wait_send()
    cswap.wait_send()
    for k in range(OWN):
        K.gvp[k, 0:PMAX, :] = K.dx[R * k : R * k + PMAX, other_half]
    for k in range(OWN):
        K.pim[OWN * core + k] = K.dx[R * k : R * k + PMAX, own_half]
    K.pim[IMG_DEV] = jnp.zeros((PMAX, HALF), BF)
    dswap = swap(K.gvp.at[:, pl.ds(0, PMAX)], K.pim.at[pl.ds(OWN * core, OWN)], 3)
    dswap.start()
    K.vg[0:1, :] = dg1
    K.vg[1:2, :] = dc1

    def cut(k, c):
        K.vgb[k] = pltpu.roll(K.vg[...], lax.rem(D - k * width, D), 1)[:, 0:128]
        return c

    lax.fori_loop(0, n_dev, cut, 0)
    for k in range(3):
        K.qkvw[k * D : (k + 1) * D, :] = tn(K.qkv[:, k * D : (k + 1) * D], K.nrm[...]).astype(BF)
    pq = put(K.qkvw, PIX, 3 * D, K.wsem.at[1])
    pq.start()
    dswap.wait()
    if not near:
        advance_sum(99)
    dout = []
    if near:
        for k in range(RSLOT):
            K.arp[k, 0:PMAX, :] = K.pim[image_of(k)]
        dout = [
            rc(K.arp.at[pair(t), pl.ds(0, PMAX)], K.dprem.at[pair(t)], 3, t, up[t])
            for t in range(SPAN)
        ]
        for t in ISSUE:
            dout[t].start()
    else:
        for k in range(RSLOT):
            K.dprem[k] = K.pim[image_of(k)]
    tot = None
    for i in range(OWN):
        dp = K.dx[R * i + PMAX : R * (i + 1), :]
        K.dpix[i] = nt(dp, K.stem[...]).astype(BF)
        t = tn(K.pix[i], dp)
        tot = t if tot is None else tot + t
    K.stem[...] = tot.astype(BF)
    ps = put(K.stem, 0, PIX, K.wsem.at[0])
    ps.start()
    for cp in eout + dout:
        cp.wait()
    po.wait()
    pq.wait()
    ps.wait()
    for cp in pin:
        cp.wait_send()

    @pl.when(first)
    def _():
        pix_go.wait_send()

    @pl.when(second)
    def _():
        pack_go.wait_send()

    if not near:
        end_sum()
        for p in range(2):
            for step in gather_steps(
                K.wsh, wall, gsems[p * n_sems : (p + 1) * n_sems], p, draining=True
            ):
                step()
            rows = (CUT, SLAB - CUT)[p] * 16
            piece = wall.at[pl.ds(0, rows)]
            pltpu.make_async_copy(piece, piece, gsems[p * n_sems + n_sems - 2]).wait()
        pltpu.make_async_copy(K.vbuf.at[pl.ds(0, 31)], K.vbuf.at[pl.ds(0, 31)], K.vsem.at[0]).wait()


def whole_block(dest, plen, rows, cot, wsh, vblk, wfull, n_dev):
    near = wfull is not None
    any_ = pl.BlockSpec(memory_space=pl.ANY)
    vmem = pl.BlockSpec(memory_space=pltpu.VMEM)
    smem = pl.BlockSpec(memory_space=pltpu.SMEM)
    total = SLAB * 32 if not near else wfull.shape[0]
    if near:
        wsh = wsh[:8]
    else:
        wfull = wsh[:8]
    outs = (
        jax.ShapeDtypeStruct((OWN, NPAD, D), BF),
        jax.ShapeDtypeStruct((n_dev, VEC, 128), F32),
        jax.ShapeDtypeStruct((total, D), BF),
        jax.ShapeDtypeStruct((RSLOT, R, HALF), BF),
        jax.ShapeDtypeStruct((RSLOT, PMAX, HALF), BF),
        jax.ShapeDtypeStruct((8, D) if near else (total, D), BF),
        jax.ShapeDtypeStruct((8, D) if near else (SLAB, D), F32),
    )
    return pl.pallas_call(
        functools.partial(x_kernel, near),
        out_shape=outs,
        in_specs=[smem, smem, any_, vmem, any_, vmem, any_],
        out_specs=(vmem, vmem, any_, any_, vmem, any_, vmem),
        scratch_shapes=[pltpu.VMEM(s, t) for _, s, t in X_SCRATCH]
        + [dma(s) for _, s in X_SEMS]
        + ([] if near else gather_sems() + gather_sems() + rs_scratch()),
        compiler_params=pltpu.CompilerParams(
            collective_id=3, has_side_effects=True, vmem_limit_bytes=63 * 2**20
        ),
    )(dest, plen, rows, cot, wsh, vblk, wfull)


def swapped(value):
    return lax.ppermute(value, "stream", [(0, 1), (1, 0)])


def body(
    stream_rows,
    dest,
    prefix_len,
    weights,
    momentum,
    average,
    vectors,
    vec_momentum,
    vec_average,
    cotangent,
):
    core = lax.axis_index("stream")
    first = core == 0
    n_dp = lax.axis_size("dp")
    n_dev = 2 * n_dp
    lane = vectors.shape[1]
    kernels = n_dp == 16

    rows = stream_rows[0, 0]
    half_rows = ROWS // 2
    lengths = prefix_len[0]
    slots = dest[0]
    shard = weights.astype(BF)
    if kernels:
        full = None
        block = jnp.pad(vectors.astype(BF), ((0, VEC - 9), (0, 128 - lane)))
    else:
        full = lax.all_gather(shard, ALL, axis=0, tiled=True)
        block = jnp.pad(vectors.astype(BF), ((0, VEC - 9), (0, 0)))
        block = lax.all_gather(block, ALL, axis=1, tiled=True)
    d_pixels, vec_blocks, grads, enc_back, prefix_back, _, late_grad = whole_block(
        slots, lengths, rows, cotangent[0], shard, block, full, n_dev
    )
    if kernels:
        early_grad, vec_grad, d_rows = summed(
            lengths, grads, vec_blocks, prefix_back, d_pixels
        )
        weight_grad = jnp.where(first, early_grad, late_grad)
    else:
        weight_grad = lax.psum_scatter(grads, ALL, scatter_dimension=0, tiled=True).astype(F32)
        vec_grad = lax.psum_scatter(vec_blocks, ALL, scatter_dimension=0, tiled=True)[0]
    vec_grad = vec_grad[:9, :lane]

    columns = jnp.arange(SEQ, dtype=jnp.int32)
    row_ok = (columns[None, :] < NP + lengths[:, None]) & (lengths[:, None] > 0)
    enc_out = jnp.concatenate([enc_back[:, PMAX : PMAX + NP], enc_back[:, :PMAX]], axis=1)
    enc_out = jnp.where(row_ok[:, :, None], enc_out, jnp.zeros((), BF))[None]

    if not kernels:
        offsets = jnp.cumsum(lengths) - lengths
        places = jnp.arange(PMAX, dtype=jnp.int32)
        row_index = offsets[:, None] + places[None, :]
        keep_mask = places[None, :] < lengths[:, None]
        rows_at = jnp.arange(ROWS, dtype=jnp.int32)
        pick = (
            (row_index.reshape(-1)[:, None] == rows_at[None, :]) & keep_mask.reshape(-1)[:, None]
        ).astype(BF)
        d_packed = tn(pick, prefix_back.reshape(RSLOT * PMAX, HALF)).astype(BF)
        d_pixels = d_pixels[:, :NP].reshape(half_rows, D)
        give = jnp.where(
            first, jnp.concatenate([d_packed[:half_rows], d_packed[half_rows:]], axis=1), d_pixels
        )
        got = swapped(give)
        d_image_rows = jnp.concatenate([d_pixels, got])
        d_text_rows = jnp.concatenate(
            [jnp.concatenate([got[:, :HALF], got[:, HALF:]], axis=0), d_packed], axis=1
        )
        d_rows = jnp.where(first, d_image_rows, d_text_rows)
    d_rows = d_rows.astype(F32)[None, None]

    rate = 0.5 * (D * IMG_DEV * n_dp * NP) ** (-0.5)
    new_momentum = MOMENT * momentum + weight_grad
    new_weights = weights - rate * (weight_grad + MOMENT * new_momentum)
    new_average = DECAY * average + (1.0 - DECAY) * new_weights
    vec_new_momentum = MOMENT * vec_momentum + vec_grad
    vec_new = vectors - rate * (vec_grad + MOMENT * vec_new_momentum)
    vec_new_average = DECAY * vec_average + (1.0 - DECAY) * vec_new
    return (
        enc_out,
        d_rows,
        weight_grad,
        new_momentum,
        new_average,
        new_weights,
        new_weights.astype(BF),
        vec_grad,
        vec_new_momentum,
        vec_new_average,
        vec_new,
        vec_new.astype(BF),
    )


def solution(mesh):
    both = P(ALL, None)
    lanes = P(None, ALL)
    in_specs = (
        P("stream", "dp", None, None),
        P("dp", None),
        P("dp", None),
        both,
        both,
        both,
        lanes,
        lanes,
        lanes,
        P("dp", None, None, "stream"),
    )
    out_specs = (
        P("dp", None, None, "stream"),
        P("stream", "dp", None, None),
        both,
        both,
        both,
        both,
        both,
        lanes,
        lanes,
        lanes,
        lanes,
        lanes,
    )
    return jax.shard_map(body, mesh=mesh, in_specs=in_specs, out_specs=out_specs, check_vma=False)
```
